32 devices in a mesh: dp: 16 (over z, x, core), tensor: 2 (over y).
Axes of the slice: x: 2, y: 2, z: 4, core: 2. Of those that a mesh axis runs over, the one named last changes fastest.
Arguments:
- layer_input: bfloat16 [16384, 1024], P('dp'), may hold values from -6 to 6
- segments: int32 [16, 1024], P('dp'), may hold values from 0 to 3, never falling along the last dimension, each value on 1 to 512 neighbouring positions
- expert_choice: int32 [16384, 2], P('dp'), may hold values from 0 to 3, as said below
- dispatch_order: int32 [16, 2048], P('dp'), may hold values from 0 to 2047, each once within a row
- norm_gain_one: float32 [1024], replicated, may hold values from 0.5 to 1.5
- w_query: bfloat16 [1024, 1024], P(None, 'tensor'), may hold values from -0.1875 to 0.1875
- w_key: bfloat16 [1024, 512], P(None, 'tensor'), may hold values from -0.1875 to 0.1875
- w_value: bfloat16 [1024, 512], P(None, 'tensor'), may hold values from -0.1875 to 0.1875
- w_out: bfloat16 [1024, 1024], P('tensor'), may hold values from -1 to 1
- norm_gain_two: float32 [1024], replicated, may hold values from 0.5 to 1.5
- w_router: bfloat16 [1024, 4], replicated, may hold values from -0.125 to 0.125
- w_gate: bfloat16 [4, 1024, 512], P(None, None, 'tensor'), may hold values from -0.1875 to 0.1875
- w_up: bfloat16 [4, 1024, 512], P(None, None, 'tensor'), may hold values from -0.1875 to 0.1875
- w_down: bfloat16 [4, 512, 1024], P(None, 'tensor'), may hold values from -0.5 to 0.5
- out_grad: bfloat16 [16384, 1024], P('dp'), may hold values from -6 to 6
Outputs:
- layer_output: bfloat16 [16384, 1024], P('dp')
- input_grad: float32 [16384, 1024], P('dp')
- norm_gain_one_grad: float32 [1024], replicated
- w_query_grad: float32 [1024, 1024], P(None, 'tensor')
- w_key_grad: float32 [1024, 512], P(None, 'tensor')
- w_value_grad: float32 [1024, 512], P(None, 'tensor')
- w_out_grad: float32 [1024, 1024], P('tensor')
- norm_gain_two_grad: float32 [1024], replicated
- w_router_grad: float32 [1024, 4], replicated
- w_gate_grad: float32 [4, 1024, 512], P(None, None, 'tensor')
- w_up_grad: float32 [4, 1024, 512], P(None, None, 'tensor')
- w_down_grad: float32 [4, 512, 1024], P(None, 'tensor')
The draws below stay inside these ranges and needn't reach their ends.
Inputs may be any that keep to these rules, and one draw needn't show every extreme that they name: `segments`: along each sequence the segment numbers never fall; a document has at most 512 tokens. `expert_choice`: each token names 2 different experts. In each sequence one expert is named by exactly 832 of its tokens, and each other expert by fewer. `dispatch_order`: each row is a permutation of the pair numbers t * 2 + k of one sequence.
All inputs are finite; a program needn't handle non-finite values.
Results may differ from the reference program's by a relative error of at most 0.014.
The reference program's roundings to bfloat16 on the way count: a program that leaves them out, or rounds other values in their place, can miss the bound.
Values sent between devices are 32-bit elements; how exact they have to be, the bound alone decides.
No kernel may reach another device: no remote copies, remote signals or barrier semaphores. Data moves between devices by JAX's collectives and lax.ppermute only.
A program may use at most 1.0625 GiB of HBM per device.

```python
import math
import jax
import jax.numpy as jnp
import numpy as np
from jax import lax

D = 1024
HEADS = 16
KV_HEADS = 8
HEAD_DIM = 64
EXP_HID = 512
EXPERTS = 4
TOPK = 2
TOK_DEV = 1024
SEQS = 16
TOKENS = 16384
CAP = 640
SEGS = 4
MOST = 512


def draw_expert_choice(key, part):
    seq_keys = jax.random.split(jax.random.fold_in(key, 11), SEQS)
    ranks = jax.vmap(lambda single: jax.random.permutation(single, TOK_DEV))(seq_keys).astype(jnp.int32)
    favoured = jax.random.randint(jax.random.fold_in(key, 12), (SEQS, 1), 0, EXPERTS).astype(jnp.int32)
    busy_count = 13 * TOK_DEV // 16
    holds = ranks < busy_count
    first_off = jax.random.randint(jax.random.fold_in(key, 13), (SEQS, TOK_DEV), 1, EXPERTS).astype(jnp.int32)
    step_off = jax.random.randint(jax.random.fold_in(key, 14), (SEQS, TOK_DEV), 1, EXPERTS - 1).astype(jnp.int32)
    second_off = 1 + (first_off - 1 + step_off) % (EXPERTS - 1)
    column_a = jnp.where(holds, favoured, (favoured + first_off) % EXPERTS)
    column_b = jnp.where(holds, (favoured + first_off) % EXPERTS, (favoured + second_off) % EXPERTS)
    flipped = jax.random.randint(jax.random.fold_in(key, 15), (SEQS, TOK_DEV), 0, 2).astype(jnp.int32)
    left_col = jnp.where(flipped == 1, column_b, column_a)
    right_col = jnp.where(flipped == 1, column_a, column_b)
    return jnp.stack([left_col, right_col], axis=-1).reshape(TOKENS, TOPK).astype(jnp.int32)


def block_scale(stream_key, shape, pieces, low, largest):
    gain = 1.0
    for axis_at, parts in pieces:
        steps = jax.random.uniform(jax.random.fold_in(jax.random.fold_in(stream_key, 6), axis_at), (parts,), jnp.float32, low / len(pieces), largest / len(pieces))
        gain = gain * jnp.repeat(jnp.exp(steps), shape[axis_at] // parts).reshape((-1,) + (1,) * (len(shape) - 1 - axis_at))
    return gain


def length_profile(number_of, total, limit, skew):
    loads = [(1 << 20) // math.isqrt(grade ** skew) + 1 for grade in range(2, number_of + 1)]
    rest, holding = total - limit - (number_of - 1), [1] * (number_of - 1)
    while rest > 0:
        movable = [i for i in range(number_of - 1) if holding[i] < limit]
        mass, left = sum([loads[i] for i in movable]), rest
        for i in movable:
            more = min(limit - holding[i], max(1, left * loads[i] // mass), rest)
            holding[i] = holding[i] + more
            rest = rest - more
    return np.array([limit] + holding)


def uneven_parts(own_key, amount, total, limit, skew):
    if amount == 2:
        one = jax.random.randint(own_key, (), max(1, total - limit), min(limit, total - 1) + 1)
        return jnp.stack([one, total - one])
    sizes = jnp.asarray(length_profile(amount, total, limit, skew), jnp.int32)
    pairs = (amount - 1) // 2
    source_of, taker = sizes[1:1 + 2 * pairs:2], sizes[2:2 + 2 * pairs:2]
    slack = jnp.minimum(source_of - 1, limit - taker)
    shifted = jax.random.randint(jax.random.fold_in(own_key, 1), (pairs,), 0, 1 << 20) % (slack + 1)
    sizes = sizes.at[1:1 + 2 * pairs:2].set(source_of - shifted).at[2:2 + 2 * pairs:2].set(taker + shifted)
    return sizes[jax.random.permutation(jax.random.fold_in(own_key, 2), amount)]


def normal_values(key, extent, scale, limit, shards=(), kind=jnp.bfloat16):
    values = scale * jax.random.normal(key, extent, jnp.float32)
    if shards:
        values = values * block_scale(key, extent, shards, -0.22, 0.18)
    return jnp.clip(values, -limit, limit).astype(kind)


def setup_inputs(seed: int = 0) -> dict:
    splits = jax.random.split(jax.random.key(seed), 16)
    layer_input = normal_values(splits[0], (TOKENS, D), 1.0, 6.0, ((0, 16),))
    segments = jax.vmap(lambda own: jnp.searchsorted(jnp.cumsum(uneven_parts(own, SEGS, TOK_DEV, MOST, 1)), jnp.arange(TOK_DEV), side="right"))(jax.random.split(splits[1], SEQS)).reshape((SEQS, TOK_DEV)).astype(jnp.int32)
    expert_choice = draw_expert_choice(jax.random.fold_in(splits[15], 71), 0)
    dispatch_order = jax.vmap(lambda own: jax.random.permutation(own, TOK_DEV * TOPK))(jax.random.split(splits[3], SEQS)).reshape((SEQS, TOK_DEV * TOPK)).astype(jnp.int32)
    norm_gain_one = jnp.clip(1.0 + 0.1 * jax.random.normal(splits[4], (D,), jnp.float32), 0.5, 1.5)
    w_query = normal_values(splits[5], (D, HEADS * HEAD_DIM), D ** -0.5, 0.1875, ((1, 2),))
    w_key = normal_values(splits[6], (D, KV_HEADS * HEAD_DIM), D ** -0.5, 0.1875, ((1, 2),))
    w_value = normal_values(splits[7], (D, KV_HEADS * HEAD_DIM), D ** -0.5, 0.1875, ((1, 2),))
    w_out = normal_values(splits[8], (HEADS * HEAD_DIM, D), (HEADS * HEAD_DIM // 32) ** -0.5, 1.0, ((0, 2),))
    norm_gain_two = jnp.clip(1.0 + 0.1 * jax.random.normal(splits[9], (D,), jnp.float32), 0.5, 1.5)
    w_router = normal_values(splits[10], (D, EXPERTS), (2 * D) ** -0.5, 0.125)
    w_gate = normal_values(splits[11], (EXPERTS, D, EXP_HID), D ** -0.5, 0.1875, ((2, 2),))
    w_up = normal_values(splits[12], (EXPERTS, D, EXP_HID), D ** -0.5, 0.1875, ((2, 2),))
    w_down = normal_values(splits[13], (EXPERTS, EXP_HID, D), (EXP_HID // 4) ** -0.5, 0.5, ((1, 2),))
    out_grad = normal_values(splits[14], (TOKENS, D), 1.0, 6.0, ((0, 16),))
    return dict(layer_input=layer_input, segments=segments, expert_choice=expert_choice, dispatch_order=dispatch_order, norm_gain_one=norm_gain_one, w_query=w_query, w_key=w_key, w_value=w_value, w_out=w_out, norm_gain_two=norm_gain_two, w_router=w_router, w_gate=w_gate, w_up=w_up, w_down=w_down, out_grad=out_grad)


highest = lax.Precision.HIGHEST
norm_eps = 1e-05
masked_value = -1e+30

@jax.custom_vjp
def low(v):
    return lax.optimization_barrier(v.astype(jnp.bfloat16)).astype(jnp.float32)

@jax.custom_vjp
def low_back(v):
    return v

def low_keep(v):
    return (low(v), None)

def low_pass(kept, grad):
    return (grad,)

def back_keep(v):
    return (v, None)

def back_low(kept, grad):
    return (low(grad),)
low.defvjp(low_keep, low_pass)
low_back.defvjp(back_keep, back_low)

def matmul(left, right):
    return jnp.dot(left, right, precision=highest, preferred_element_type=jnp.float32)

def rms_scale(values, gain_vec):
    return values * lax.rsqrt(lax.optimization_barrier(jnp.mean(values * values, axis=-1, keepdims=True)) + norm_eps) * gain_vec

def softmax_last(values):
    peak_value = lax.optimization_barrier(jnp.max(values, axis=-1, keepdims=True))
    raised = jnp.exp(values - peak_value)
    return raised / lax.optimization_barrier(jnp.sum(raised, axis=-1, keepdims=True))

def dispatch_tables(choice_rows, order_row):
    pair_count = order_row.shape[0]
    pair_expert = choice_rows.reshape(-1)
    ordered = pair_expert[order_row]
    expert_ids = jnp.arange(EXPERTS, dtype=jnp.int32)
    one_hot = (ordered[:, None] == expert_ids[None, :]).astype(jnp.int32)
    earlier = lax.optimization_barrier(jnp.sum((jnp.cumsum(one_hot, axis=0) - one_hot) * one_hot, axis=1))
    target = jnp.where(earlier < CAP, ordered * CAP + earlier, EXPERTS * CAP).astype(jnp.int32)
    pair_target = jnp.zeros((pair_count,), jnp.int32).at[order_row].set(target)
    pair_ids = jnp.arange(pair_count, dtype=jnp.int32)
    empty_token = choice_rows.shape[0]
    slot_token = jnp.full((EXPERTS * CAP + 1,), empty_token, jnp.int32).at[pair_target].set(pair_ids // TOPK)
    slot_pair = jnp.full((EXPERTS * CAP + 1,), pair_count, jnp.int32).at[pair_target].set(pair_ids)
    return (slot_token[:EXPERTS * CAP], slot_pair[:EXPERTS * CAP])

def attend_sequence(packed):
    query_heads, key_heads, value_heads, seg_ids = packed
    group_size = HEADS // KV_HEADS
    keys_wide = jnp.repeat(key_heads, group_size, axis=1)
    values_wide = jnp.repeat(value_heads, group_size, axis=1)
    scores = jnp.einsum('qhd,khd->hqk', query_heads, keys_wide, precision=highest) * HEAD_DIM ** (-0.5)
    positions = jnp.arange(TOK_DEV, dtype=jnp.int32)
    allowed = (seg_ids[:, None] == seg_ids[None, :]) & (positions[None, :] <= positions[:, None])
    scores = low_back(jnp.where(allowed[None], scores, masked_value))
    probs_low = low(softmax_last(scores))
    attended = jnp.einsum('hqk,khd->qhd', probs_low, values_wide, precision=highest)
    return low_back(low(attended))

def expert_sequence(normed, gating, w_gate, w_up, w_down, slot_token, slot_pair):
    padded = jnp.concatenate([normed, jnp.zeros((1, D), normed.dtype)], axis=0)
    routed_rows = padded[slot_token].reshape(EXPERTS, CAP, D)
    gate_flat = jnp.concatenate([gating.reshape(-1), jnp.zeros((1,), gating.dtype)])
    slot_weight = gate_flat[slot_pair]
    gate_proj = low_back(jnp.einsum('ecd,edf->ecf', routed_rows, w_gate, precision=highest))
    up_proj = low_back(jnp.einsum('ecd,edf->ecf', routed_rows, w_up, precision=highest))
    hidden = low(gate_proj * jax.nn.sigmoid(gate_proj) * up_proj)
    expert_out = low_back(jnp.einsum('ecf,efd->ecd', hidden, w_down, precision=highest)).reshape(EXPERTS * CAP, D)
    combined = jnp.zeros((TOK_DEV + 1, D), expert_out.dtype).at[slot_token].add(slot_weight[:, None] * expert_out)
    return combined[:TOK_DEV]

def reference(layer_input, segments, expert_choice, dispatch_order, norm_gain_one, w_query, w_key, w_value, w_out, norm_gain_two, w_router, w_gate, w_up, w_down, out_grad):
    choice_rows = expert_choice.reshape(SEQS, TOK_DEV, TOPK)
    slot_token, slot_pair = jax.vmap(dispatch_tables)(choice_rows, dispatch_order)

    def forward(hidden_in, gain_one, query_w, key_w, value_w, out_w, gain_two, router_w, gate_w, up_w, down_w):
        residual = hidden_in.reshape(SEQS, TOK_DEV, D)
        normed_one = low(rms_scale(residual, gain_one))
        query_heads = low_back(low(matmul(normed_one, query_w))).reshape(SEQS, TOK_DEV, HEADS, HEAD_DIM)
        key_heads = low_back(low(matmul(normed_one, key_w))).reshape(SEQS, TOK_DEV, KV_HEADS, HEAD_DIM)
        value_heads = low_back(low(matmul(normed_one, value_w))).reshape(SEQS, TOK_DEV, KV_HEADS, HEAD_DIM)
        attended = lax.map(jax.checkpoint(attend_sequence), (query_heads, key_heads, value_heads, segments))
        attn_total = low_back(matmul(attended.reshape(SEQS, TOK_DEV, HEADS * HEAD_DIM), out_w))
        middle = residual + attn_total
        normed_two = low(rms_scale(middle, gain_two))
        logits = low_back(matmul(normed_two, router_w))
        picked = jnp.take_along_axis(logits, choice_rows, axis=-1)
        gating = softmax_last(picked)
        routed = jax.vmap(expert_sequence, in_axes=(0, 0, None, None, None, 0, 0))(normed_two, gating, gate_w, up_w, down_w, slot_token, slot_pair)
        return (middle + routed).reshape(SEQS * TOK_DEV, D)
    params = tuple((member.astype(jnp.float32) for member in (layer_input, norm_gain_one, w_query, w_key, w_value, w_out, norm_gain_two, w_router, w_gate, w_up, w_down)))
    result, pullback = jax.vjp(forward, *params)
    grads = pullback(out_grad.astype(jnp.float32))
    return (result.astype(jnp.bfloat16), grads[0], grads[1], grads[2], grads[3], grads[4], grads[5], grads[6], grads[7], grads[8], grads[9], grads[10])
```

```python
import jax
import jax.numpy as jnp
from jax import lax
from jax.sharding import PartitionSpec as P

D = 1024
HEAD_DIM = 64
EXPERTS = 4
TOPK = 2
CAP = 640


norm_eps = 1e-05
masked_value = -1e30


def normalize(values):
    inverse = lax.rsqrt(jnp.mean(values * values, axis=-1, keepdims=True) + norm_eps)
    return (values * inverse, inverse)


def norm_back(grad_normed, normed, inverse, gain_vec):
    scaled = grad_normed * gain_vec
    mean_term = jnp.mean(scaled * normed, axis=-1, keepdims=True)
    return (inverse * (scaled - normed * mean_term), jnp.sum(grad_normed * normed, axis=0))


def softmax_last(values):
    peak_value = jnp.max(values, axis=-1, keepdims=True)
    raised = jnp.exp(values - peak_value)
    return raised / jnp.sum(raised, axis=-1, keepdims=True)


def dispatch_tables(choice_rows, order_row):
    pair_count = order_row.shape[0]
    pair_expert = choice_rows.reshape(-1)
    ordered = pair_expert[order_row]
    expert_ids = jnp.arange(EXPERTS, dtype=jnp.int32)
    one_hot = (ordered[:, None] == expert_ids[None, :]).astype(jnp.int32)
    earlier = jnp.sum((jnp.cumsum(one_hot, axis=0) - one_hot) * one_hot, axis=1)
    target = jnp.where(earlier < CAP, ordered * CAP + earlier, EXPERTS * CAP)
    pair_target = jnp.zeros((pair_count,), jnp.int32).at[order_row].set(target)
    pair_ids = jnp.arange(pair_count, dtype=jnp.int32)
    empty_token = choice_rows.shape[0]
    slot_token = (
        jnp.full((EXPERTS * CAP + 1,), empty_token, jnp.int32).at[pair_target].set(pair_ids // TOPK)
    )
    slot_pair = jnp.full((EXPERTS * CAP + 1,), pair_count, jnp.int32).at[pair_target].set(pair_ids)
    return (slot_token[: EXPERTS * CAP], slot_pair[: EXPERTS * CAP])


def block_scores(query_block, key_heads, seg_query, seg_keys, begin_row, score_scale):
    scores = (
        jnp.einsum("rkgd,ckd->kgrc", query_block, key_heads, preferred_element_type=jnp.float32)
        * score_scale
    )
    row_pos = begin_row + jnp.arange(query_block.shape[0], dtype=jnp.int32)
    col_pos = jnp.arange(key_heads.shape[0], dtype=jnp.int32)
    allowed = (seg_query[:, None] == seg_keys[None, :]) & (col_pos[None, :] <= row_pos[:, None])
    return jnp.where(allowed, scores, masked_value)


def pack_grads(parts_count, wide, tall, vectors):
    rows = jnp.concatenate(wide + tall + [jnp.stack(vectors)], axis=0)
    return jnp.pad(rows, ((0, -rows.shape[0] % (8 * parts_count)), (0, 0)))


def per_device(
    layer_input,
    segments,
    expert_choice,
    dispatch_order,
    norm_gain_one,
    w_query,
    w_key,
    w_value,
    w_out,
    norm_gain_two,
    w_router,
    w_gate,
    w_up,
    w_down,
    out_grad,
):
    length = layer_input.shape[0]
    score_scale = HEAD_DIM ** (-0.5)
    local_heads = w_query.shape[1] // HEAD_DIM
    local_kv = w_key.shape[1] // HEAD_DIM
    group_size = local_heads // local_kv
    block_rows = min(512, length)
    parts_count = lax.axis_size("dp")
    seg_ids = segments[0]
    residual = layer_input.astype(jnp.float32)
    normed_one, inverse_one = normalize(residual)
    input_one = (normed_one * norm_gain_one).astype(jnp.bfloat16)
    query_heads = (
        jnp.dot(input_one, w_query, preferred_element_type=jnp.float32)
        .astype(jnp.bfloat16)
        .reshape(length, local_kv, group_size, HEAD_DIM)
    )
    key_heads = (
        jnp.dot(input_one, w_key, preferred_element_type=jnp.float32)
        .astype(jnp.bfloat16)
        .reshape(length, local_kv, HEAD_DIM)
    )
    value_heads = (
        jnp.dot(input_one, w_value, preferred_element_type=jnp.float32)
        .astype(jnp.bfloat16)
        .reshape(length, local_kv, HEAD_DIM)
    )
    heads_out = []
    log_sums = []
    for begin_row in range(0, length, block_rows):
        finish = begin_row + block_rows
        scores = block_scores(
            query_heads[begin_row:finish],
            key_heads[:finish],
            seg_ids[begin_row:finish],
            seg_ids[:finish],
            begin_row,
            score_scale,
        )
        row_peak = jnp.max(scores, axis=-1, keepdims=True)
        raised = jnp.exp(scores - row_peak)
        row_total = jnp.sum(raised, axis=-1, keepdims=True)
        probs_low = (raised / row_total).astype(jnp.bfloat16)
        heads_out.append(
            jnp.einsum(
                "kgrc,ckd->rkgd",
                probs_low,
                value_heads[:finish],
                preferred_element_type=jnp.float32,
            ).astype(jnp.bfloat16)
        )
        log_sums.append(row_peak + jnp.log(row_total))
    attended = jnp.concatenate(heads_out, axis=0).reshape(length, local_heads * HEAD_DIM)
    attn_part = jnp.dot(attended, w_out, preferred_element_type=jnp.float32)
    attn_total = lax.psum(attn_part, "tensor")
    middle = residual + attn_total
    normed_two, inverse_two = normalize(middle)
    input_two = (normed_two * norm_gain_two).astype(jnp.bfloat16)
    logits = jnp.dot(input_two, w_router, preferred_element_type=jnp.float32)
    choice_hot = (
        expert_choice[:, :, None] == jnp.arange(EXPERTS, dtype=jnp.int32)[None, None, :]
    ).astype(jnp.float32)
    picked = jnp.sum(logits[:, None, :] * choice_hot, axis=-1)
    gating = softmax_last(picked)
    slot_token, slot_pair = dispatch_tables(expert_choice, dispatch_order[0])
    padded = jnp.concatenate([input_two, jnp.zeros((1, D), jnp.bfloat16)], axis=0)
    routed_rows = padded[slot_token].reshape(EXPERTS, CAP, D)
    pair_total = length * TOPK
    gate_flat = jnp.concatenate([gating.reshape(-1), jnp.zeros((1,), jnp.float32)])
    slot_weight = gate_flat[slot_pair]
    gate_proj = jnp.einsum("ecd,edf->ecf", routed_rows, w_gate, preferred_element_type=jnp.float32)
    up_proj = jnp.einsum("ecd,edf->ecf", routed_rows, w_up, preferred_element_type=jnp.float32)
    sigma_gate = jax.nn.sigmoid(gate_proj)
    activated = gate_proj * sigma_gate
    hidden = (activated * up_proj).astype(jnp.bfloat16)
    expert_part = jnp.einsum(
        "ecf,efd->ecd", hidden, w_down, preferred_element_type=jnp.float32
    ).reshape(EXPERTS * CAP, D)
    routed_part = (
        jnp.zeros((length + 1, D), jnp.float32)
        .at[slot_token]
        .add(slot_weight[:, None] * expert_part)[:length]
    )
    routed_total = lax.psum(routed_part, "tensor")
    block_out = (middle + routed_total).astype(jnp.bfloat16)
    grad_top = out_grad.astype(jnp.float32)
    grad_padded = jnp.concatenate([grad_top, jnp.zeros((1, D), jnp.float32)], axis=0)
    slot_grad = grad_padded[slot_token]
    grad_expert = (slot_weight[:, None] * slot_grad).astype(jnp.bfloat16).reshape(EXPERTS, CAP, D)
    gate_slot_part = jnp.sum(slot_grad * expert_part, axis=-1)
    gate_pair_part = (
        jnp.zeros((pair_total + 1,), jnp.float32)
        .at[slot_pair]
        .add(gate_slot_part)[:pair_total]
        .reshape(length, TOPK)
    )
    grad_hidden = jnp.einsum(
        "ecd,efd->ecf", grad_expert, w_down, preferred_element_type=jnp.float32
    )
    grad_wdown = jnp.einsum("ecf,ecd->efd", hidden, grad_expert, preferred_element_type=jnp.float32)
    grad_gate_proj = (
        grad_hidden * up_proj * sigma_gate * (1.0 + gate_proj * (1.0 - sigma_gate))
    ).astype(jnp.bfloat16)
    grad_up_proj = (grad_hidden * activated).astype(jnp.bfloat16)
    grad_wgate = jnp.einsum(
        "ecd,ecf->edf", routed_rows, grad_gate_proj, preferred_element_type=jnp.float32
    )
    grad_wup = jnp.einsum(
        "ecd,ecf->edf", routed_rows, grad_up_proj, preferred_element_type=jnp.float32
    )
    grad_rows = jnp.einsum(
        "ecf,edf->ecd", grad_gate_proj, w_gate, preferred_element_type=jnp.float32
    )
    grad_rows = (
        grad_rows
        + jnp.einsum("ecf,edf->ecd", grad_up_proj, w_up, preferred_element_type=jnp.float32)
    ).reshape(EXPERTS * CAP, D)
    routed_grad_part = (
        jnp.zeros((length + 1, D), jnp.float32).at[slot_token].add(grad_rows)[:length]
    )
    routed_grad, gate_pair_grad = lax.psum((routed_grad_part, gate_pair_part), "tensor")
    grad_picked = gating * (
        gate_pair_grad - jnp.sum(gating * gate_pair_grad, axis=-1, keepdims=True)
    )
    grad_logits = jnp.sum(grad_picked[:, :, None] * choice_hot, axis=1).astype(jnp.bfloat16)
    grad_router = jnp.einsum(
        "td,te->de", input_two, grad_logits, preferred_element_type=jnp.float32
    )
    grad_input_two = routed_grad + jnp.einsum(
        "te,de->td", grad_logits, w_router, preferred_element_type=jnp.float32
    )
    grad_middle_norm, grad_gain_two = norm_back(
        grad_input_two, normed_two, inverse_two, norm_gain_two
    )
    grad_middle = grad_top + grad_middle_norm
    grad_attn = grad_middle.astype(jnp.bfloat16)
    grad_wout = jnp.einsum("tn,td->nd", attended, grad_attn, preferred_element_type=jnp.float32)
    grad_heads = (
        jnp.einsum("td,nd->tn", grad_attn, w_out, preferred_element_type=jnp.float32)
        .astype(jnp.bfloat16)
        .reshape(length, local_kv, group_size, HEAD_DIM)
    )
    grad_keys_sum = jnp.zeros((length, local_kv, HEAD_DIM), jnp.float32)
    grad_values_sum = jnp.zeros((length, local_kv, HEAD_DIM), jnp.float32)
    grad_query_list = []
    for index_block, begin_row in enumerate(range(0, length, block_rows)):
        finish = begin_row + block_rows
        query_block = query_heads[begin_row:finish]
        scores = block_scores(
            query_block,
            key_heads[:finish],
            seg_ids[begin_row:finish],
            seg_ids[:finish],
            begin_row,
            score_scale,
        )
        probs_exact = jnp.exp(scores - log_sums[index_block])
        probs_low = probs_exact.astype(jnp.bfloat16)
        grad_out_block = grad_heads[begin_row:finish]
        grad_probs = jnp.einsum(
            "rkgd,ckd->kgrc",
            grad_out_block,
            value_heads[:finish],
            preferred_element_type=jnp.float32,
        )
        row_dot = jnp.sum(probs_exact * grad_probs, axis=-1, keepdims=True)
        grad_scores = (probs_exact * (grad_probs - row_dot)).astype(jnp.bfloat16)
        grad_query_list.append(
            (
                jnp.einsum(
                    "kgrc,ckd->rkgd",
                    grad_scores,
                    key_heads[:finish],
                    preferred_element_type=jnp.float32,
                )
                * score_scale
            ).astype(jnp.bfloat16)
        )
        grad_keys_sum = grad_keys_sum.at[:finish].add(
            jnp.einsum(
                "kgrc,rkgd->ckd", grad_scores, query_block, preferred_element_type=jnp.float32
            )
            * score_scale
        )
        grad_values_sum = grad_values_sum.at[:finish].add(
            jnp.einsum(
                "kgrc,rkgd->ckd", probs_low, grad_out_block, preferred_element_type=jnp.float32
            )
        )
    grad_query = jnp.concatenate(grad_query_list, axis=0).reshape(length, local_heads * HEAD_DIM)
    grad_keys = grad_keys_sum.astype(jnp.bfloat16).reshape(length, local_kv * HEAD_DIM)
    grad_values = grad_values_sum.astype(jnp.bfloat16).reshape(length, local_kv * HEAD_DIM)
    grad_wquery = jnp.einsum("td,tn->dn", input_one, grad_query, preferred_element_type=jnp.float32)
    grad_wkey = jnp.einsum("td,tn->dn", input_one, grad_keys, preferred_element_type=jnp.float32)
    grad_wvalue = jnp.einsum(
        "td,tn->dn", input_one, grad_values, preferred_element_type=jnp.float32
    )
    input_grad_part = jnp.einsum(
        "tn,dn->td", grad_query, w_query, preferred_element_type=jnp.float32
    )
    input_grad_part = input_grad_part + jnp.einsum(
        "tn,dn->td", grad_keys, w_key, preferred_element_type=jnp.float32
    )
    input_grad_part = input_grad_part + jnp.einsum(
        "tn,dn->td", grad_values, w_value, preferred_element_type=jnp.float32
    )
    input_grad_one = lax.psum(input_grad_part, "tensor")
    grad_resid_norm, grad_gain_one = norm_back(
        input_grad_one, normed_one, inverse_one, norm_gain_one
    )
    grad_input = grad_middle + grad_resid_norm
    gate_wide = jnp.concatenate([grad_wgate[e] for e in range(EXPERTS)], axis=1)
    up_wide = jnp.concatenate([grad_wup[e] for e in range(EXPERTS)], axis=1)
    qkv_wide = jnp.concatenate([grad_wquery, grad_wkey, grad_wvalue], axis=1)
    hidden_part = w_down.shape[1]
    down_rows = grad_wdown.reshape(EXPERTS * hidden_part, D)
    packed = pack_grads(
        parts_count,
        [gate_wide, up_wide, qkv_wide],
        [down_rows, grad_wout],
        [grad_gain_one, grad_gain_two] + [grad_router[:, e] for e in range(EXPERTS)],
    )
    shares = lax.psum_scatter(packed, "dp", scatter_dimension=0, tiled=True)
    total = lax.all_gather(shares, "dp", axis=0, tiled=True)
    split = [hidden_part * e for e in range(EXPERTS + 1)]
    sum_gate = jnp.stack([total[:D, split[e] : split[e + 1]] for e in range(EXPERTS)])
    sum_up = jnp.stack([total[D : 2 * D, split[e] : split[e + 1]] for e in range(EXPERTS)])
    q_cols = w_query.shape[1]
    kv_cols = w_key.shape[1]
    sum_query = total[2 * D : 3 * D, :q_cols]
    sum_key = total[2 * D : 3 * D, q_cols : q_cols + kv_cols]
    sum_value = total[2 * D : 3 * D, q_cols + kv_cols : q_cols + 2 * kv_cols]
    at = 3 * D
    sum_down = total[at : at + EXPERTS * hidden_part].reshape(w_down.shape)
    at += EXPERTS * hidden_part
    sum_out = total[at : at + w_out.shape[0]]
    at += w_out.shape[0]
    small = total[at : at + 2 + EXPERTS]
    return (
        block_out,
        grad_input,
        small[0],
        sum_query,
        sum_key,
        sum_value,
        sum_out,
        small[1],
        small[2 : 2 + EXPERTS].T,
        sum_gate,
        sum_up,
        sum_down,
    )


def solution(mesh):
    in_specs = (
        P("dp", None),
        P("dp", None),
        P("dp", None),
        P("dp", None),
        P(),
        P(None, "tensor"),
        P(None, "tensor"),
        P(None, "tensor"),
        P("tensor", None),
        P(),
        P(),
        P(None, None, "tensor"),
        P(None, None, "tensor"),
        P(None, "tensor", None),
        P("dp", None),
    )
    out_specs = (
        P("dp", None),
        P("dp", None),
        P(),
        P(None, "tensor"),
        P(None, "tensor"),
        P(None, "tensor"),
        P("tensor", None),
        P(),
        P(),
        P(None, None, "tensor"),
        P(None, None, "tensor"),
        P(None, "tensor", None),
    )
    return jax.shard_map(
        per_device, mesh=mesh, in_specs=in_specs, out_specs=out_specs, check_vma=False
    )
```

```python
import functools

import jax
import jax.numpy as jnp
from jax import lax
from jax.experimental import pallas as pl
from jax.experimental.pallas import tpu as pltpu
from jax.sharding import PartitionSpec as P

D = 1024
HEAD_DIM = 64
EXPERTS = 4
TOPK = 2
CAP = 640
MOST = 512
ROWS8 = 8

norm_eps = 1e-05
masked_value = -1e30
f32 = jnp.float32
bf16 = jnp.bfloat16
i32 = jnp.int32

NN = (((1,), (0,)), ((), ()))
NT = (((1,), (1,)), ((), ()))
TN = (((0,), (0,)), ((), ()))


def mm(left, right, dims=NN):
    return lax.dot_general(left, right, dims, preferred_element_type=f32)


def full_spec(shape):
    zeros = (0,) * len(shape)
    return pl.BlockSpec(shape, lambda *_: zeros, pipeline_mode=pl.Buffered(1))


def route_kernel(choice_ref, order_ref, slot_ref):
    length = choice_ref.shape[1]
    pairs = 2 * length
    order = order_ref[...]
    where_pair = (order & 1) * length + (order >> 1)
    match = (lax.broadcasted_iota(i32, (pairs, pairs), 0) == where_pair).astype(f32).astype(bf16)
    experts = lax.broadcasted_iota(i32, (ROWS8, length), 0)
    first = (choice_ref[0:1, :] == experts).astype(f32)
    second = (choice_ref[1:2, :] == experts).astype(f32)
    hot = jnp.concatenate([first, second], axis=1)
    ordered = mm(hot.astype(bf16), match)
    step = 512
    tri = (
        lax.broadcasted_iota(i32, (step, step), 0) < lax.broadcasted_iota(i32, (step, step), 1)
    ).astype(f32)
    carry = jnp.zeros((ROWS8, 1), f32)
    ranks = []
    for begin in range(0, pairs, step):
        part = ordered[:, begin : begin + step]
        inside = mm(part.astype(bf16), tri.astype(bf16)) + carry
        ranks.append(jnp.sum(inside * part, axis=0, keepdims=True))
        carry = carry + jnp.sum(part, axis=1, keepdims=True)
    rank = jnp.concatenate(ranks, axis=1)
    high = jnp.floor(rank * (1.0 / 64.0))
    low_part = rank - 64.0 * high
    row_id = lax.broadcasted_iota(i32, (ROWS8, pairs), 0)
    both = jnp.where(row_id == 0, high, jnp.where(row_id == 1, low_part, 0.0))
    back = mm(both.astype(bf16), match, NT)
    slot = (64.0 * back[0:1, :] + back[1:2, :]).astype(i32)
    slot_ref[...] = jnp.where(
        first > 0.5, slot[:, :length], jnp.where(second > 0.5, slot[:, length:], -1)
    )


def route(choice_t, order):
    length = choice_t.shape[1]
    return pl.pallas_call(
        route_kernel,
        out_shape=jax.ShapeDtypeStruct((ROWS8, length), i32),
        compiler_params=pltpu.CompilerParams(vmem_limit_bytes=50 << 20),
        name="route",
    )(choice_t, order)


def attn_blocks(length, rows):
    blocks = []
    for begin in range(0, length, rows):
        start = max(0, begin + rows - MOST - rows)
        start = max(0, (begin + 1 - MOST) // 128 * 128)
        blocks.append((begin, start, begin + rows))
    return blocks


def attn_fwd_kernel(rows, q_ref, k_ref, v_ref, segc_ref, segr_ref, o_ref):
    length = q_ref.shape[0]
    for begin, start, stop in attn_blocks(length, rows):
        wide = stop - start
        row_pos = begin + lax.broadcasted_iota(i32, (rows, wide), 0)
        col_pos = start + lax.broadcasted_iota(i32, (rows, wide), 1)
        allowed = (segc_ref[begin:stop, :] == segr_ref[:, start:stop]) & (col_pos <= row_pos)
        bias = jnp.where(allowed, 0.0, masked_value)
        bias = jnp.concatenate([bias, bias], axis=0)
        for kv in range(2):
            lo = kv * HEAD_DIM
            q_two = jnp.concatenate(
                [
                    q_ref[begin:stop, 2 * lo : 2 * lo + HEAD_DIM],
                    q_ref[begin:stop, 2 * lo + HEAD_DIM : 2 * lo + 2 * HEAD_DIM],
                ],
                axis=0,
            )
            q_two = q_two * jnp.asarray(HEAD_DIM**-0.5, bf16)
            scores = mm(q_two, k_ref[start:stop, lo : lo + HEAD_DIM], NT) + bias
            peak = jnp.max(scores, axis=1, keepdims=True)
            raised = jnp.exp(scores - peak)
            total = jnp.sum(raised, axis=1, keepdims=True)
            probs = (raised * (1.0 / total)).astype(bf16)
            out = mm(probs, v_ref[start:stop, lo : lo + HEAD_DIM])
            out = out.astype(bf16).astype(f32)
            o_ref[begin:stop, 2 * lo : 2 * lo + 2 * HEAD_DIM] = jnp.concatenate(
                [out[:rows], out[rows:]], axis=1
            )


def attn_fwd(qkv, seg_col, seg_row, q_cols):
    length = qkv.shape[0]
    pairs = q_cols // 256
    return pl.pallas_call(
        functools.partial(attn_fwd_kernel, 256),
        grid=(pairs,),
        in_specs=[
            pl.BlockSpec((length, 256), lambda g: (0, g)),
            pl.BlockSpec((length, 128), lambda g: (0, 2 * pairs + g)),
            pl.BlockSpec((length, 128), lambda g: (0, 3 * pairs + g)),
            full_spec((length, 1)),
            full_spec((1, length)),
        ],
        out_specs=pl.BlockSpec((length, 256), lambda g: (0, g)),
        out_shape=jax.ShapeDtypeStruct((length, q_cols), f32),
        compiler_params=pltpu.CompilerParams(vmem_limit_bytes=50 << 20),
        name="attn_fwd",
    )(qkv, qkv, qkv, seg_col, seg_row)


def attn_bwd_kernel(
    rows, q_ref, k_ref, v_ref, do_ref, segc_ref, segr_ref, dq_ref, dk_ref, dv_ref, dks, dvs
):
    length = q_ref.shape[0]
    scale = HEAD_DIM**-0.5
    dks[...] = jnp.zeros_like(dks)
    dvs[...] = jnp.zeros_like(dvs)
    for begin, start, stop in attn_blocks(length, rows):
        wide = stop - start
        row_pos = begin + lax.broadcasted_iota(i32, (wide, rows), 1)
        col_pos = start + lax.broadcasted_iota(i32, (wide, rows), 0)
        allowed = (segr_ref[:, begin:stop] == segc_ref[start:stop, :]) & (col_pos <= row_pos)
        bias = jnp.where(allowed, 0.0, masked_value)
        bias = jnp.concatenate([bias, bias], axis=1)
        for kv in range(2):
            lo = kv * HEAD_DIM
            q_two = jnp.concatenate(
                [
                    q_ref[begin:stop, 2 * lo : 2 * lo + HEAD_DIM],
                    q_ref[begin:stop, 2 * lo + HEAD_DIM : 2 * lo + 2 * HEAD_DIM],
                ],
                axis=0,
            )
            q_two = q_two * jnp.asarray(scale, bf16)
            do_two = jnp.concatenate(
                [
                    do_ref[begin:stop, 2 * lo : 2 * lo + HEAD_DIM],
                    do_ref[begin:stop, 2 * lo + HEAD_DIM : 2 * lo + 2 * HEAD_DIM],
                ],
                axis=0,
            )
            k_win = k_ref[start:stop, lo : lo + HEAD_DIM]
            v_win = v_ref[start:stop, lo : lo + HEAD_DIM]
            scores = mm(k_win, q_two, NT) + bias
            peak = jnp.max(scores, axis=0, keepdims=True)
            raised = jnp.exp(scores - peak)
            total = jnp.sum(raised, axis=0, keepdims=True)
            probs = raised * (1.0 / total)
            grad_probs = mm(v_win, do_two, NT)
            row_dot = jnp.sum(probs * grad_probs, axis=0, keepdims=True)
            grad_scores = (probs * (grad_probs - row_dot)).astype(bf16)
            dvs[start:stop, lo : lo + HEAD_DIM] += mm(probs.astype(bf16), do_two)
            dks[start:stop, lo : lo + HEAD_DIM] += mm(grad_scores, q_two)
            dq = (mm(grad_scores, k_win, TN) * scale).astype(bf16)
            dq_ref[begin:stop, 2 * lo : 2 * lo + 2 * HEAD_DIM] = jnp.concatenate(
                [dq[:rows], dq[rows:]], axis=1
            )
    dk_ref[...] = dks[...].astype(bf16)
    dv_ref[...] = dvs[...].astype(bf16)


def attn_bwd(qkv, grad_heads, seg_col, seg_row, q_cols):
    length = qkv.shape[0]
    pairs = q_cols // 256
    return pl.pallas_call(
        functools.partial(attn_bwd_kernel, 256),
        grid=(pairs,),
        in_specs=[
            pl.BlockSpec((length, 256), lambda g: (0, g)),
            pl.BlockSpec((length, 128), lambda g: (0, 2 * pairs + g)),
            pl.BlockSpec((length, 128), lambda g: (0, 3 * pairs + g)),
            pl.BlockSpec((length, 256), lambda g: (0, g)),
            full_spec((length, 1)),
            full_spec((1, length)),
        ],
        out_specs=[
            pl.BlockSpec((length, 256), lambda g: (0, g)),
            pl.BlockSpec((length, 128), lambda g: (0, g)),
            pl.BlockSpec((length, 128), lambda g: (0, g)),
        ],
        out_shape=[
            jax.ShapeDtypeStruct((length, q_cols), bf16),
            jax.ShapeDtypeStruct((length, q_cols // 2), bf16),
            jax.ShapeDtypeStruct((length, q_cols // 2), bf16),
        ],
        scratch_shapes=[pltpu.VMEM((length, 128), f32), pltpu.VMEM((length, 128), f32)],
        compiler_params=pltpu.CompilerParams(vmem_limit_bytes=50 << 20),
        name="attn_bwd",
    )(qkv, qkv, qkv, grad_heads, seg_col, seg_row)


def moe_kernel(
    h_s,
    g2_ref,
    wr_ref,
    slotr_ref,
    slotc_ref,
    dy_ref,
    wg_ref,
    wu_ref,
    wd_ref,
    wgx_ref,
    wux_ref,
    wdx_ref,
    out_ref,
    dh_ref,
    dwg_ref,
    dwu_ref,
    dwd_ref,
    small_ref,
    xn_s,
    moe_s,
    gate_s,
    dgate_s,
):
    e = pl.program_id(0)
    length = h_s.shape[0]
    chunk = 256

    @pl.when(e == 0)
    def _():
        def start_rows(c, _):
            rows = pl.ds(pl.multiple_of(c * chunk, chunk), chunk)
            h1 = h_s[rows, :]
            inverse = lax.rsqrt(jnp.mean(h1 * h1, axis=1, keepdims=True) + norm_eps)
            xn_s[rows, :] = (h1 * inverse * g2_ref[...]).astype(bf16)
            return 0

        lax.fori_loop(0, length // chunk, start_rows, 0)
        moe_s[...] = jnp.zeros_like(moe_s)
        dh_ref[...] = jnp.zeros_like(dh_ref)
        dgate_s[...] = jnp.zeros_like(dgate_s)
        logits = mm(wr_ref[...].astype(bf16), xn_s[...], NT)
        chosen = slotr_ref[...] >= 0
        logits = jnp.where(chosen, logits, masked_value)
        peak = jnp.max(logits, axis=0, keepdims=True)
        raised = jnp.where(chosen, jnp.exp(logits - peak), 0.0)
        gate_s[...] = raised / jnp.sum(raised, axis=0, keepdims=True)

    xn = xn_s[...]
    slot_row = slotr_ref[pl.ds(e, 1), :]
    mask = lax.broadcasted_iota(i32, (CAP, length), 0) == slot_row
    place = mask.astype(f32).astype(bf16)
    lane8 = lax.broadcasted_iota(i32, (length, ROWS8), 1)
    slot_col = jnp.sum(jnp.where(lane8 == e, slotc_ref[...], 0), axis=1, keepdims=True)
    place_t = (lax.broadcasted_iota(i32, (length, CAP), 1) == slot_col).astype(f32).astype(bf16)
    gate = jnp.sum(jnp.where(mask, gate_s[pl.ds(e, 1), :], 0.0), axis=1, keepdims=True)
    rows_in = mm(place, xn).astype(bf16)
    dy_slot = mm(place, dy_ref[...])
    dy_gated = (gate * dy_slot).astype(bf16)

    halves = []
    y = None
    for own in (True, False):
        wg = wg_ref[0] if own else wgx_ref[...].astype(bf16)
        wu = wu_ref[0] if own else wux_ref[...].astype(bf16)
        wd = wd_ref[0] if own else wdx_ref[...].astype(bf16)
        g = mm(rows_in, wg)
        u = mm(rows_in, wu)
        sig = 1.0 / (1.0 + jnp.exp(-g))
        act = g * sig
        hid = (act * u).astype(bf16)
        part = mm(hid, wd)
        y = part if y is None else y + part
        dhid = mm(dy_gated, wd, NT)
        dg = (dhid * u * sig * (1.0 + g * (1.0 - sig))).astype(bf16)
        du = (dhid * act).astype(bf16)
        dx = mm(dg, wg, NT) + mm(du, wu, NT)
        halves.append(dx)
        if own:
            dwd_ref[...] = mm(hid, dy_gated, TN)
            dwg_ref[...] = mm(rows_in, dg, TN)
            dwu_ref[...] = mm(rows_in, du, TN)
    dgate_slot = jnp.sum(dy_slot * y, axis=1, keepdims=True)
    dgate_s[pl.ds(e, 1), :] = jnp.sum(jnp.where(mask, dgate_slot, 0.0), axis=0, keepdims=True)
    moe_s[...] += mm(place_t, (gate * y).astype(bf16))
    dh_ref[...] += mm(place_t, (halves[0] + halves[1]).astype(bf16))

    @pl.when(e == EXPERTS - 1)
    def _():
        gates = gate_s[...]
        dgates = dgate_s[...]
        dsel = gates * (dgates - jnp.sum(gates * dgates, axis=0, keepdims=True))
        dlog = dsel.astype(bf16)
        drouter = mm(dlog, xn_s[...])
        wr = wr_ref[...].astype(bf16)
        dlog_t = dsel.T.astype(bf16)
        small_ref[...] = jnp.zeros_like(small_ref)
        small_ref[0:EXPERTS, :] = drouter[0:EXPERTS, :]

        def end_rows(c, total):
            rows = pl.ds(pl.multiple_of(c * chunk, chunk), chunk)
            h1 = h_s[rows, :]
            inverse = lax.rsqrt(jnp.mean(h1 * h1, axis=1, keepdims=True) + norm_eps)
            n2 = h1 * inverse
            out_ref[rows, :] = (h1 + moe_s[rows, :]).astype(bf16)
            return total

        lax.fori_loop(0, length // chunk, end_rows, 0)
        gain = jnp.zeros((1, D), f32)
        for c in range(length // chunk):
            rows = slice(c * chunk, (c + 1) * chunk)
            h1 = h_s[rows, :]
            inverse = lax.rsqrt(jnp.mean(h1 * h1, axis=1, keepdims=True) + norm_eps)
            n2 = h1 * inverse
            dxn = dh_ref[rows, :] + mm(dlog_t[rows, :], wr)
            gain = gain + jnp.sum(dxn * n2, axis=0, keepdims=True)
            scaled = dxn * g2_ref[...]
            mean_term = jnp.mean(scaled * n2, axis=1, keepdims=True)
            dh_ref[rows, :] = dy_ref[rows, :].astype(f32) + inverse * (scaled - n2 * mean_term)
        small_ref[EXPERTS : EXPERTS + 1, :] = gain


def out_kernel(x_ref, oa_ref, ob_ref, wo_ref, wox_ref, h_ref):
    h_ref[...] = x_ref[...].astype(f32) + (
        mm(oa_ref[...].astype(bf16), wo_ref[...])
        + mm(ob_ref[...].astype(bf16), wox_ref[...].astype(bf16))
    )


def out_project(x, oa, ob, wo, other, at):
    length, q_cols = oa.shape
    rows = 256
    return pl.pallas_call(
        out_kernel,
        grid=(length // rows,),
        in_specs=[
            pl.BlockSpec((rows, D), lambda i: (i, 0)),
            pl.BlockSpec((rows, q_cols), lambda i: (i, 0)),
            pl.BlockSpec((rows, q_cols), lambda i: (i, 0)),
            full_spec((q_cols, D)),
            pl.BlockSpec((q_cols, D), lambda i: (at, 0), pipeline_mode=pl.Buffered(1)),
        ],
        out_specs=pl.BlockSpec((rows, D), lambda i: (i, 0)),
        out_shape=jax.ShapeDtypeStruct((length, D), f32),
        name="out_project",
    )(x, oa, ob, wo, other)


def moe(h1, other, g2, wr_t, slot_row, slot_col, dy, w_gate, w_up, w_down):
    length = h1.shape[0]
    hid = w_down.shape[1]
    wide = EXPERTS * hid
    down_at = 2 * D // hid
    return pl.pallas_call(
        moe_kernel,
        grid=(EXPERTS,),
        in_specs=[
            full_spec((length, D)),
            full_spec((1, D)),
            full_spec((ROWS8, D)),
            full_spec((ROWS8, length)),
            full_spec((length, ROWS8)),
            full_spec((length, D)),
            pl.BlockSpec((1, D, hid), lambda e: (e, 0, 0)),
            pl.BlockSpec((1, D, hid), lambda e: (e, 0, 0)),
            pl.BlockSpec((1, hid, D), lambda e: (e, 0, 0)),
            pl.BlockSpec((D, hid), lambda e: (0, e)),
            pl.BlockSpec((D, hid), lambda e: (1, e)),
            pl.BlockSpec((hid, D), lambda e: (down_at + e, 0)),
        ],
        out_specs=[
            full_spec((length, D)),
            full_spec((length, D)),
            pl.BlockSpec((D, hid), lambda e: (0, e)),
            pl.BlockSpec((D, hid), lambda e: (0, e)),
            pl.BlockSpec((hid, D), lambda e: (e, 0)),
            full_spec((ROWS8, D)),
        ],
        out_shape=[
            jax.ShapeDtypeStruct((length, D), bf16),
            jax.ShapeDtypeStruct((length, D), f32),
            jax.ShapeDtypeStruct((D, wide), f32),
            jax.ShapeDtypeStruct((D, wide), f32),
            jax.ShapeDtypeStruct((wide, D), f32),
            jax.ShapeDtypeStruct((ROWS8, D), f32),
        ],
        scratch_shapes=[
            pltpu.VMEM((length, D), bf16),
            pltpu.VMEM((length, D), f32),
            pltpu.VMEM((ROWS8, length), f32),
            pltpu.VMEM((ROWS8, length), f32),
        ],
        compiler_params=pltpu.CompilerParams(vmem_limit_bytes=60 << 20),
        name="moe",
    )(h1, g2, wr_t, slot_row, slot_col, dy, w_gate, w_up, w_down, other, other, other)


def swap_tensor(values):
    size = lax.axis_size("tensor")
    return lax.ppermute(values, "tensor", [(i, i ^ 1) for i in range(size)])


def gather_other(w_gate, w_up, w_down, w_out):
    parts = lax.axis_size("dp")
    packed = jnp.concatenate(
        [
            jnp.concatenate([w_gate[e] for e in range(EXPERTS)], axis=1),
            jnp.concatenate([w_up[e] for e in range(EXPERTS)], axis=1),
            w_down.reshape(-1, D),
            w_out,
        ],
        axis=0,
    )
    rows = packed.shape[0] // parts
    share = lax.dynamic_slice_in_dim(packed, lax.axis_index("dp") * rows, rows, 0).astype(f32)
    return lax.all_gather(swap_tensor(share), "dp", axis=0, tiled=True)


def sum_dp(values):
    share = lax.psum_scatter(values, "dp", scatter_dimension=0, tiled=True)
    return lax.all_gather(share, "dp", axis=0, tiled=True)


def per_device(
    layer_input,
    segments,
    expert_choice,
    dispatch_order,
    norm_gain_one,
    w_query,
    w_key,
    w_value,
    w_out,
    norm_gain_two,
    w_router,
    w_gate,
    w_up,
    w_down,
    out_grad,
):
    length = layer_input.shape[0]
    q_cols = w_query.shape[1]
    kv_cols = w_key.shape[1]
    hid = w_down.shape[1]
    wide = EXPERTS * hid
    other = gather_other(w_gate, w_up, w_down, w_out)
    slot_row = route(expert_choice.T, dispatch_order)
    slot_col = slot_row.T
    seg_row = segments
    seg_col = segments.reshape(length, 1)

    residual = layer_input.astype(f32)
    inverse_one = lax.rsqrt(jnp.mean(residual * residual, axis=-1, keepdims=True) + norm_eps)
    normed_one = residual * inverse_one
    input_one = (normed_one * norm_gain_one).astype(bf16)
    w_qkv = jnp.concatenate([w_query, w_key, w_value], axis=1)
    qkv = jnp.dot(input_one, w_qkv, preferred_element_type=f32).astype(bf16)
    attended = attn_fwd(qkv, seg_col, seg_row, q_cols)
    attended_other = swap_tensor(attended)

    wr_t = jnp.pad(w_router.T.astype(f32), ((0, ROWS8 - EXPERTS), (0, 0)))
    out_at = (2 * D + wide) // q_cols
    middle = out_project(layer_input, attended, attended_other, w_out, other, out_at)
    block_out, grad_middle, grad_gate, grad_up, grad_down, small = moe(
        middle,
        other,
        norm_gain_two[None, :],
        wr_t,
        slot_row,
        slot_col,
        out_grad,
        w_gate,
        w_up,
        w_down,
    )
    expert_sum = sum_dp(jnp.concatenate([grad_gate, grad_up, grad_down], axis=0))

    grad_attn = grad_middle.astype(bf16)
    attended_low = attended.astype(bf16)
    grad_wout = jnp.einsum("tn,td->nd", attended_low, grad_attn, preferred_element_type=f32)
    grad_heads = jnp.einsum("td,nd->tn", grad_attn, w_out, preferred_element_type=f32).astype(bf16)
    dq, dk, dv = attn_bwd(qkv, grad_heads, seg_col, seg_row, q_cols)
    dqkv = jnp.concatenate([dq, dk, dv], axis=1)
    grad_wqkv = jnp.einsum("td,tn->dn", input_one, dqkv, preferred_element_type=f32)
    part = jnp.einsum("tn,dn->td", dqkv, w_qkv, preferred_element_type=f32)
    grad_input_one = part + swap_tensor(part)
    scaled = grad_input_one * norm_gain_one
    mean_term = jnp.mean(scaled * normed_one, axis=-1, keepdims=True)
    grad_gain_one = jnp.sum(grad_input_one * normed_one, axis=0)
    grad_input = grad_middle + inverse_one * (scaled - normed_one * mean_term)

    small = jnp.concatenate([small[: EXPERTS + 1], grad_gain_one[None, :]], axis=0)
    packed = jnp.concatenate([grad_wqkv, grad_wout, small], axis=0)
    parts = lax.axis_size("dp")
    packed = jnp.pad(packed, ((0, -packed.shape[0] % (8 * parts)), (0, 0)))
    attn_sum = sum_dp(packed)

    sum_gate = jnp.stack([expert_sum[:D, hid * e : hid * (e + 1)] for e in range(EXPERTS)])
    sum_up = jnp.stack([expert_sum[D : 2 * D, hid * e : hid * (e + 1)] for e in range(EXPERTS)])
    sum_down = expert_sum[2 * D : 2 * D + wide].reshape(w_down.shape)
    at = D + q_cols
    return (
        block_out,
        grad_input,
        attn_sum[at + EXPERTS + 1],
        attn_sum[:D, :q_cols],
        attn_sum[:D, q_cols : q_cols + kv_cols],
        attn_sum[:D, q_cols + kv_cols :],
        attn_sum[D:at],
        attn_sum[at + EXPERTS],
        attn_sum[at : at + EXPERTS].T,
        sum_gate,
        sum_up,
        sum_down,
    )


def solution(mesh):
    in_specs = (
        P("dp", None),
        P("dp", None),
        P("dp", None),
        P("dp", None),
        P(),
        P(None, "tensor"),
        P(None, "tensor"),
        P(None, "tensor"),
        P("tensor", None),
        P(),
        P(),
        P(None, None, "tensor"),
        P(None, None, "tensor"),
        P(None, "tensor", None),
        P("dp", None),
    )
    out_specs = (
        P("dp", None),
        P("dp", None),
        P(),
        P(None, "tensor"),
        P(None, "tensor"),
        P(None, "tensor"),
        P("tensor", None),
        P(),
        P(),
        P(None, None, "tensor"),
        P(None, None, "tensor"),
        P(None, "tensor", None),
    )
    return jax.shard_map(
        per_device, mesh=mesh, in_specs=in_specs, out_specs=out_specs, check_vma=False
    )
```

```python
import functools

import jax
import jax.numpy as jnp
from jax import lax
from jax.experimental import pallas as pl
from jax.experimental.pallas import tpu as pltpu
from jax.sharding import PartitionSpec as P

D = 1024
HEAD_DIM = 64
EXPERTS = 4
TOPK = 2
CAP = 640
MOST = 512
ROWS8 = 8

norm_eps = 1e-05
masked_value = -1e30
f32 = jnp.float32
bf16 = jnp.bfloat16
i32 = jnp.int32

NN = (((1,), (0,)), ((), ()))
NT = (((1,), (1,)), ((), ()))
TN = (((0,), (0,)), ((), ()))


def mm(left, right, dims=NN):
    return lax.dot_general(left, right, dims, preferred_element_type=f32)


def full_spec(shape):
    zeros = (0,) * len(shape)
    return pl.BlockSpec(shape, lambda *_: zeros, pipeline_mode=pl.Buffered(1))


def route_kernel(choice_ref, order_ref, slot_ref):
    length = choice_ref.shape[1]
    pairs = 2 * length
    order = order_ref[...]
    where_pair = (order & 1) * length + (order >> 1)
    match = (lax.broadcasted_iota(i32, (pairs, pairs), 0) == where_pair).astype(f32).astype(bf16)
    experts = lax.broadcasted_iota(i32, (ROWS8, length), 0)
    first = (choice_ref[0:1, :] == experts).astype(f32)
    second = (choice_ref[1:2, :] == experts).astype(f32)
    hot = jnp.concatenate([first, second], axis=1)
    ordered = mm(hot.astype(bf16), match)
    step = 512
    tri = (
        lax.broadcasted_iota(i32, (step, step), 0) < lax.broadcasted_iota(i32, (step, step), 1)
    ).astype(f32)
    carry = jnp.zeros((ROWS8, 1), f32)
    ranks = []
    for begin in range(0, pairs, step):
        part = ordered[:, begin : begin + step]
        inside = mm(part.astype(bf16), tri.astype(bf16)) + carry
        ranks.append(jnp.sum(inside * part, axis=0, keepdims=True))
        carry = carry + jnp.sum(part, axis=1, keepdims=True)
    rank = jnp.concatenate(ranks, axis=1)
    high = jnp.floor(rank * (1.0 / 64.0))
    low_part = rank - 64.0 * high
    row_id = lax.broadcasted_iota(i32, (ROWS8, pairs), 0)
    both = jnp.where(row_id == 0, high, jnp.where(row_id == 1, low_part, 0.0))
    back = mm(both.astype(bf16), match, NT)
    slot = (64.0 * back[0:1, :] + back[1:2, :]).astype(i32)
    slot_ref[...] = jnp.where(
        first > 0.5, slot[:, :length], jnp.where(second > 0.5, slot[:, length:], -1)
    )


def route(choice_t, order):
    length = choice_t.shape[1]
    return pl.pallas_call(
        route_kernel,
        out_shape=jax.ShapeDtypeStruct((ROWS8, length), i32),
        compiler_params=pltpu.CompilerParams(vmem_limit_bytes=50 << 20),
        cost_estimate=pl.CostEstimate(flops=1_000_000_000, transcendentals=0, bytes_accessed=1),
        name="route",
    )(choice_t, order)


def attn_blocks(length, rows):
    blocks = []
    for begin in range(0, length, rows):
        start = max(0, begin + rows - MOST - rows)
        start = max(0, (begin + 1 - MOST) // 128 * 128)
        blocks.append((begin, start, begin + rows))
    return blocks


def attn_fwd_kernel(rows, q_ref, k_ref, v_ref, segc_ref, segr_ref, o_ref):
    length = q_ref.shape[0]
    for begin, start, stop in attn_blocks(length, rows):
        wide = stop - start
        row_pos = begin + lax.broadcasted_iota(i32, (rows, wide), 0)
        col_pos = start + lax.broadcasted_iota(i32, (rows, wide), 1)
        allowed = (segc_ref[begin:stop, :] == segr_ref[:, start:stop]) & (col_pos <= row_pos)
        bias = jnp.where(allowed, 0.0, masked_value)
        bias = jnp.concatenate([bias, bias], axis=0)
        for kv in range(2):
            lo = kv * HEAD_DIM
            q_two = jnp.concatenate(
                [
                    q_ref[begin:stop, 2 * lo : 2 * lo + HEAD_DIM],
                    q_ref[begin:stop, 2 * lo + HEAD_DIM : 2 * lo + 2 * HEAD_DIM],
                ],
                axis=0,
            )
            q_two = q_two * jnp.asarray(HEAD_DIM**-0.5, bf16)
            scores = mm(q_two, k_ref[start:stop, lo : lo + HEAD_DIM], NT) + bias
            peak = jnp.max(scores, axis=1, keepdims=True)
            raised = jnp.exp(scores - peak)
            total = jnp.sum(raised, axis=1, keepdims=True)
            probs = (raised * (1.0 / total)).astype(bf16)
            out = mm(probs, v_ref[start:stop, lo : lo + HEAD_DIM])
            out = out.astype(bf16).astype(f32)
            o_ref[begin:stop, 2 * lo : 2 * lo + 2 * HEAD_DIM] = jnp.concatenate(
                [out[:rows], out[rows:]], axis=1
            )


def attn_fwd(qkv, seg_col, seg_row, q_cols, g):
    length = qkv.shape[0]
    pairs = q_cols // 256
    return pl.pallas_call(
        functools.partial(attn_fwd_kernel, 256),
        grid=(1,),
        in_specs=[
            pl.BlockSpec((length, 256), lambda _: (0, g)),
            pl.BlockSpec((length, 128), lambda _: (0, 2 * pairs + g)),
            pl.BlockSpec((length, 128), lambda _: (0, 3 * pairs + g)),
            full_spec((length, 1)),
            full_spec((1, length)),
        ],
        out_specs=pl.BlockSpec((length, 256), lambda _: (0, 0)),
        out_shape=jax.ShapeDtypeStruct((length, 256), f32),
        compiler_params=pltpu.CompilerParams(vmem_limit_bytes=50 << 20),
        cost_estimate=pl.CostEstimate(flops=1_000_000_000, transcendentals=0, bytes_accessed=1),
        name="attn_fwd",
    )(qkv, qkv, qkv, seg_col, seg_row)


def attn_bwd_kernel(
    rows, q_ref, k_ref, v_ref, do_ref, segc_ref, segr_ref, dq_ref, dk_ref, dv_ref, dks, dvs
):
    length = q_ref.shape[0]
    scale = HEAD_DIM**-0.5
    dks[...] = jnp.zeros_like(dks)
    dvs[...] = jnp.zeros_like(dvs)
    for begin, start, stop in attn_blocks(length, rows):
        wide = stop - start
        row_pos = begin + lax.broadcasted_iota(i32, (wide, rows), 1)
        col_pos = start + lax.broadcasted_iota(i32, (wide, rows), 0)
        allowed = (segr_ref[:, begin:stop] == segc_ref[start:stop, :]) & (col_pos <= row_pos)
        bias = jnp.where(allowed, 0.0, masked_value)
        bias = jnp.concatenate([bias, bias], axis=1)
        for kv in range(2):
            lo = kv * HEAD_DIM
            q_two = jnp.concatenate(
                [
                    q_ref[begin:stop, 2 * lo : 2 * lo + HEAD_DIM],
                    q_ref[begin:stop, 2 * lo + HEAD_DIM : 2 * lo + 2 * HEAD_DIM],
                ],
                axis=0,
            )
            q_two = q_two * jnp.asarray(scale, bf16)
            do_two = jnp.concatenate(
                [
                    do_ref[begin:stop, 2 * lo : 2 * lo + HEAD_DIM],
                    do_ref[begin:stop, 2 * lo + HEAD_DIM : 2 * lo + 2 * HEAD_DIM],
                ],
                axis=0,
            )
            k_win = k_ref[start:stop, lo : lo + HEAD_DIM]
            v_win = v_ref[start:stop, lo : lo + HEAD_DIM]
            scores = mm(k_win, q_two, NT) + bias
            peak = jnp.max(scores, axis=0, keepdims=True)
            raised = jnp.exp(scores - peak)
            total = jnp.sum(raised, axis=0, keepdims=True)
            probs = raised * (1.0 / total)
            grad_probs = mm(v_win, do_two, NT)
            row_dot = jnp.sum(probs * grad_probs, axis=0, keepdims=True)
            grad_scores = (probs * (grad_probs - row_dot)).astype(bf16)
            dvs[start:stop, lo : lo + HEAD_DIM] += mm(probs.astype(bf16), do_two)
            dks[start:stop, lo : lo + HEAD_DIM] += mm(grad_scores, q_two)
            dq = (mm(grad_scores, k_win, TN) * scale).astype(bf16)
            dq_ref[begin:stop, 2 * lo : 2 * lo + 2 * HEAD_DIM] = jnp.concatenate(
                [dq[:rows], dq[rows:]], axis=1
            )
    dk_ref[...] = dks[...].astype(bf16)
    dv_ref[...] = dvs[...].astype(bf16)


def attn_bwd(qkv, grad_heads, seg_col, seg_row, q_cols):
    length = qkv.shape[0]
    pairs = q_cols // 256
    return pl.pallas_call(
        functools.partial(attn_bwd_kernel, 256),
        grid=(pairs,),
        in_specs=[
            pl.BlockSpec((length, 256), lambda g: (0, g)),
            pl.BlockSpec((length, 128), lambda g: (0, 2 * pairs + g)),
            pl.BlockSpec((length, 128), lambda g: (0, 3 * pairs + g)),
            pl.BlockSpec((length, 256), lambda g: (0, g)),
            full_spec((length, 1)),
            full_spec((1, length)),
        ],
        out_specs=[
            pl.BlockSpec((length, 256), lambda g: (0, g)),
            pl.BlockSpec((length, 128), lambda g: (0, g)),
            pl.BlockSpec((length, 128), lambda g: (0, g)),
        ],
        out_shape=[
            jax.ShapeDtypeStruct((length, q_cols), bf16),
            jax.ShapeDtypeStruct((length, q_cols // 2), bf16),
            jax.ShapeDtypeStruct((length, q_cols // 2), bf16),
        ],
        scratch_shapes=[pltpu.VMEM((length, 128), f32), pltpu.VMEM((length, 128), f32)],
        compiler_params=pltpu.CompilerParams(vmem_limit_bytes=50 << 20),
        cost_estimate=pl.CostEstimate(flops=24213000000, transcendentals=0, bytes_accessed=1),
        name="attn_bwd",
    )(qkv, qkv, qkv, grad_heads, seg_col, seg_row)


def place_rows(slot_row, length):
    return lax.broadcasted_iota(i32, (CAP, length), 0) == slot_row


def expert_own_kernel(groups, *refs):
    x_ref = refs[0]
    oa = refs[1 : 1 + groups]
    ob = refs[1 + groups : 1 + 2 * groups]
    (
        wo_ref,
        wox_ref,
        g2_ref,
        wr_ref,
        slotr_ref,
        dy_ref,
        wg_ref,
        wu_ref,
        wd_ref,
        h_ref,
        xn_ref,
        gate_ref,
        rows_ref,
        dys_ref,
        hid_ref,
        dg_ref,
        du_ref,
        dwg_ref,
        dwu_ref,
        dwd_ref,
    ) = refs[1 + 2 * groups :]
    e = pl.program_id(0)
    length = x_ref.shape[0]
    chunk = 256

    @pl.when(e == 0)
    def _():
        for c in range(length // chunk):
            rows = slice(c * chunk, (c + 1) * chunk)
            attn = None
            for g in range(groups):
                cols = slice(g * 256, (g + 1) * 256)
                one = mm(oa[g][rows, :].astype(bf16), wo_ref[cols, :])
                two = mm(ob[g][rows, :].astype(bf16), wox_ref[cols, :].astype(bf16))
                attn = one + two if attn is None else attn + one + two
            h1 = x_ref[rows, :].astype(f32) + attn
            h_ref[rows, :] = h1
            inverse = lax.rsqrt(jnp.mean(h1 * h1, axis=1, keepdims=True) + norm_eps)
            xn_ref[rows, :] = (h1 * inverse * g2_ref[...]).astype(bf16)
        logits = mm(wr_ref[...].astype(bf16), xn_ref[...], NT)
        chosen = slotr_ref[...] >= 0
        logits = jnp.where(chosen, logits, masked_value)
        peak = jnp.max(logits, axis=0, keepdims=True)
        raised = jnp.where(chosen, jnp.exp(logits - peak), 0.0)
        gate_ref[...] = raised / jnp.sum(raised, axis=0, keepdims=True)

    mask = place_rows(slotr_ref[pl.ds(e, 1), :], length)
    place = mask.astype(f32).astype(bf16)
    gate = jnp.sum(jnp.where(mask, gate_ref[pl.ds(e, 1), :], 0.0), axis=1, keepdims=True)
    rows_in = mm(place, xn_ref[...]).astype(bf16)
    dy_slot = mm(place, dy_ref[...])
    rows_ref[...] = rows_in
    dys_ref[...] = dy_slot.astype(bf16)
    dy_gated = (gate * dy_slot).astype(bf16)
    g = mm(rows_in, wg_ref[0])
    u = mm(rows_in, wu_ref[0])
    sig = 1.0 / (1.0 + jnp.exp(-g))
    act = g * sig
    hid = (act * u).astype(bf16)
    dhid = mm(dy_gated, wd_ref[0], NT)
    dg = (dhid * u * sig * (1.0 + g * (1.0 - sig))).astype(bf16)
    du = (dhid * act).astype(bf16)
    hid_ref[...] = hid
    dg_ref[...] = dg
    du_ref[...] = du
    dwd = mm(hid, dy_gated, TN)
    wide = dwd_ref.shape[-1]
    for c in range(D // wide):
        dwd_ref[0, c] = dwd[:, c * wide : (c + 1) * wide]
    dwg_ref[0] = mm(rows_in, dg, TN)
    dwu_ref[0] = mm(rows_in, du, TN)


def expert_own(x, mine, theirs, w_out, w_out_other, g2, wr_t, slot_row, dy, w_gate, w_up, w_down):
    length = x.shape[0]
    hid = w_down.shape[1]
    groups = len(mine)
    slots = EXPERTS * CAP
    q_cols = w_out.shape[0]
    return pl.pallas_call(
        functools.partial(expert_own_kernel, groups),
        grid=(EXPERTS,),
        in_specs=[full_spec((length, D))]
        + [full_spec((length, 256))] * (2 * groups)
        + [
            full_spec((q_cols, D)),
            full_spec((q_cols, D)),
            full_spec((1, D)),
            full_spec((ROWS8, D)),
            full_spec((ROWS8, length)),
            full_spec((length, D)),
            pl.BlockSpec((1, D, hid), lambda e: (e, 0, 0)),
            pl.BlockSpec((1, D, hid), lambda e: (e, 0, 0)),
            pl.BlockSpec((1, hid, D), lambda e: (e, 0, 0)),
        ],
        out_specs=[
            full_spec((length, D)),
            full_spec((length, D)),
            full_spec((ROWS8, length)),
            pl.BlockSpec((CAP, D), lambda e: (e, 0)),
            pl.BlockSpec((CAP, D), lambda e: (e, 0)),
            pl.BlockSpec((CAP, hid), lambda e: (e, 0)),
            pl.BlockSpec((CAP, hid), lambda e: (e, 0)),
            pl.BlockSpec((CAP, hid), lambda e: (e, 0)),
            pl.BlockSpec((1, D, hid), lambda e: (e, 0, 0)),
            pl.BlockSpec((1, D, hid), lambda e: (e, 0, 0)),
            pl.BlockSpec((1, D // hid, hid, hid), lambda e: (e, 0, 0, 0)),
        ],
        out_shape=[
            jax.ShapeDtypeStruct((length, D), f32),
            jax.ShapeDtypeStruct((length, D), bf16),
            jax.ShapeDtypeStruct((ROWS8, length), f32),
            jax.ShapeDtypeStruct((slots, D), bf16),
            jax.ShapeDtypeStruct((slots, D), bf16),
            jax.ShapeDtypeStruct((slots, hid), bf16),
            jax.ShapeDtypeStruct((slots, hid), bf16),
            jax.ShapeDtypeStruct((slots, hid), bf16),
            jax.ShapeDtypeStruct((EXPERTS, D, hid), f32),
            jax.ShapeDtypeStruct((EXPERTS, D, hid), f32),
            jax.ShapeDtypeStruct((EXPERTS, D // hid, hid, hid), f32),
        ],
        compiler_params=pltpu.CompilerParams(vmem_limit_bytes=60 << 20),
        cost_estimate=pl.CostEstimate(flops=39202000000, transcendentals=0, bytes_accessed=1),
        name="expert_own",
    )(x, *mine, *theirs, w_out, w_out_other, g2, wr_t, slot_row, dy, w_gate, w_up, w_down)


def expert_all_kernel(
    base,
    count,
    last,
    gate_ref,
    slotr_ref,
    slotc_ref,
    rows_ref,
    dys_ref,
    hid_ref,
    dg_ref,
    du_ref,
    wg_ref,
    wu_ref,
    wd_ref,
    wgx_ref,
    wux_ref,
    wdx_ref,
    *rest,
):
    if last:
        (h_ref, xn_ref, g2_ref, wr_ref, dy_ref, moe_in, dh_in, dgate_in) = rest[:8]
        (out_ref, dh_ref, small_ref, moe_s, dgate_s) = rest[8:]
    else:
        (moe_s, dh_ref, dgate_s) = rest
    step = pl.program_id(0)
    e = step + base
    length = slotr_ref.shape[1]
    chunk = 256

    @pl.when(step == 0)
    def _():
        if last:
            moe_s[...] = moe_in[...]
            dh_ref[...] = dh_in[...]
            dgate_s[...] = dgate_in[...]
        else:
            moe_s[...] = jnp.zeros_like(moe_s)
            dh_ref[...] = jnp.zeros_like(dh_ref)
            dgate_s[...] = jnp.zeros_like(dgate_s)

    mask = place_rows(slotr_ref[pl.ds(e, 1), :], length)
    lane8 = lax.broadcasted_iota(i32, (length, ROWS8), 1)
    slot_col = jnp.sum(jnp.where(lane8 == e, slotc_ref[...], 0), axis=1, keepdims=True)
    place_t = (lax.broadcasted_iota(i32, (length, CAP), 1) == slot_col).astype(f32).astype(bf16)
    gate = jnp.sum(jnp.where(mask, gate_ref[pl.ds(e, 1), :], 0.0), axis=1, keepdims=True)
    rows_in = rows_ref[...]
    dy_slot = dys_ref[...].astype(f32)
    dy_gated = (gate * dy_slot).astype(bf16)
    hid_wide = wgx_ref.shape[1]
    wg = wgx_ref[...].astype(bf16)
    wu = wux_ref[...].astype(bf16)
    wd = jnp.concatenate(
        [wdx_ref[c * hid_wide : (c + 1) * hid_wide, :] for c in range(D // hid_wide)], axis=1
    ).astype(bf16)
    g = mm(rows_in, wg)
    u = mm(rows_in, wu)
    sig = 1.0 / (1.0 + jnp.exp(-g))
    act = g * sig
    hid = (act * u).astype(bf16)
    dhid = mm(dy_gated, wd, NT)
    dg = (dhid * u * sig * (1.0 + g * (1.0 - sig))).astype(bf16)
    du = (dhid * act).astype(bf16)
    y = mm(hid_ref[...], wd_ref[0]) + mm(hid, wd)
    dx = mm(dg_ref[...], wg_ref[0], NT) + mm(du_ref[...], wu_ref[0], NT)
    dx = dx + mm(dg, wg, NT) + mm(du, wu, NT)
    dgate_slot = jnp.sum(dy_slot * y, axis=1, keepdims=True)
    dgate_s[pl.ds(e, 1), :] = jnp.sum(jnp.where(mask, dgate_slot, 0.0), axis=0, keepdims=True)
    moe_s[...] += mm(place_t, (gate * y).astype(bf16))
    dh_ref[...] += mm(place_t, dx.astype(bf16))
    if not last:
        return

    @pl.when(step == count - 1)
    def _():
        gates = gate_ref[...]
        dgates = dgate_s[...]
        dsel = gates * (dgates - jnp.sum(gates * dgates, axis=0, keepdims=True))
        drouter = mm(dsel.astype(bf16), xn_ref[...])
        wr = wr_ref[...].astype(bf16)
        dlog_t = dsel.T.astype(bf16)
        small_ref[...] = jnp.zeros_like(small_ref)
        small_ref[0:EXPERTS, :] = drouter[0:EXPERTS, :]
        gain = jnp.zeros((1, D), f32)
        for c in range(length // chunk):
            rows = slice(c * chunk, (c + 1) * chunk)
            h1 = h_ref[rows, :]
            out_ref[rows, :] = (h1 + moe_s[rows, :]).astype(bf16)
            inverse = lax.rsqrt(jnp.mean(h1 * h1, axis=1, keepdims=True) + norm_eps)
            n2 = h1 * inverse
            dxn = dh_ref[rows, :] + mm(dlog_t[rows, :], wr)
            gain = gain + jnp.sum(dxn * n2, axis=0, keepdims=True)
            scaled = dxn * g2_ref[...]
            mean_term = jnp.mean(scaled * n2, axis=1, keepdims=True)
            dh_ref[rows, :] = dy_ref[rows, :].astype(f32) + inverse * (scaled - n2 * mean_term)
        small_ref[EXPERTS : EXPERTS + 1, :] = gain


def expert_all(base, count, routing, kept, weights, other, tail=None):
    gates, slot_row, slot_col = routing
    w_gate, w_up, w_down = weights
    length = slot_row.shape[1]
    hid = w_down.shape[1]
    last = tail is not None
    slot_block = lambda wide: pl.BlockSpec((CAP, wide), lambda e: (base + e, 0))
    weight_in = pl.BlockSpec((1, D, hid), lambda e: (base + e, 0, 0))
    other_block = lambda at: pl.BlockSpec((D, hid), lambda e: (at + base + e, 0))
    whole = full_spec((length, D))
    in_specs = [
        full_spec((ROWS8, length)),
        full_spec((ROWS8, length)),
        full_spec((length, ROWS8)),
        slot_block(D),
        slot_block(D),
        slot_block(hid),
        slot_block(hid),
        slot_block(hid),
        weight_in,
        weight_in,
        pl.BlockSpec((1, hid, D), lambda e: (base + e, 0, 0)),
        other_block(0),
        other_block(EXPERTS),
        other_block(2 * EXPERTS),
    ]
    acc = jax.ShapeDtypeStruct((length, D), f32)
    rows8 = jax.ShapeDtypeStruct((ROWS8, length), f32)
    if last:
        in_specs += [whole, whole, full_spec((1, D)), full_spec((ROWS8, D)), whole]
        in_specs += [whole, whole, full_spec((ROWS8, length))]
        out_specs = [whole, whole, full_spec((ROWS8, D))]
        out_shape = [
            jax.ShapeDtypeStruct((length, D), bf16),
            acc,
            jax.ShapeDtypeStruct((ROWS8, D), f32),
        ]
        scratch = [pltpu.VMEM((length, D), f32), pltpu.VMEM((ROWS8, length), f32)]
    else:
        out_specs = [whole, whole, full_spec((ROWS8, length))]
        out_shape = [acc, acc, rows8]
        scratch = []
    return pl.pallas_call(
        functools.partial(expert_all_kernel, base, count, last),
        grid=(count,),
        in_specs=in_specs,
        out_specs=out_specs,
        out_shape=out_shape,
        scratch_shapes=scratch,
        compiler_params=pltpu.CompilerParams(vmem_limit_bytes=60 << 20),
        cost_estimate=pl.CostEstimate(flops=24_000_000_000, transcendentals=0, bytes_accessed=1),
        name="expert_all",
    )(gates, slot_row, slot_col, *kept, w_gate, w_up, w_down, other, other, other, *(tail or ()))


def swap_tensor(values):
    size = lax.axis_size("tensor")
    return lax.ppermute(values, "tensor", [(i, i ^ 1) for i in range(size)])


def together(*values):
    return lax.optimization_barrier(values)


def column_blocks(values, wide):
    return [values[..., c : c + wide] for c in range(0, values.shape[-1], wide)]


def start_experts(w_gate, w_up, w_down):
    parts = lax.axis_size("dp")
    at = lax.axis_index("dp")
    hid = w_down.shape[1]
    down = jnp.stack(column_blocks(w_down, hid), axis=1)
    shares = []
    for packed in (w_gate, w_up, down):
        packed = packed.reshape(-1, hid)
        rows = packed.shape[0] // parts
        shares.append(lax.dynamic_slice_in_dim(packed, at * rows, rows, 0))
    return swap_tensor(jnp.stack(shares).astype(f32))


def gather_experts(swapped):
    whole = lax.all_gather(swapped, "dp", axis=1, tiled=True)
    return whole.reshape(-1, whole.shape[-1])


def swap_bit(values, bit):
    size = lax.axis_size("dp")
    return lax.ppermute(values, "dp", [(i, i ^ bit) for i in range(size)])


def side_of(bit):
    return (lax.axis_index("dp") // bit) & 1


def blocks_of(values):
    parts = lax.axis_size("dp")
    return values.reshape(parts // 4, 2, 2, -1, values.shape[-1])


def scatter_start(values, bit):
    side = side_of(bit)
    axis = 2 if bit == 1 else 1
    pick = lambda which: lax.dynamic_index_in_dim(values, which, axis, keepdims=False)
    return pick(side), swap_bit(pick(1 - side), bit)


def scatter_pair(values, bit):
    mine, got = scatter_start(values, bit)
    return mine + got


def scatter_far(values):
    size = values.shape[0]
    me = lax.axis_index("dp") // 4
    piece = lambda c: lax.dynamic_index_in_dim(values, c, 0, keepdims=False)
    return piece(me), [swap_bit(piece(me ^ k), 4 * k) for k in range(size - 1, 0, -1)]


def add_all(mine, parts):
    for part in parts:
        mine = mine + part
    return mine


def gather_join(values, got, bit):
    return jnp.where(
        side_of(bit) == 0, jnp.concatenate([values, got]), jnp.concatenate([got, values])
    )


def sum_small(values):
    bit = 1
    while bit < lax.axis_size("dp"):
        values = values + swap_bit(values, bit)
        bit *= 2
    return values


def start_out(w_out):
    at = lax.axis_index("dp")
    rows = w_out.shape[0] // 4
    place = (at & 1) * 2 + ((at >> 1) & 1)
    return swap_tensor(lax.dynamic_slice_in_dim(w_out, place * rows, rows, 0).astype(f32))


def per_device(
    layer_input,
    segments,
    expert_choice,
    dispatch_order,
    norm_gain_one,
    w_query,
    w_key,
    w_value,
    w_out,
    norm_gain_two,
    w_router,
    w_gate,
    w_up,
    w_down,
    out_grad,
):
    length = layer_input.shape[0]
    q_cols = w_query.shape[1]
    hid = w_down.shape[1]
    flat = lambda grad: grad.reshape(-1, grad.shape[-1])
    seg_row = segments
    seg_col = segments.reshape(length, 1)
    whole = start_out(w_out)
    swapped = start_experts(w_gate, w_up, w_down)

    residual = layer_input.astype(f32)
    inverse_one = lax.rsqrt(jnp.mean(residual * residual, axis=-1, keepdims=True) + norm_eps)
    normed_one = residual * inverse_one
    input_one = (normed_one * norm_gain_one).astype(bf16)
    w_qkv = jnp.concatenate([w_query, w_key, w_value], axis=1)
    qkv = jnp.dot(input_one, w_qkv, preferred_element_type=f32).astype(bf16)

    qkv, whole = together(qkv, whole)
    first = attn_fwd(qkv, seg_col, seg_row, q_cols, 0)
    got = swap_bit(whole, 2)
    first, got, qkv = together(first, got, qkv)
    whole = gather_join(whole, got, 2)
    whole, qkv = together(whole, qkv)
    second = attn_fwd(qkv, seg_col, seg_row, q_cols, 1)
    got = swap_bit(whole, 1)
    first, second, got, swapped = together(first, second, got, swapped)
    mine = [first, second]
    theirs = [swap_tensor(first), swap_tensor(second)]
    other = gather_experts(swapped)
    w_out_other = gather_join(whole, got, 1)
    order, _ = together(dispatch_order, second)
    slot_row = route(expert_choice.T, order)
    slot_col = slot_row.T

    wr_t = jnp.pad(w_router.T.astype(f32), ((0, ROWS8 - EXPERTS), (0, 0)))
    g2 = norm_gain_two[None, :]
    middle, input_two, gates, *kept, grad_gate, grad_up, grad_down = expert_own(
        layer_input, mine, theirs, w_out, w_out_other, g2, wr_t, slot_row, out_grad, w_gate, w_up, w_down
    )
    weights = (w_gate, w_up, w_down)
    routing = (gates, slot_row, slot_col)
    c_gate = scatter_pair(blocks_of(grad_gate), 1)
    c_gate, gates, grad_up, grad_down = together(c_gate, gates, grad_up, grad_down)
    mine_gate, got_gate = scatter_start(c_gate, 2)
    mine_up, got_up = scatter_start(blocks_of(grad_up), 1)
    mine_down, got_down = scatter_start(blocks_of(grad_down), 1)
    split = EXPERTS // 2
    partial = expert_all(0, split, (gates, slot_row, slot_col), kept, weights, other)
    got_gate, got_up, got_down, partial = together(got_gate, got_up, got_down, partial)
    x_gate = mine_gate + got_gate
    c_up = mine_up + got_up
    c_down = mine_down + got_down
    x_gate, c_up, c_down, partial = together(x_gate, c_up, c_down, partial)
    near_gate, far_gate = scatter_far(x_gate)
    mine_up, got_up = scatter_start(c_up, 2)
    tail = (middle, input_two, g2, wr_t, out_grad, *partial)
    block_out, grad_middle, small = expert_all(
        split, EXPERTS - split, routing, kept, weights, other, tail
    )
    grad_attn = grad_middle.astype(bf16)
    grad_heads = jnp.einsum("td,nd->tn", grad_attn, w_out, preferred_element_type=f32).astype(bf16)
    far_gate, got_up, grad_heads, grad_attn = together(far_gate, got_up, grad_heads, grad_attn)
    own_gate = add_all(near_gate, far_gate)
    x_up = mine_up + got_up
    x_up, grad_heads, c_down = together(x_up, grad_heads, c_down)
    near_up, far_up = scatter_far(x_up)
    mine_down, got_down = scatter_start(c_down, 2)
    dq, dk, dv = attn_bwd(qkv, grad_heads, seg_col, seg_row, q_cols)
    far_up, got_down, dq, dk, dv = together(far_up, got_down, dq, dk, dv)
    own_up = add_all(near_up, far_up)
    sum_into = lax.all_gather(jnp.stack([own_gate, own_up]), "dp", axis=1, tiled=True)
    near_down, far_down = scatter_far(mine_down + got_down)

    dqkv = jnp.concatenate([dq, dk, dv], axis=1)
    part = jnp.einsum("tn,dn->td", dqkv, w_qkv, preferred_element_type=f32)
    part_other = swap_tensor(part)
    attended = jnp.concatenate(mine, axis=1).astype(bf16)
    queries = [
        jnp.einsum("td,tn->dn", input_one, one, preferred_element_type=f32)
        for one in column_blocks(dq, hid)
    ]
    grad_key = jnp.einsum("td,tn->dn", input_one, dk, preferred_element_type=f32)
    grad_value = jnp.einsum("td,tn->dn", input_one, dv, preferred_element_type=f32)
    grad_wout = jnp.einsum("tn,td->nd", attended, grad_attn, preferred_element_type=f32)
    chunks = [
        jnp.concatenate(column_blocks(grad_wout, hid), axis=0),
        jnp.concatenate(queries, axis=0),
        jnp.concatenate([grad_key, grad_value], axis=0),
    ]
    owned = [add_all(near_down, far_down)]
    for grad in chunks:
        crossed = scatter_pair(scatter_pair(blocks_of(grad), 1), 2)
        owned.append(add_all(*scatter_far(crossed)))
    parts = lax.axis_size("dp")
    part_other, small, owned = together(part_other, small, owned)
    grad_input_one = part + part_other
    grad_gain_one = jnp.sum(grad_input_one * normed_one, axis=0)
    small = sum_small(jnp.concatenate([small[: EXPERTS + 1], grad_gain_one[None, :]], axis=0))
    rest = lax.all_gather(jnp.concatenate(owned, axis=0), "dp", axis=0, tiled=False)
    pieces = []
    at = 0
    for one in owned:
        rows = one.shape[0]
        pieces.append(rest[:, at : at + rows].reshape(parts * rows, hid))
        at += rows
    sum_down = pieces[0].reshape(EXPERTS, D // hid, hid, hid)
    sum_down = jnp.concatenate([sum_down[:, c] for c in range(D // hid)], axis=-1)
    unblock = lambda rows, height: jnp.concatenate(
        [rows[at : at + height] for at in range(0, rows.shape[0], height)], axis=1
    )
    sum_out = unblock(pieces[1], q_cols)
    sum_query = unblock(pieces[2], D)
    scaled = grad_input_one * norm_gain_one
    mean_term = jnp.mean(scaled * normed_one, axis=-1, keepdims=True)
    grad_input = grad_middle + inverse_one * (scaled - normed_one * mean_term)
    return (
        block_out,
        grad_input,
        small[EXPERTS + 1],
        sum_query,
        pieces[3][:D],
        pieces[3][D:],
        sum_out,
        small[EXPERTS],
        small[:EXPERTS].T,
        sum_into[0].reshape(w_gate.shape),
        sum_into[1].reshape(w_up.shape),
        sum_down,
    )


def solution(mesh):
    in_specs = (
        P("dp", None),
        P("dp", None),
        P("dp", None),
        P("dp", None),
        P(),
        P(None, "tensor"),
        P(None, "tensor"),
        P(None, "tensor"),
        P("tensor", None),
        P(),
        P(),
        P(None, None, "tensor"),
        P(None, None, "tensor"),
        P(None, "tensor", None),
        P("dp", None),
    )
    out_specs = (
        P("dp", None),
        P("dp", None),
        P(),
        P(None, "tensor"),
        P(None, "tensor"),
        P(None, "tensor"),
        P("tensor", None),
        P(),
        P(),
        P(None, None, "tensor"),
        P(None, None, "tensor"),
        P(None, "tensor", None),
    )
    return jax.shard_map(
        per_device, mesh=mesh, in_specs=in_specs, out_specs=out_specs, check_vma=False
    )
```

```python
import functools

import jax
import jax.numpy as jnp
from jax import lax
from jax.experimental import pallas as pl
from jax.experimental.pallas import tpu as pltpu
from jax.sharding import PartitionSpec as P

D = 1024
HEAD_DIM = 64
EXPERTS = 4
TOPK = 2
CAP = 640
MOST = 512
ROWS8 = 8

norm_eps = 1e-05
masked_value = -1e30
f32 = jnp.float32
bf16 = jnp.bfloat16
i32 = jnp.int32

NN = (((1,), (0,)), ((), ()))
NT = (((1,), (1,)), ((), ()))
TN = (((0,), (0,)), ((), ()))


def mm(left, right, dims=NN):
    return lax.dot_general(left, right, dims, preferred_element_type=f32)


def full_spec(shape):
    zeros = (0,) * len(shape)
    return pl.BlockSpec(shape, lambda *_: zeros, pipeline_mode=pl.Buffered(1))


def route_kernel(choice_ref, order_ref, slot_ref):
    length = choice_ref.shape[1]
    pairs = 2 * length
    order = order_ref[...]
    where_pair = (order & 1) * length + (order >> 1)
    match = (lax.broadcasted_iota(i32, (pairs, pairs), 0) == where_pair).astype(f32).astype(bf16)
    experts = lax.broadcasted_iota(i32, (ROWS8, length), 0)
    first = (choice_ref[0:1, :] == experts).astype(f32)
    second = (choice_ref[1:2, :] == experts).astype(f32)
    hot = jnp.concatenate([first, second], axis=1)
    ordered = mm(hot.astype(bf16), match)
    step = 512
    tri = (
        lax.broadcasted_iota(i32, (step, step), 0) < lax.broadcasted_iota(i32, (step, step), 1)
    ).astype(f32)
    carry = jnp.zeros((ROWS8, 1), f32)
    ranks = []
    for begin in range(0, pairs, step):
        part = ordered[:, begin : begin + step]
        inside = mm(part.astype(bf16), tri.astype(bf16)) + carry
        ranks.append(jnp.sum(inside * part, axis=0, keepdims=True))
        carry = carry + jnp.sum(part, axis=1, keepdims=True)
    rank = jnp.concatenate(ranks, axis=1)
    high = jnp.floor(rank * (1.0 / 64.0))
    low_part = rank - 64.0 * high
    row_id = lax.broadcasted_iota(i32, (ROWS8, pairs), 0)
    both = jnp.where(row_id == 0, high, jnp.where(row_id == 1, low_part, 0.0))
    back = mm(both.astype(bf16), match, NT)
    slot = (64.0 * back[0:1, :] + back[1:2, :]).astype(i32)
    slot_ref[...] = jnp.where(
        first > 0.5, slot[:, :length], jnp.where(second > 0.5, slot[:, length:], -1)
    )


def route(choice_t, order):
    length = choice_t.shape[1]
    return pl.pallas_call(
        route_kernel,
        out_shape=jax.ShapeDtypeStruct((ROWS8, length), i32),
        compiler_params=pltpu.CompilerParams(vmem_limit_bytes=50 << 20),
        cost_estimate=pl.CostEstimate(flops=1_000_000_000, transcendentals=0, bytes_accessed=1),
        name="route",
    )(choice_t, order)


def project_kernel(x_ref, g_ref, wq_ref, wk_ref, wv_ref, xn_ref, qkv_ref):
    x = x_ref[...].astype(f32)
    inverse = lax.rsqrt(jnp.mean(x * x, axis=1, keepdims=True) + norm_eps)
    xn = (x * inverse * g_ref[...]).astype(bf16)
    xn_ref[...] = xn
    at = 0
    for w_ref in (wq_ref, wk_ref, wv_ref):
        wide = w_ref.shape[1]
        qkv_ref[:, at : at + wide] = mm(xn, w_ref[...]).astype(bf16)
        at += wide


def project(x, gain, w_query, w_key, w_value):
    length = x.shape[0]
    q_cols = w_query.shape[1]
    kv_cols = w_key.shape[1]
    wide = q_cols + 2 * kv_cols
    rows = 256
    return pl.pallas_call(
        project_kernel,
        grid=(length // rows,),
        in_specs=[
            pl.BlockSpec((rows, D), lambda i: (i, 0)),
            full_spec((1, D)),
            full_spec((D, q_cols)),
            full_spec((D, kv_cols)),
            full_spec((D, kv_cols)),
        ],
        out_specs=[
            pl.BlockSpec((rows, D), lambda i: (i, 0)),
            pl.BlockSpec((rows, wide), lambda i: (i, 0)),
        ],
        out_shape=[
            jax.ShapeDtypeStruct((length, D), bf16),
            jax.ShapeDtypeStruct((length, wide), bf16),
        ],
        cost_estimate=pl.CostEstimate(flops=1_000_000_000, transcendentals=0, bytes_accessed=1),
        name="project",
    )(x, gain, w_query, w_key, w_value)


def attn_blocks(length, rows):
    blocks = []
    for begin in range(0, length, rows):
        start = max(0, begin + rows - MOST - rows)
        start = max(0, (begin + 1 - MOST) // 128 * 128)
        blocks.append((begin, start, begin + rows))
    return blocks


def attn_fwd_kernel(rows, q_ref, k_ref, v_ref, segc_ref, segr_ref, o_ref):
    length = q_ref.shape[0]
    for begin, start, stop in attn_blocks(length, rows):
        wide = stop - start
        row_pos = begin + lax.broadcasted_iota(i32, (rows, wide), 0)
        col_pos = start + lax.broadcasted_iota(i32, (rows, wide), 1)
        allowed = (segc_ref[begin:stop, :] == segr_ref[:, start:stop]) & (col_pos <= row_pos)
        bias = jnp.where(allowed, 0.0, masked_value)
        bias = jnp.concatenate([bias, bias], axis=0)
        for kv in range(2):
            lo = kv * HEAD_DIM
            q_two = jnp.concatenate(
                [
                    q_ref[begin:stop, 2 * lo : 2 * lo + HEAD_DIM],
                    q_ref[begin:stop, 2 * lo + HEAD_DIM : 2 * lo + 2 * HEAD_DIM],
                ],
                axis=0,
            )
            q_two = q_two * jnp.asarray(HEAD_DIM**-0.5, bf16)
            scores = mm(q_two, k_ref[start:stop, lo : lo + HEAD_DIM], NT) + bias
            peak = jnp.max(scores, axis=1, keepdims=True)
            raised = jnp.exp(scores - peak)
            total = jnp.sum(raised, axis=1, keepdims=True)
            probs = (raised * (1.0 / total)).astype(bf16)
            out = mm(probs, v_ref[start:stop, lo : lo + HEAD_DIM])
            out = out.astype(bf16).astype(f32)
            o_ref[begin:stop, 2 * lo : 2 * lo + 2 * HEAD_DIM] = jnp.concatenate(
                [out[:rows], out[rows:]], axis=1
            )


def attn_fwd(qkv, seg_col, seg_row, q_cols, g):
    length = qkv.shape[0]
    pairs = q_cols // 256
    return pl.pallas_call(
        functools.partial(attn_fwd_kernel, 256),
        grid=(1,),
        in_specs=[
            pl.BlockSpec((length, 256), lambda _: (0, g)),
            pl.BlockSpec((length, 128), lambda _: (0, 2 * pairs + g)),
            pl.BlockSpec((length, 128), lambda _: (0, 3 * pairs + g)),
            full_spec((length, 1)),
            full_spec((1, length)),
        ],
        out_specs=pl.BlockSpec((length, 256), lambda _: (0, 0)),
        out_shape=jax.ShapeDtypeStruct((length, 256), f32),
        compiler_params=pltpu.CompilerParams(vmem_limit_bytes=50 << 20),
        cost_estimate=pl.CostEstimate(flops=1_000_000_000, transcendentals=0, bytes_accessed=1),
        name="attn_fwd",
    )(qkv, qkv, qkv, seg_col, seg_row)


def attn_bwd_kernel(
    rows, q_ref, k_ref, v_ref, do_ref, segc_ref, segr_ref, dq_ref, dk_ref, dv_ref, dks, dvs
):
    length = q_ref.shape[0]
    scale = HEAD_DIM**-0.5
    dks[...] = jnp.zeros_like(dks)
    dvs[...] = jnp.zeros_like(dvs)
    for begin, start, stop in attn_blocks(length, rows):
        wide = stop - start
        row_pos = begin + lax.broadcasted_iota(i32, (wide, rows), 1)
        col_pos = start + lax.broadcasted_iota(i32, (wide, rows), 0)
        allowed = (segr_ref[:, begin:stop] == segc_ref[start:stop, :]) & (col_pos <= row_pos)
        bias = jnp.where(allowed, 0.0, masked_value)
        bias = jnp.concatenate([bias, bias], axis=1)
        for kv in range(2):
            lo = kv * HEAD_DIM
            q_two = jnp.concatenate(
                [
                    q_ref[begin:stop, 2 * lo : 2 * lo + HEAD_DIM],
                    q_ref[begin:stop, 2 * lo + HEAD_DIM : 2 * lo + 2 * HEAD_DIM],
                ],
                axis=0,
            )
            q_two = q_two * jnp.asarray(scale, bf16)
            do_two = jnp.concatenate(
                [
                    do_ref[begin:stop, 2 * lo : 2 * lo + HEAD_DIM],
                    do_ref[begin:stop, 2 * lo + HEAD_DIM : 2 * lo + 2 * HEAD_DIM],
                ],
                axis=0,
            )
            k_win = k_ref[start:stop, lo : lo + HEAD_DIM]
            v_win = v_ref[start:stop, lo : lo + HEAD_DIM]
            scores = mm(k_win, q_two, NT) + bias
            peak = jnp.max(scores, axis=0, keepdims=True)
            raised = jnp.exp(scores - peak)
            total = jnp.sum(raised, axis=0, keepdims=True)
            probs = raised * (1.0 / total)
            grad_probs = mm(v_win, do_two, NT)
            row_dot = jnp.sum(probs * grad_probs, axis=0, keepdims=True)
            grad_scores = (probs * (grad_probs - row_dot)).astype(bf16)
            dvs[start:stop, lo : lo + HEAD_DIM] += mm(probs.astype(bf16), do_two)
            dks[start:stop, lo : lo + HEAD_DIM] += mm(grad_scores, q_two)
            dq = (mm(grad_scores, k_win, TN) * scale).astype(bf16)
            dq_ref[begin:stop, 2 * lo : 2 * lo + 2 * HEAD_DIM] = jnp.concatenate(
                [dq[:rows], dq[rows:]], axis=1
            )
    dk_ref[...] = dks[...].astype(bf16)
    dv_ref[...] = dvs[...].astype(bf16)


def attn_bwd(qkv, grad_heads, seg_col, seg_row, q_cols):
    length = qkv.shape[0]
    pairs = q_cols // 256
    return pl.pallas_call(
        functools.partial(attn_bwd_kernel, 256),
        grid=(pairs,),
        in_specs=[
            pl.BlockSpec((length, 256), lambda g: (0, g)),
            pl.BlockSpec((length, 128), lambda g: (0, 2 * pairs + g)),
            pl.BlockSpec((length, 128), lambda g: (0, 3 * pairs + g)),
            pl.BlockSpec((length, 256), lambda g: (0, g)),
            full_spec((length, 1)),
            full_spec((1, length)),
        ],
        out_specs=[
            pl.BlockSpec((length, 256), lambda g: (0, g)),
            pl.BlockSpec((length, 128), lambda g: (0, g)),
            pl.BlockSpec((length, 128), lambda g: (0, g)),
        ],
        out_shape=[
            jax.ShapeDtypeStruct((length, q_cols), bf16),
            jax.ShapeDtypeStruct((length, q_cols // 2), bf16),
            jax.ShapeDtypeStruct((length, q_cols // 2), bf16),
        ],
        scratch_shapes=[pltpu.VMEM((length, 128), f32), pltpu.VMEM((length, 128), f32)],
        compiler_params=pltpu.CompilerParams(vmem_limit_bytes=50 << 20),
        cost_estimate=pl.CostEstimate(flops=24213000000, transcendentals=0, bytes_accessed=1),
        name="attn_bwd",
    )(qkv, qkv, qkv, grad_heads, seg_col, seg_row)


def attn_grads_kernel(
    side_ref, xn_ref, dq_ref, dk_ref, dv_ref, wq_ref, wk_ref, wv_ref, part_ref, mine_ref, send_ref, keep
):
    xn = xn_ref[...]
    wide = dk_ref.shape[1]
    side = side_ref[0, 0]
    queries = [mm(xn, dq_ref[:, c : c + wide], TN) for c in range(0, dq_ref.shape[1], wide)]
    hand_out(jnp.concatenate(queries, axis=0), keep, side, mine_ref, send_ref, 0)
    values = [mm(xn, dk_ref[...], TN), mm(xn, dv_ref[...], TN)]
    hand_out(jnp.concatenate(values, axis=0), keep, side, mine_ref, send_ref, 1)
    part = mm(dq_ref[...], wq_ref[...], NT) + mm(dk_ref[...], wk_ref[...], NT)
    part_ref[...] = part + mm(dv_ref[...], wv_ref[...], NT)


def attn_grads(side, xn, dq, dk, dv, w_query, w_key, w_value):
    length = xn.shape[0]
    wide = dk.shape[1]
    parts = lax.axis_size("dp")
    rows = 2 * dq.shape[1] // wide * D // parts
    shape = jax.ShapeDtypeStruct((parts // 4, 2, rows, wide), f32)
    arrays = (xn, dq, dk, dv, w_query, w_key, w_value)
    return pl.pallas_call(
        attn_grads_kernel,
        grid=(1,),
        in_specs=[pl.BlockSpec(memory_space=pltpu.SMEM)] + [full_spec(one.shape) for one in arrays],
        out_specs=[full_spec((length, D)), full_spec(shape.shape), full_spec(shape.shape)],
        out_shape=[jax.ShapeDtypeStruct((length, D), f32), shape, shape],
        scratch_shapes=[pltpu.VMEM((dq.shape[1] // wide * D, wide), f32)],
        compiler_params=pltpu.CompilerParams(vmem_limit_bytes=50 << 20),
        cost_estimate=pl.CostEstimate(flops=1, transcendentals=0, bytes_accessed=1),
        name="attn_grads",
    )(side, *arrays)


def place_rows(slot_row, length):
    return lax.broadcasted_iota(i32, (CAP, length), 0) == slot_row


def expert_pre_kernel(groups, *refs):
    x_ref = refs[0]
    oa = refs[1 : 1 + groups]
    wo_ref, slotr_ref, dy_ref, h_ref, dys_ref = refs[1 + groups :]
    e = pl.program_id(0)
    length = x_ref.shape[0]
    step = length // EXPERTS
    rows = pl.ds(pl.multiple_of(e * step, step), step)
    total = x_ref[rows, :].astype(f32)
    for g in range(groups):
        total = total + mm(oa[g][rows, :].astype(bf16), wo_ref[g * 256 : (g + 1) * 256, :])
    h_ref[...] = total
    place = place_rows(slotr_ref[pl.ds(e, 1), :], length).astype(f32).astype(bf16)
    dys_ref[...] = mm(place, dy_ref[...]).astype(bf16)


def expert_pre(x, mine, w_out, slot_row, dy):
    length = x.shape[0]
    groups = len(mine)
    return pl.pallas_call(
        functools.partial(expert_pre_kernel, groups),
        grid=(EXPERTS,),
        in_specs=[full_spec((length, D))]
        + [full_spec((length, 256))] * groups
        + [full_spec(w_out.shape), full_spec((ROWS8, length)), full_spec((length, D))],
        out_specs=[
            pl.BlockSpec((length // EXPERTS, D), lambda e: (e, 0)),
            pl.BlockSpec((CAP, D), lambda e: (e, 0)),
        ],
        out_shape=[
            jax.ShapeDtypeStruct((length, D), f32),
            jax.ShapeDtypeStruct((EXPERTS * CAP, D), bf16),
        ],
        compiler_params=pltpu.CompilerParams(vmem_limit_bytes=50 << 20),
        cost_estimate=pl.CostEstimate(flops=1_000_000_000, transcendentals=0, bytes_accessed=1),
        name="expert_pre",
    )(x, *mine, w_out, slot_row, dy)


def hand_out(value, keep, side, mine_ref, send_ref, place=0):
    keep[...] = value
    far = mine_ref.shape[0]
    rows = value.shape[0] // (4 * far)
    to = slice(place * rows, (place + 1) * rows)
    for z in range(far):
        for x in range(2):
            at = 4 * z + 2 * x
            mine_ref[z, x, to] = keep[pl.ds(pl.multiple_of((at + side) * rows, rows), rows), :]
            send_ref[z, x, to] = keep[pl.ds(pl.multiple_of((at + 1 - side) * rows, rows), rows), :]


def expert_own_kernel(groups, side_ref, *refs):
    part_ref = refs[0]
    ob = refs[1 : 1 + groups]
    (
        wox_ref,
        g2_ref,
        wr_ref,
        slotr_ref,
        dys_ref,
        wg_ref,
        wu_ref,
        wd_ref,
        h_ref,
        xn_ref,
        gate_ref,
        rows_ref,
        hid_ref,
        dg_ref,
        du_ref,
        mine_up,
        send_up,
        mine_two,
        send_two,
        keep,
    ) = refs[1 + groups :]
    side = side_ref[0, 0]
    e = pl.program_id(0)
    length = part_ref.shape[0]
    chunk = 256

    @pl.when(e == 0)
    def _():
        for c in range(length // chunk):
            rows = slice(c * chunk, (c + 1) * chunk)
            h1 = part_ref[rows, :]
            for g in range(groups):
                cols = slice(g * 256, (g + 1) * 256)
                h1 = h1 + mm(ob[g][rows, :].astype(bf16), wox_ref[cols, :].astype(bf16))
            h_ref[rows, :] = h1
            inverse = lax.rsqrt(jnp.mean(h1 * h1, axis=1, keepdims=True) + norm_eps)
            xn_ref[rows, :] = (h1 * inverse * g2_ref[...]).astype(bf16)
        logits = mm(wr_ref[...].astype(bf16), xn_ref[...], NT)
        chosen = slotr_ref[...] >= 0
        logits = jnp.where(chosen, logits, masked_value)
        peak = jnp.max(logits, axis=0, keepdims=True)
        raised = jnp.where(chosen, jnp.exp(logits - peak), 0.0)
        gate_ref[...] = raised / jnp.sum(raised, axis=0, keepdims=True)

    mask = place_rows(slotr_ref[pl.ds(e, 1), :], length)
    place = mask.astype(f32).astype(bf16)
    gate = jnp.sum(jnp.where(mask, gate_ref[pl.ds(e, 1), :], 0.0), axis=1, keepdims=True)
    rows_in = mm(place, xn_ref[...]).astype(bf16)
    rows_ref[...] = rows_in
    dy_gated = (gate * dys_ref[...].astype(f32)).astype(bf16)
    g = mm(rows_in, wg_ref[0])
    u = mm(rows_in, wu_ref[0])
    sig = 1.0 / (1.0 + jnp.exp(-g))
    act = g * sig
    hid = (act * u).astype(bf16)
    dhid = mm(dy_gated, wd_ref[0], NT)
    dg = (dhid * u * sig * (1.0 + g * (1.0 - sig))).astype(bf16)
    du = (dhid * act).astype(bf16)
    hid_ref[...] = hid
    dg_ref[...] = dg
    du_ref[...] = du
    hand_out(mm(rows_in, du, TN), keep, side, mine_up, send_up)
    hand_out(mm(rows_in, dg, TN), keep, side, mine_two, send_two)
    dwd = mm(hid, dy_gated, TN)
    wide = hid.shape[1]
    blocks = [dwd[:, c : c + wide] for c in range(0, D, wide)]
    hand_out(jnp.concatenate(blocks, axis=0), keep, side, mine_two, send_two, 1)


def piece_specs(hid, arrays):
    parts = lax.axis_size("dp")
    far = parts // 4
    rows = arrays * EXPERTS * D // parts
    spec = pl.BlockSpec((far // EXPERTS, 2, rows, hid), lambda e: (e, 0, 0, 0))
    return spec, jax.ShapeDtypeStruct((far, 2, rows, hid), f32)


def expert_own(side, part, theirs, w_out_other, g2, wr_t, slot_row, dys, w_gate, w_up, w_down):
    length = part.shape[0]
    hid = w_down.shape[1]
    groups = len(theirs)
    slots = EXPERTS * CAP
    q_cols = w_out_other.shape[0]
    piece, shape = piece_specs(hid, 1)
    piece_two, shape_two = piece_specs(hid, 2)
    return pl.pallas_call(
        functools.partial(expert_own_kernel, groups),
        grid=(EXPERTS,),
        in_specs=[pl.BlockSpec(memory_space=pltpu.SMEM), full_spec((length, D))]
        + [full_spec((length, 256))] * groups
        + [
            full_spec((q_cols, D)),
            full_spec((1, D)),
            full_spec((ROWS8, D)),
            full_spec((ROWS8, length)),
            pl.BlockSpec((CAP, D), lambda e: (e, 0)),
            pl.BlockSpec((1, D, hid), lambda e: (e, 0, 0)),
            pl.BlockSpec((1, D, hid), lambda e: (e, 0, 0)),
            pl.BlockSpec((1, hid, D), lambda e: (e, 0, 0)),
        ],
        out_specs=[
            full_spec((length, D)),
            full_spec((length, D)),
            full_spec((ROWS8, length)),
            pl.BlockSpec((CAP, D), lambda e: (e, 0)),
            pl.BlockSpec((CAP, hid), lambda e: (e, 0)),
            pl.BlockSpec((CAP, hid), lambda e: (e, 0)),
            pl.BlockSpec((CAP, hid), lambda e: (e, 0)),
            piece,
            piece,
            piece_two,
            piece_two,
        ],
        out_shape=[
            jax.ShapeDtypeStruct((length, D), f32),
            jax.ShapeDtypeStruct((length, D), bf16),
            jax.ShapeDtypeStruct((ROWS8, length), f32),
            jax.ShapeDtypeStruct((slots, D), bf16),
            jax.ShapeDtypeStruct((slots, hid), bf16),
            jax.ShapeDtypeStruct((slots, hid), bf16),
            jax.ShapeDtypeStruct((slots, hid), bf16),
            shape,
            shape,
            shape_two,
            shape_two,
        ],
        scratch_shapes=[pltpu.VMEM((D, hid), f32)],
        compiler_params=pltpu.CompilerParams(vmem_limit_bytes=60 << 20),
        cost_estimate=pl.CostEstimate(flops=39202000000, transcendentals=0, bytes_accessed=1),
        name="expert_own",
    )(side, part, *theirs, w_out_other, g2, wr_t, slot_row, dys, w_gate, w_up, w_down)


def expert_all_kernel(
    gate_ref,
    slotr_ref,
    slotc_ref,
    rows_ref,
    dys_ref,
    hid_ref,
    dg_ref,
    du_ref,
    wg_ref,
    wu_ref,
    wd_ref,
    wgx_ref,
    wux_ref,
    wdx_ref,
    *rest,
):
    (h_ref, xn_ref, g2_ref, wr_ref, dy_ref) = rest[:5]
    (out_ref, dh_ref, da_ref, small_ref, moe_s, dgate_s) = rest[5:]
    e = pl.program_id(0)
    length = slotr_ref.shape[1]
    chunk = 256

    @pl.when(e == 0)
    def _():
        moe_s[...] = jnp.zeros_like(moe_s)
        dh_ref[...] = jnp.zeros_like(dh_ref)
        dgate_s[...] = jnp.zeros_like(dgate_s)

    mask = place_rows(slotr_ref[pl.ds(e, 1), :], length)
    lane8 = lax.broadcasted_iota(i32, (length, ROWS8), 1)
    slot_col = jnp.sum(jnp.where(lane8 == e, slotc_ref[...], 0), axis=1, keepdims=True)
    place_t = (lax.broadcasted_iota(i32, (length, CAP), 1) == slot_col).astype(f32).astype(bf16)
    gate = jnp.sum(jnp.where(mask, gate_ref[pl.ds(e, 1), :], 0.0), axis=1, keepdims=True)
    rows_in = rows_ref[...]
    dy_slot = dys_ref[...].astype(f32)
    dy_gated = (gate * dy_slot).astype(bf16)
    hid_wide = wgx_ref.shape[1]
    wg = wgx_ref[...].astype(bf16)
    wu = wux_ref[...].astype(bf16)
    wd = jnp.concatenate(
        [wdx_ref[c * hid_wide : (c + 1) * hid_wide, :] for c in range(D // hid_wide)], axis=1
    ).astype(bf16)
    g = mm(rows_in, wg)
    u = mm(rows_in, wu)
    sig = 1.0 / (1.0 + jnp.exp(-g))
    act = g * sig
    hid = (act * u).astype(bf16)
    dhid = mm(dy_gated, wd, NT)
    dg = (dhid * u * sig * (1.0 + g * (1.0 - sig))).astype(bf16)
    du = (dhid * act).astype(bf16)
    y = mm(hid_ref[...], wd_ref[0]) + mm(hid, wd)
    dx = mm(dg_ref[...], wg_ref[0], NT) + mm(du_ref[...], wu_ref[0], NT)
    dx = dx + mm(dg, wg, NT) + mm(du, wu, NT)
    dgate_slot = jnp.sum(dy_slot * y, axis=1, keepdims=True)
    dgate_s[pl.ds(e, 1), :] = jnp.sum(jnp.where(mask, dgate_slot, 0.0), axis=0, keepdims=True)
    moe_s[...] += mm(place_t, (gate * y).astype(bf16))
    dh_ref[...] += mm(place_t, dx.astype(bf16))

    @pl.when(e == EXPERTS - 1)
    def _():
        gates = gate_ref[...]
        dgates = dgate_s[...]
        dsel = gates * (dgates - jnp.sum(gates * dgates, axis=0, keepdims=True))
        drouter = mm(dsel.astype(bf16), xn_ref[...])
        wr = wr_ref[...].astype(bf16)
        dlog_t = dsel.T.astype(bf16)
        small_ref[...] = jnp.zeros_like(small_ref)
        small_ref[0:EXPERTS, :] = drouter[0:EXPERTS, :]
        gain = jnp.zeros((1, D), f32)
        for c in range(length // chunk):
            rows = slice(c * chunk, (c + 1) * chunk)
            h1 = h_ref[rows, :]
            out_ref[rows, :] = (h1 + moe_s[rows, :]).astype(bf16)
            inverse = lax.rsqrt(jnp.mean(h1 * h1, axis=1, keepdims=True) + norm_eps)
            n2 = h1 * inverse
            dxn = dh_ref[rows, :] + mm(dlog_t[rows, :], wr)
            gain = gain + jnp.sum(dxn * n2, axis=0, keepdims=True)
            scaled = dxn * g2_ref[...]
            mean_term = jnp.mean(scaled * n2, axis=1, keepdims=True)
            dh1 = dy_ref[rows, :].astype(f32) + inverse * (scaled - n2 * mean_term)
            dh_ref[rows, :] = dh1
            da_ref[rows, :] = dh1.astype(bf16)
        small_ref[EXPERTS : EXPERTS + 1, :] = gain


def expert_all(routing, kept, weights, other, tail):
    gates, slot_row, slot_col = routing
    w_gate, w_up, w_down = weights
    length = slot_row.shape[1]
    hid = w_down.shape[1]
    slot_block = lambda wide: pl.BlockSpec((CAP, wide), lambda e: (e, 0))
    weight_in = pl.BlockSpec((1, D, hid), lambda e: (e, 0, 0))
    other_block = lambda at: pl.BlockSpec((D, hid), lambda e: (at + e, 0))
    whole = full_spec((length, D))
    in_specs = [
        full_spec((ROWS8, length)),
        full_spec((ROWS8, length)),
        full_spec((length, ROWS8)),
        slot_block(D),
        slot_block(D),
        slot_block(hid),
        slot_block(hid),
        slot_block(hid),
        weight_in,
        weight_in,
        pl.BlockSpec((1, hid, D), lambda e: (e, 0, 0)),
        other_block(0),
        other_block(EXPERTS),
        other_block(2 * EXPERTS),
    ]
    in_specs += [whole, whole, full_spec((1, D)), full_spec((ROWS8, D)), whole]
    return pl.pallas_call(
        expert_all_kernel,
        grid=(EXPERTS,),
        in_specs=in_specs,
        out_specs=[whole, whole, whole, full_spec((ROWS8, D))],
        out_shape=[
            jax.ShapeDtypeStruct((length, D), bf16),
            jax.ShapeDtypeStruct((length, D), f32),
            jax.ShapeDtypeStruct((length, D), bf16),
            jax.ShapeDtypeStruct((ROWS8, D), f32),
        ],
        scratch_shapes=[pltpu.VMEM((length, D), f32), pltpu.VMEM((ROWS8, length), f32)],
        compiler_params=pltpu.CompilerParams(vmem_limit_bytes=60 << 20),
        cost_estimate=pl.CostEstimate(flops=24_000_000_000, transcendentals=0, bytes_accessed=1),
        name="expert_all",
    )(gates, slot_row, slot_col, *kept, w_gate, w_up, w_down, other, other, other, *tail)


def swap_tensor(values):
    size = lax.axis_size("tensor")
    return lax.ppermute(values, "tensor", [(i, i ^ 1) for i in range(size)])


def together(*values):
    return lax.optimization_barrier(values)


def column_blocks(values, wide):
    return [values[..., c : c + wide] for c in range(0, values.shape[-1], wide)]


def start_experts(w_gate, w_up, w_down):
    parts = lax.axis_size("dp")
    at = lax.axis_index("dp")
    hid = w_down.shape[1]
    down = jnp.stack(column_blocks(w_down, hid), axis=1)
    shares = []
    for packed in (w_gate, w_up, down):
        packed = packed.reshape(-1, hid)
        rows = packed.shape[0] // parts
        shares.append(lax.dynamic_slice_in_dim(packed, at * rows, rows, 0))
    return swap_tensor(jnp.stack(shares).astype(f32))


def gather_experts(swapped):
    whole = lax.all_gather(swapped, "dp", axis=1, tiled=True)
    return whole.reshape(-1, whole.shape[-1])


def swap_bit(values, bit):
    size = lax.axis_size("dp")
    return lax.ppermute(values, "dp", [(i, i ^ bit) for i in range(size)])


def side_of(bit):
    return (lax.axis_index("dp") // bit) & 1


def blocks_of(values):
    parts = lax.axis_size("dp")
    return values.reshape(parts // 4, 2, 2, -1, values.shape[-1])


def picked(terms, which, axis):
    total = None
    for term in terms:
        part = lax.dynamic_index_in_dim(term, which, axis, keepdims=False)
        total = part if total is None else total + part
    return total


def core_terms(values):
    side = side_of(1)
    return picked([values], side, 2), [(picked([values], 1 - side, 2), 1)]


def x_terms(terms):
    side = side_of(2)
    axis = terms[0].ndim - 3
    return picked(terms, side, axis), [(picked(terms, 1 - side, axis), 2)]


def far_terms(terms):
    size = terms[0].shape[0]
    me = lax.axis_index("dp") // 4
    sends = [(picked(terms, me ^ k, 0), 4 * k) for k in range(size - 1, 0, -1)]
    return picked(terms, me, 0), sends


def send_all(keep, sends):
    return [keep] + [swap_bit(values, bit) for values, bit in sends]


def prepare(staged, *others):
    bits = [[bit for _, bit in sends] for _, sends in staged]
    values = [(keep, [value for value, _ in sends]) for keep, sends in staged]
    values, *others = together(values, *others)
    staged = [(keep, list(zip(sends, bit))) for (keep, sends), bit in zip(values, bits)]
    return [staged, *others]


def total_of(terms):
    return sum(terms[1:], terms[0])


def gather_join(values, got, bit):
    return jnp.where(
        side_of(bit) == 0, jnp.concatenate([values, got]), jnp.concatenate([got, values])
    )


def sum_small(values):
    bit = 1
    while bit < lax.axis_size("dp"):
        values = values + swap_bit(values, bit)
        bit *= 2
    return values


def start_out(w_out):
    at = lax.axis_index("dp")
    rows = w_out.shape[0] // 4
    place = (at & 1) * 2 + ((at >> 1) & 1)
    return swap_tensor(lax.dynamic_slice_in_dim(w_out, place * rows, rows, 0).astype(f32))


def per_device(
    layer_input,
    segments,
    expert_choice,
    dispatch_order,
    norm_gain_one,
    w_query,
    w_key,
    w_value,
    w_out,
    norm_gain_two,
    w_router,
    w_gate,
    w_up,
    w_down,
    out_grad,
):
    length = layer_input.shape[0]
    q_cols = w_query.shape[1]
    hid = w_down.shape[1]
    flat = lambda grad: grad.reshape(-1, grad.shape[-1])
    seg_row = segments
    seg_col = segments.reshape(length, 1)
    whole = start_out(w_out)
    input_one, qkv = project(layer_input, norm_gain_one[None, :], w_query, w_key, w_value)
    qkv, weights = together(qkv, (w_gate, w_up, w_down))
    swapped = start_experts(*weights)
    first = attn_fwd(qkv, seg_col, seg_row, q_cols, 0)
    first, whole, qkv = together(first, whole, qkv)
    got = swap_bit(whole, 2)
    second = attn_fwd(qkv, seg_col, seg_row, q_cols, 1)
    slot_row = route(expert_choice.T, dispatch_order)
    first, second, slot_row, got, swapped = together(first, second, slot_row, got, swapped)
    other = gather_experts(swapped)
    mine = [first, second]
    theirs = [swap_tensor(first), swap_tensor(second)]
    whole = gather_join(whole, got, 2)
    w_out_other = gather_join(whole, swap_bit(whole, 1), 1)
    slot_col = slot_row.T

    wr_t = jnp.pad(w_router.T.astype(f32), ((0, ROWS8 - EXPERTS), (0, 0)))
    g2 = norm_gain_two[None, :]
    side = jnp.full((1, 1), side_of(1), i32)
    h_part, dys = expert_pre(layer_input, mine, w_out, slot_row, out_grad)
    middle, input_two, gates, rows_in, *rest = expert_own(
        side,
        h_part,
        theirs,
        w_out_other,
        g2,
        wr_t,
        slot_row,
        dys,
        w_gate,
        w_up,
        w_down,
    )
    *kept, mine_up, send_up, mine_two, send_two = rest
    kept = [rows_in, dys, *kept]
    got_up = swap_bit(send_up, 1)
    got_two = swap_bit(send_two, 1)
    (up, two), gates = prepare([far_terms([mine_up, got_up]), x_terms([mine_two, got_two])], gates)
    up, two = send_all(*up), send_all(*two)
    block_out, grad_middle, grad_attn, small = expert_all(
        (gates, slot_row, slot_col),
        kept,
        (w_gate, w_up, w_down),
        other,
        (middle, input_two, g2, wr_t, out_grad),
    )
    grad_heads = jnp.einsum("td,nd->tn", grad_attn, w_out, preferred_element_type=f32).astype(bf16)
    up, two, grad_heads, grad_attn = together(up, two, grad_heads, grad_attn)
    attended = jnp.concatenate(mine, axis=1).astype(bf16)
    grad_wout = jnp.einsum("tn,td->nd", attended, grad_attn, preferred_element_type=f32)
    grad_wout = jnp.concatenate(column_blocks(grad_wout, hid), axis=0)
    (two, up, out), grad_heads = prepare(
        [far_terms(two), x_terms([total_of(up)]), core_terms(blocks_of(grad_wout))], grad_heads
    )
    two, up, out = [send_all(*one) for one in (two, up, out)]
    up, out, grad_heads = together(up, out, grad_heads)
    (out,), grad_heads = prepare([x_terms(out)], grad_heads)
    out = send_all(*out)
    dq, dk, dv = attn_bwd(qkv, grad_heads, seg_col, seg_row, q_cols)
    part, mine_qkv, send_qkv = attn_grads(side, input_one, dq, dk, dv, w_query, w_key, w_value)
    two, out, part, mine_qkv, send_qkv = together(two, out, part, mine_qkv, send_qkv)
    owned = jnp.concatenate([total_of(two).reshape(2, -1, hid), total_of(up)[None]], axis=0)
    sum_experts = lax.all_gather(owned, "dp", axis=1, tiled=True)
    part_other = swap_tensor(part)
    owned = [total_of(send_all(*far_terms(out)))]
    crossed = send_all(*x_terms([mine_qkv, swap_bit(send_qkv, 1)]))
    owned.append(total_of(send_all(*far_terms(crossed))))
    part_other, small, owned, sum_experts = together(part_other, small, owned, sum_experts)
    rest = lax.all_gather(jnp.concatenate(owned, axis=0), "dp", axis=0, tiled=False)
    residual = layer_input.astype(f32)
    inverse_one = lax.rsqrt(jnp.mean(residual * residual, axis=-1, keepdims=True) + norm_eps)
    normed_one = residual * inverse_one
    grad_input_one = part + part_other
    grad_gain_one = jnp.sum(grad_input_one * normed_one, axis=0)
    small = sum_small(jnp.concatenate([small[: EXPERTS + 1], grad_gain_one[None, :]], axis=0))
    scaled = grad_input_one * norm_gain_one
    mean_term = jnp.mean(scaled * normed_one, axis=-1, keepdims=True)
    grad_input = grad_middle + inverse_one * (scaled - normed_one * mean_term)
    split = owned[0].shape[0]
    half = split + owned[1].shape[0] // 2
    sum_out = rest[:, :split].reshape(-1, hid)
    sum_query = rest[:, split:half].reshape(-1, hid)
    sum_kv = rest[:, half:].reshape(-1, hid)
    sum_down = sum_experts[1].reshape(EXPERTS, D // hid, hid, hid)
    sum_down = jnp.concatenate([sum_down[:, c] for c in range(D // hid)], axis=-1)
    unblock = lambda rows, height: jnp.concatenate(
        [rows[at : at + height] for at in range(0, rows.shape[0], height)], axis=1
    )
    return (
        block_out,
        grad_input,
        small[EXPERTS + 1],
        unblock(sum_query, D),
        sum_kv[:D],
        sum_kv[D:],
        unblock(sum_out, q_cols),
        small[EXPERTS],
        small[:EXPERTS].T,
        sum_experts[0].reshape(w_gate.shape),
        sum_experts[2].reshape(w_up.shape),
        sum_down,
    )


def solution(mesh):
    in_specs = (
        P("dp", None),
        P("dp", None),
        P("dp", None),
        P("dp", None),
        P(),
        P(None, "tensor"),
        P(None, "tensor"),
        P(None, "tensor"),
        P("tensor", None),
        P(),
        P(),
        P(None, None, "tensor"),
        P(None, None, "tensor"),
        P(None, "tensor", None),
        P("dp", None),
    )
    out_specs = (
        P("dp", None),
        P("dp", None),
        P(),
        P(None, "tensor"),
        P(None, "tensor"),
        P(None, "tensor"),
        P("tensor", None),
        P(),
        P(),
        P(None, None, "tensor"),
        P(None, None, "tensor"),
        P(None, "tensor", None),
    )
    return jax.shard_map(
        per_device, mesh=mesh, in_specs=in_specs, out_specs=out_specs, check_vma=False
    )
```

```python
import functools

import jax
import jax.numpy as jnp
from jax import lax
from jax.experimental import pallas as pl
from jax.experimental.pallas import tpu as pltpu
from jax.sharding import PartitionSpec as P

D = 1024
HEAD_DIM = 64
EXPERTS = 4
TOPK = 2
CAP = 640
MOST = 512
ROWS8 = 8

norm_eps = 1e-05
masked_value = -1e30
f32 = jnp.float32
bf16 = jnp.bfloat16
i32 = jnp.int32

NN = (((1,), (0,)), ((), ()))
NT = (((1,), (1,)), ((), ()))
TN = (((0,), (0,)), ((), ()))


def mm(left, right, dims=NN):
    return lax.dot_general(left, right, dims, preferred_element_type=f32)


def full_spec(shape):
    zeros = (0,) * len(shape)
    return pl.BlockSpec(shape, lambda *_: zeros, pipeline_mode=pl.Buffered(1))


def route_kernel(choice_ref, order_ref, slot_ref):
    length = choice_ref.shape[1]
    pairs = 2 * length
    order = order_ref[...]
    where_pair = (order & 1) * length + (order >> 1)
    match = (lax.broadcasted_iota(i32, (pairs, pairs), 0) == where_pair).astype(f32).astype(bf16)
    experts = lax.broadcasted_iota(i32, (ROWS8, length), 0)
    first = (choice_ref[0:1, :] == experts).astype(f32)
    second = (choice_ref[1:2, :] == experts).astype(f32)
    hot = jnp.concatenate([first, second], axis=1)
    ordered = mm(hot.astype(bf16), match)
    step = 512
    tri = (
        lax.broadcasted_iota(i32, (step, step), 0) < lax.broadcasted_iota(i32, (step, step), 1)
    ).astype(f32)
    carry = jnp.zeros((ROWS8, 1), f32)
    ranks = []
    for begin in range(0, pairs, step):
        part = ordered[:, begin : begin + step]
        inside = mm(part.astype(bf16), tri.astype(bf16)) + carry
        ranks.append(jnp.sum(inside * part, axis=0, keepdims=True))
        carry = carry + jnp.sum(part, axis=1, keepdims=True)
    rank = jnp.concatenate(ranks, axis=1)
    high = jnp.floor(rank * (1.0 / 64.0))
    low_part = rank - 64.0 * high
    row_id = lax.broadcasted_iota(i32, (ROWS8, pairs), 0)
    both = jnp.where(row_id == 0, high, jnp.where(row_id == 1, low_part, 0.0))
    back = mm(both.astype(bf16), match, NT)
    slot = (64.0 * back[0:1, :] + back[1:2, :]).astype(i32)
    slot_ref[...] = jnp.where(
        first > 0.5, slot[:, :length], jnp.where(second > 0.5, slot[:, length:], -1)
    )


def route(choice_t, order):
    length = choice_t.shape[1]
    return pl.pallas_call(
        route_kernel,
        out_shape=jax.ShapeDtypeStruct((ROWS8, length), i32),
        compiler_params=pltpu.CompilerParams(vmem_limit_bytes=50 << 20),
        cost_estimate=pl.CostEstimate(flops=1, transcendentals=0, bytes_accessed=1),
        name="route",
    )(choice_t, order)


def project_kernel(x_ref, g_ref, wq_ref, wk_ref, wv_ref, xn_ref, qkv_ref):
    x = x_ref[...].astype(f32)
    inverse = lax.rsqrt(jnp.mean(x * x, axis=1, keepdims=True) + norm_eps)
    xn = (x * inverse * g_ref[...]).astype(bf16)
    xn_ref[...] = xn
    at = 0
    for w_ref in (wq_ref, wk_ref, wv_ref):
        wide = w_ref.shape[1]
        qkv_ref[:, at : at + wide] = mm(xn, w_ref[...]).astype(bf16)
        at += wide


def project(x, gain, w_query, w_key, w_value):
    length = x.shape[0]
    q_cols = w_query.shape[1]
    kv_cols = w_key.shape[1]
    wide = q_cols + 2 * kv_cols
    rows = 256
    return pl.pallas_call(
        project_kernel,
        grid=(length // rows,),
        in_specs=[
            pl.BlockSpec((rows, D), lambda i: (i, 0)),
            full_spec((1, D)),
            full_spec((D, q_cols)),
            full_spec((D, kv_cols)),
            full_spec((D, kv_cols)),
        ],
        out_specs=[
            pl.BlockSpec((rows, D), lambda i: (i, 0)),
            pl.BlockSpec((rows, wide), lambda i: (i, 0)),
        ],
        out_shape=[
            jax.ShapeDtypeStruct((length, D), bf16),
            jax.ShapeDtypeStruct((length, wide), bf16),
        ],
        cost_estimate=pl.CostEstimate(flops=1, transcendentals=0, bytes_accessed=1),
        name="project",
    )(x, gain, w_query, w_key, w_value)


def attn_blocks(length, rows):
    blocks = []
    for begin in range(0, length, rows):
        start = max(0, begin + rows - MOST - rows)
        start = max(0, (begin + 1 - MOST) // 128 * 128)
        blocks.append((begin, start, begin + rows))
    return blocks


def attn_fwd_kernel(rows, q_ref, k_ref, v_ref, segc_ref, segr_ref, o_ref):
    length = q_ref.shape[0]
    for begin, start, stop in attn_blocks(length, rows):
        wide = stop - start
        row_pos = begin + lax.broadcasted_iota(i32, (rows, wide), 0)
        col_pos = start + lax.broadcasted_iota(i32, (rows, wide), 1)
        allowed = (segc_ref[begin:stop, :] == segr_ref[:, start:stop]) & (col_pos <= row_pos)
        bias = jnp.where(allowed, 0.0, masked_value)
        bias = jnp.concatenate([bias, bias], axis=0)
        for kv in range(2):
            lo = kv * HEAD_DIM
            q_two = jnp.concatenate(
                [
                    q_ref[begin:stop, 2 * lo : 2 * lo + HEAD_DIM],
                    q_ref[begin:stop, 2 * lo + HEAD_DIM : 2 * lo + 2 * HEAD_DIM],
                ],
                axis=0,
            )
            q_two = q_two * jnp.asarray(HEAD_DIM**-0.5, bf16)
            scores = mm(q_two, k_ref[start:stop, lo : lo + HEAD_DIM], NT) + bias
            peak = jnp.max(scores, axis=1, keepdims=True)
            raised = jnp.exp(scores - peak)
            total = jnp.sum(raised, axis=1, keepdims=True)
            probs = (raised * (1.0 / total)).astype(bf16)
            out = mm(probs, v_ref[start:stop, lo : lo + HEAD_DIM])
            out = out.astype(bf16).astype(f32)
            o_ref[begin:stop, 2 * lo : 2 * lo + 2 * HEAD_DIM] = jnp.concatenate(
                [out[:rows], out[rows:]], axis=1
            )


def attn_fwd(qkv, seg_col, seg_row, q_cols, g):
    length = qkv.shape[0]
    pairs = q_cols // 256
    return pl.pallas_call(
        functools.partial(attn_fwd_kernel, 256),
        grid=(1,),
        in_specs=[
            pl.BlockSpec((length, 256), lambda _: (0, g)),
            pl.BlockSpec((length, 128), lambda _: (0, 2 * pairs + g)),
            pl.BlockSpec((length, 128), lambda _: (0, 3 * pairs + g)),
            full_spec((length, 1)),
            full_spec((1, length)),
        ],
        out_specs=pl.BlockSpec((length, 256), lambda _: (0, 0)),
        out_shape=jax.ShapeDtypeStruct((length, 256), f32),
        compiler_params=pltpu.CompilerParams(vmem_limit_bytes=50 << 20),
        cost_estimate=pl.CostEstimate(flops=1, transcendentals=0, bytes_accessed=1),
        name="attn_fwd",
    )(qkv, qkv, qkv, seg_col, seg_row)


def attn_bwd_kernel(
    rows, q_ref, k_ref, v_ref, do_ref, segc_ref, segr_ref, dq_ref, dk_ref, dv_ref, dks, dvs
):
    length = q_ref.shape[0]
    scale = HEAD_DIM**-0.5
    dks[...] = jnp.zeros_like(dks)
    dvs[...] = jnp.zeros_like(dvs)
    for begin, start, stop in attn_blocks(length, rows):
        wide = stop - start
        row_pos = begin + lax.broadcasted_iota(i32, (wide, rows), 1)
        col_pos = start + lax.broadcasted_iota(i32, (wide, rows), 0)
        allowed = (segr_ref[:, begin:stop] == segc_ref[start:stop, :]) & (col_pos <= row_pos)
        bias = jnp.where(allowed, 0.0, masked_value)
        bias = jnp.concatenate([bias, bias], axis=1)
        for kv in range(2):
            lo = kv * HEAD_DIM
            q_two = jnp.concatenate(
                [
                    q_ref[begin:stop, 2 * lo : 2 * lo + HEAD_DIM],
                    q_ref[begin:stop, 2 * lo + HEAD_DIM : 2 * lo + 2 * HEAD_DIM],
                ],
                axis=0,
            )
            q_two = q_two * jnp.asarray(scale, bf16)
            do_two = jnp.concatenate(
                [
                    do_ref[begin:stop, 2 * lo : 2 * lo + HEAD_DIM],
                    do_ref[begin:stop, 2 * lo + HEAD_DIM : 2 * lo + 2 * HEAD_DIM],
                ],
                axis=0,
            )
            k_win = k_ref[start:stop, lo : lo + HEAD_DIM]
            v_win = v_ref[start:stop, lo : lo + HEAD_DIM]
            scores = mm(k_win, q_two, NT) + bias
            peak = jnp.max(scores, axis=0, keepdims=True)
            raised = jnp.exp(scores - peak)
            total = jnp.sum(raised, axis=0, keepdims=True)
            probs = raised * (1.0 / total)
            grad_probs = mm(v_win, do_two, NT)
            row_dot = jnp.sum(probs * grad_probs, axis=0, keepdims=True)
            grad_scores = (probs * (grad_probs - row_dot)).astype(bf16)
            dvs[start:stop, lo : lo + HEAD_DIM] += mm(probs.astype(bf16), do_two)
            dks[start:stop, lo : lo + HEAD_DIM] += mm(grad_scores, q_two)
            dq = (mm(grad_scores, k_win, TN) * scale).astype(bf16)
            dq_ref[begin:stop, 2 * lo : 2 * lo + 2 * HEAD_DIM] = jnp.concatenate(
                [dq[:rows], dq[rows:]], axis=1
            )
    dk_ref[...] = dks[...].astype(bf16)
    dv_ref[...] = dvs[...].astype(bf16)


def attn_bwd(qkv, grad_heads, seg_col, seg_row, q_cols):
    length = qkv.shape[0]
    pairs = q_cols // 256
    return pl.pallas_call(
        functools.partial(attn_bwd_kernel, 256),
        grid=(pairs,),
        in_specs=[
            pl.BlockSpec((length, 256), lambda g: (0, g)),
            pl.BlockSpec((length, 128), lambda g: (0, 2 * pairs + g)),
            pl.BlockSpec((length, 128), lambda g: (0, 3 * pairs + g)),
            pl.BlockSpec((length, 256), lambda g: (0, g)),
            full_spec((length, 1)),
            full_spec((1, length)),
        ],
        out_specs=[
            pl.BlockSpec((length, 256), lambda g: (0, g)),
            pl.BlockSpec((length, 128), lambda g: (0, g)),
            pl.BlockSpec((length, 128), lambda g: (0, g)),
        ],
        out_shape=[
            jax.ShapeDtypeStruct((length, q_cols), bf16),
            jax.ShapeDtypeStruct((length, q_cols // 2), bf16),
            jax.ShapeDtypeStruct((length, q_cols // 2), bf16),
        ],
        scratch_shapes=[pltpu.VMEM((length, 128), f32), pltpu.VMEM((length, 128), f32)],
        compiler_params=pltpu.CompilerParams(vmem_limit_bytes=50 << 20),
        cost_estimate=pl.CostEstimate(flops=24213000000, transcendentals=0, bytes_accessed=1),
        name="attn_bwd",
    )(qkv, qkv, qkv, grad_heads, seg_col, seg_row)


def attn_grads_kernel(
    side_ref, xn_ref, dq_ref, dk_ref, dv_ref, wq_ref, wk_ref, wv_ref, part_ref, mine_ref, send_ref, keep
):
    xn = xn_ref[...]
    wide = dk_ref.shape[1]
    side = side_ref[0, 0]
    queries = [mm(xn, dq_ref[:, c : c + wide], TN) for c in range(0, dq_ref.shape[1], wide)]
    hand_out(jnp.concatenate(queries, axis=0), keep, side, mine_ref, send_ref, 0)
    values = [mm(xn, dk_ref[...], TN), mm(xn, dv_ref[...], TN)]
    hand_out(jnp.concatenate(values, axis=0), keep, side, mine_ref, send_ref, 1)
    part = mm(dq_ref[...], wq_ref[...], NT) + mm(dk_ref[...], wk_ref[...], NT)
    part_ref[...] = part + mm(dv_ref[...], wv_ref[...], NT)


def attn_grads(side, xn, dq, dk, dv, w_query, w_key, w_value):
    length = xn.shape[0]
    wide = dk.shape[1]
    parts = lax.axis_size("dp")
    rows = 2 * dq.shape[1] // wide * D // parts
    shape = jax.ShapeDtypeStruct((parts // 4, 2, rows, wide), f32)
    arrays = (xn, dq, dk, dv, w_query, w_key, w_value)
    return pl.pallas_call(
        attn_grads_kernel,
        grid=(1,),
        in_specs=[pl.BlockSpec(memory_space=pltpu.SMEM)] + [full_spec(one.shape) for one in arrays],
        out_specs=[full_spec((length, D)), full_spec(shape.shape), full_spec(shape.shape)],
        out_shape=[jax.ShapeDtypeStruct((length, D), f32), shape, shape],
        scratch_shapes=[pltpu.VMEM((dq.shape[1] // wide * D, wide), f32)],
        compiler_params=pltpu.CompilerParams(vmem_limit_bytes=50 << 20),
        cost_estimate=pl.CostEstimate(flops=1, transcendentals=0, bytes_accessed=1),
        name="attn_grads",
    )(side, *arrays)


def attn_sums_kernel(in_ref, out_ref, q_ref, k_ref, v_ref):
    c = pl.program_id(0)
    pieces = in_ref.shape[0]
    rows = in_ref.shape[1] // 3
    for p in range(pieces):
        to = slice(p * rows, (p + 1) * rows)
        out_ref[to, :] = in_ref[p, :rows, :]
        q_ref[to, :] = in_ref[p, rows : 2 * rows, :]

    @pl.when(c < 2)
    def _():
        for p in range(pieces):
            k_ref[p * rows : (p + 1) * rows, :] = in_ref[p, 2 * rows :, :]

    @pl.when(c >= 2)
    def _():
        for p in range(pieces):
            v_ref[p * rows : (p + 1) * rows, :] = in_ref[p, 2 * rows :, :]


def attn_sums(gathered, q_cols):
    parts, rows, wide = gathered.shape
    block = (q_cols, wide)
    return pl.pallas_call(
        attn_sums_kernel,
        grid=(4,),
        in_specs=[pl.BlockSpec((parts // 4, rows, wide), lambda c: (c, 0, 0))],
        out_specs=[
            pl.BlockSpec(block, lambda c: (0, c)),
            pl.BlockSpec(block, lambda c: (c % 2, c // 2)),
            pl.BlockSpec(block, lambda c: (jnp.minimum(c, 1), 0)),
            pl.BlockSpec(block, lambda c: (jnp.maximum(c - 2, 0), 0)),
        ],
        out_shape=[
            jax.ShapeDtypeStruct((q_cols, D), f32),
            jax.ShapeDtypeStruct((D, q_cols), f32),
            jax.ShapeDtypeStruct((D, wide), f32),
            jax.ShapeDtypeStruct((D, wide), f32),
        ],
        cost_estimate=pl.CostEstimate(flops=5_000_000_000, transcendentals=0, bytes_accessed=1),
        name="attn_sums",
    )(gathered)


def place_rows(slot_row, length):
    return lax.broadcasted_iota(i32, (CAP, length), 0) == slot_row


def expert_pre_kernel(groups, *refs):
    x_ref = refs[0]
    oa = refs[1 : 1 + groups]
    wo_ref, slotr_ref, dy_ref, h_ref, dys_ref = refs[1 + groups :]
    e = pl.program_id(0)
    length = x_ref.shape[0]
    step = length // EXPERTS
    rows = pl.ds(pl.multiple_of(e * step, step), step)
    total = x_ref[rows, :].astype(f32)
    for g in range(groups):
        total = total + mm(oa[g][rows, :].astype(bf16), wo_ref[g * 256 : (g + 1) * 256, :])
    h_ref[...] = total
    place = place_rows(slotr_ref[pl.ds(e, 1), :], length).astype(f32).astype(bf16)
    dys_ref[...] = mm(place, dy_ref[...]).astype(bf16)


def expert_pre(x, mine, w_out, slot_row, dy):
    length = x.shape[0]
    groups = len(mine)
    return pl.pallas_call(
        functools.partial(expert_pre_kernel, groups),
        grid=(EXPERTS,),
        in_specs=[full_spec((length, D))]
        + [full_spec((length, 256))] * groups
        + [full_spec(w_out.shape), full_spec((ROWS8, length)), full_spec((length, D))],
        out_specs=[
            pl.BlockSpec((length // EXPERTS, D), lambda e: (e, 0)),
            pl.BlockSpec((CAP, D), lambda e: (e, 0)),
        ],
        out_shape=[
            jax.ShapeDtypeStruct((length, D), f32),
            jax.ShapeDtypeStruct((EXPERTS * CAP, D), bf16),
        ],
        compiler_params=pltpu.CompilerParams(vmem_limit_bytes=50 << 20),
        cost_estimate=pl.CostEstimate(flops=1, transcendentals=0, bytes_accessed=1),
        name="expert_pre",
    )(x, *mine, w_out, slot_row, dy)


def hand_out(value, keep, side, mine_ref, send_ref, place=0):
    keep[...] = value
    far = mine_ref.shape[0]
    rows = value.shape[0] // (4 * far)
    to = slice(place * rows, (place + 1) * rows)
    for z in range(far):
        for x in range(2):
            at = 4 * z + 2 * x
            mine_ref[z, x, to] = keep[pl.ds(pl.multiple_of((at + side) * rows, rows), rows), :]
            send_ref[z, x, to] = keep[pl.ds(pl.multiple_of((at + 1 - side) * rows, rows), rows), :]


def expert_own_kernel(groups, side_ref, *refs):
    part_ref = refs[0]
    ob = refs[1 : 1 + groups]
    wox_pieces = refs[1 + groups : 5 + groups]
    (
        g2_ref,
        wr_ref,
        slotr_ref,
        dys_ref,
        wg_ref,
        wu_ref,
        wd_ref,
        h_ref,
        xn_ref,
        gate_ref,
        rows_ref,
        hid_ref,
        dg_ref,
        du_ref,
        mine_up,
        send_up,
        mine_two,
        send_two,
        keep,
        wox_ref,
    ) = refs[5 + groups :]
    side = side_ref[0, 0]
    e = pl.program_id(0)
    length = part_ref.shape[0]
    chunk = 256

    @pl.when(e == 0)
    def _():
        x_side = side_ref[0, 1]
        for at, piece in enumerate(wox_pieces):
            core = side if at < 2 else 1 - side
            place = 2 * core + (x_side if at % 2 == 0 else 1 - x_side)
            height = piece.shape[0]
            to = pl.ds(pl.multiple_of(place * height, height), height)
            wox_ref[to, :] = piece[...].astype(bf16)
        for c in range(length // chunk):
            rows = slice(c * chunk, (c + 1) * chunk)
            h1 = part_ref[rows, :]
            for g in range(groups):
                cols = slice(g * 256, (g + 1) * 256)
                h1 = h1 + mm(ob[g][rows, :].astype(bf16), wox_ref[cols, :])
            h_ref[rows, :] = h1
            inverse = lax.rsqrt(jnp.mean(h1 * h1, axis=1, keepdims=True) + norm_eps)
            xn_ref[rows, :] = (h1 * inverse * g2_ref[...]).astype(bf16)
        logits = mm(wr_ref[...].astype(bf16), xn_ref[...], NT)
        chosen = slotr_ref[...] >= 0
        logits = jnp.where(chosen, logits, masked_value)
        peak = jnp.max(logits, axis=0, keepdims=True)
        raised = jnp.where(chosen, jnp.exp(logits - peak), 0.0)
        gate_ref[...] = raised / jnp.sum(raised, axis=0, keepdims=True)

    mask = place_rows(slotr_ref[pl.ds(e, 1), :], length)
    place = mask.astype(f32).astype(bf16)
    gate = jnp.sum(jnp.where(mask, gate_ref[pl.ds(e, 1), :], 0.0), axis=1, keepdims=True)
    rows_in = mm(place, xn_ref[...]).astype(bf16)
    rows_ref[...] = rows_in
    dy_gated = (gate * dys_ref[...].astype(f32)).astype(bf16)
    g = mm(rows_in, wg_ref[0])
    u = mm(rows_in, wu_ref[0])
    sig = 1.0 / (1.0 + jnp.exp(-g))
    act = g * sig
    hid = (act * u).astype(bf16)
    dhid = mm(dy_gated, wd_ref[0], NT)
    dg = (dhid * u * sig * (1.0 + g * (1.0 - sig))).astype(bf16)
    du = (dhid * act).astype(bf16)
    hid_ref[...] = hid
    dg_ref[...] = dg
    du_ref[...] = du
    both = mm(rows_in, jnp.concatenate([du, dg], axis=1), TN)
    half = du.shape[1]
    hand_out(both[:, :half], keep, side, mine_up, send_up)
    hand_out(both[:, half:], keep, side, mine_two, send_two)
    dwd = mm(hid, dy_gated, TN)
    wide = hid.shape[1]
    blocks = [dwd[:, c : c + wide] for c in range(0, D, wide)]
    hand_out(jnp.concatenate(blocks, axis=0), keep, side, mine_two, send_two, 1)


def piece_specs(hid, arrays):
    parts = lax.axis_size("dp")
    far = parts // 4
    rows = arrays * EXPERTS * D // parts
    spec = pl.BlockSpec((far // EXPERTS, 2, rows, hid), lambda e: (e, 0, 0, 0))
    return spec, jax.ShapeDtypeStruct((far, 2, rows, hid), f32)


def expert_own(side, part, theirs, w_out_other, g2, wr_t, slot_row, dys, w_gate, w_up, w_down):
    length = part.shape[0]
    hid = w_down.shape[1]
    groups = len(theirs)
    slots = EXPERTS * CAP
    q_cols = 4 * w_out_other[0].shape[0]
    piece, shape = piece_specs(hid, 1)
    piece_two, shape_two = piece_specs(hid, 2)
    return pl.pallas_call(
        functools.partial(expert_own_kernel, groups),
        grid=(EXPERTS,),
        in_specs=[pl.BlockSpec(memory_space=pltpu.SMEM), full_spec((length, D))]
        + [full_spec((length, 256))] * groups
        + [
            *[full_spec(one.shape) for one in w_out_other],
            full_spec((1, D)),
            full_spec((ROWS8, D)),
            full_spec((ROWS8, length)),
            pl.BlockSpec((CAP, D), lambda e: (e, 0)),
            pl.BlockSpec((1, D, hid), lambda e: (e, 0, 0)),
            pl.BlockSpec((1, D, hid), lambda e: (e, 0, 0)),
            pl.BlockSpec((1, hid, D), lambda e: (e, 0, 0)),
        ],
        out_specs=[
            full_spec((length, D)),
            full_spec((length, D)),
            full_spec((ROWS8, length)),
            pl.BlockSpec((CAP, D), lambda e: (e, 0)),
            pl.BlockSpec((CAP, hid), lambda e: (e, 0)),
            pl.BlockSpec((CAP, hid), lambda e: (e, 0)),
            pl.BlockSpec((CAP, hid), lambda e: (e, 0)),
            piece,
            piece,
            piece_two,
            piece_two,
        ],
        out_shape=[
            jax.ShapeDtypeStruct((length, D), f32),
            jax.ShapeDtypeStruct((length, D), bf16),
            jax.ShapeDtypeStruct((ROWS8, length), f32),
            jax.ShapeDtypeStruct((slots, D), bf16),
            jax.ShapeDtypeStruct((slots, hid), bf16),
            jax.ShapeDtypeStruct((slots, hid), bf16),
            jax.ShapeDtypeStruct((slots, hid), bf16),
            shape,
            shape,
            shape_two,
            shape_two,
        ],
        scratch_shapes=[pltpu.VMEM((D, hid), f32), pltpu.VMEM((q_cols, D), bf16)],
        compiler_params=pltpu.CompilerParams(vmem_limit_bytes=60 << 20),
        cost_estimate=pl.CostEstimate(flops=39202000000, transcendentals=0, bytes_accessed=1),
        name="expert_own",
    )(side, part, *theirs, *w_out_other, g2, wr_t, slot_row, dys, w_gate, w_up, w_down)


def expert_all_kernel(
    gate_ref,
    slotr_ref,
    slotc_ref,
    rows_ref,
    dys_ref,
    hid_ref,
    dg_ref,
    du_ref,
    wg_ref,
    wu_ref,
    wd_ref,
    wgx_ref,
    wux_ref,
    wdx_ref,
    *rest,
):
    (h_ref, xn_ref, g2_ref, wr_ref, dy_ref) = rest[:5]
    (out_ref, dh_ref, da_ref, small_ref, moe_s, dgate_s) = rest[5:]
    e = pl.program_id(0)
    length = slotr_ref.shape[1]
    chunk = 256

    @pl.when(e == 0)
    def _():
        moe_s[...] = jnp.zeros_like(moe_s)
        dh_ref[...] = jnp.zeros_like(dh_ref)
        dgate_s[...] = jnp.zeros_like(dgate_s)

    mask = place_rows(slotr_ref[pl.ds(e, 1), :], length)
    lane8 = lax.broadcasted_iota(i32, (length, ROWS8), 1)
    slot_col = jnp.sum(jnp.where(lane8 == e, slotc_ref[...], 0), axis=1, keepdims=True)
    place_t = (lax.broadcasted_iota(i32, (length, CAP), 1) == slot_col).astype(f32).astype(bf16)
    gate = jnp.sum(jnp.where(mask, gate_ref[pl.ds(e, 1), :], 0.0), axis=1, keepdims=True)
    rows_in = rows_ref[...]
    dy_slot = dys_ref[...].astype(f32)
    dy_gated = (gate * dy_slot).astype(bf16)
    hid_wide = wgx_ref.shape[1]
    wg = wgx_ref[...].astype(bf16)
    wu = wux_ref[...].astype(bf16)
    wd = jnp.concatenate(
        [wdx_ref[c * hid_wide : (c + 1) * hid_wide, :] for c in range(D // hid_wide)], axis=1
    ).astype(bf16)
    g = mm(rows_in, wg)
    u = mm(rows_in, wu)
    sig = 1.0 / (1.0 + jnp.exp(-g))
    act = g * sig
    hid = (act * u).astype(bf16)
    dhid = mm(dy_gated, wd, NT)
    dg = (dhid * u * sig * (1.0 + g * (1.0 - sig))).astype(bf16)
    du = (dhid * act).astype(bf16)
    y = mm(hid_ref[...], wd_ref[0]) + mm(hid, wd)
    dx = mm(dg_ref[...], wg_ref[0], NT) + mm(du_ref[...], wu_ref[0], NT)
    dx = dx + mm(dg, wg, NT) + mm(du, wu, NT)
    dgate_slot = jnp.sum(dy_slot * y, axis=1, keepdims=True)
    dgate_s[pl.ds(e, 1), :] = jnp.sum(jnp.where(mask, dgate_slot, 0.0), axis=0, keepdims=True)
    moe_s[...] += mm(place_t, (gate * y).astype(bf16))
    dh_ref[...] += mm(place_t, dx.astype(bf16))

    @pl.when(e == EXPERTS - 1)
    def _():
        gates = gate_ref[...]
        dgates = dgate_s[...]
        dsel = gates * (dgates - jnp.sum(gates * dgates, axis=0, keepdims=True))
        drouter = mm(dsel.astype(bf16), xn_ref[...])
        wr = wr_ref[...].astype(bf16)
        dlog_t = dsel.T.astype(bf16)
        small_ref[...] = jnp.zeros_like(small_ref)
        small_ref[0:EXPERTS, :] = drouter[0:EXPERTS, :]
        gain = jnp.zeros((1, D), f32)
        for c in range(length // chunk):
            rows = slice(c * chunk, (c + 1) * chunk)
            h1 = h_ref[rows, :]
            out_ref[rows, :] = (h1 + moe_s[rows, :]).astype(bf16)
            inverse = lax.rsqrt(jnp.mean(h1 * h1, axis=1, keepdims=True) + norm_eps)
            n2 = h1 * inverse
            dxn = dh_ref[rows, :] + mm(dlog_t[rows, :], wr)
            gain = gain + jnp.sum(dxn * n2, axis=0, keepdims=True)
            scaled = dxn * g2_ref[...]
            mean_term = jnp.mean(scaled * n2, axis=1, keepdims=True)
            dh1 = dy_ref[rows, :].astype(f32) + inverse * (scaled - n2 * mean_term)
            dh_ref[rows, :] = dh1
            da_ref[rows, :] = dh1.astype(bf16)
        small_ref[EXPERTS : EXPERTS + 1, :] = gain


def expert_all(routing, kept, weights, other, tail):
    gates, slot_row, slot_col = routing
    w_gate, w_up, w_down = weights
    length = slot_row.shape[1]
    hid = w_down.shape[1]
    slot_block = lambda wide: pl.BlockSpec((CAP, wide), lambda e: (e, 0))
    weight_in = pl.BlockSpec((1, D, hid), lambda e: (e, 0, 0))
    other_block = lambda at: pl.BlockSpec((D, hid), lambda e: (at + e, 0))
    whole = full_spec((length, D))
    in_specs = [
        full_spec((ROWS8, length)),
        full_spec((ROWS8, length)),
        full_spec((length, ROWS8)),
        slot_block(D),
        slot_block(D),
        slot_block(hid),
        slot_block(hid),
        slot_block(hid),
        weight_in,
        weight_in,
        pl.BlockSpec((1, hid, D), lambda e: (e, 0, 0)),
        other_block(0),
        other_block(EXPERTS),
        other_block(2 * EXPERTS),
    ]
    in_specs += [whole, whole, full_spec((1, D)), full_spec((ROWS8, D)), whole]
    return pl.pallas_call(
        expert_all_kernel,
        grid=(EXPERTS,),
        in_specs=in_specs,
        out_specs=[whole, whole, whole, full_spec((ROWS8, D))],
        out_shape=[
            jax.ShapeDtypeStruct((length, D), bf16),
            jax.ShapeDtypeStruct((length, D), f32),
            jax.ShapeDtypeStruct((length, D), bf16),
            jax.ShapeDtypeStruct((ROWS8, D), f32),
        ],
        scratch_shapes=[pltpu.VMEM((length, D), f32), pltpu.VMEM((ROWS8, length), f32)],
        compiler_params=pltpu.CompilerParams(vmem_limit_bytes=60 << 20),
        cost_estimate=pl.CostEstimate(flops=24_000_000_000, transcendentals=0, bytes_accessed=1),
        name="expert_all",
    )(gates, slot_row, slot_col, *kept, w_gate, w_up, w_down, other, other, other, *tail)


def swap_tensor(values):
    size = lax.axis_size("tensor")
    return lax.ppermute(values, "tensor", [(i, i ^ 1) for i in range(size)])


def together(*values):
    return lax.optimization_barrier(values)


def column_blocks(values, wide):
    return [values[..., c : c + wide] for c in range(0, values.shape[-1], wide)]


def start_experts(w_gate, w_up, w_down):
    parts = lax.axis_size("dp")
    at = lax.axis_index("dp")
    hid = w_down.shape[1]
    down = jnp.stack(column_blocks(w_down, hid), axis=1)
    shares = []
    for packed in (w_gate, w_up, down):
        packed = packed.reshape(-1, hid)
        rows = packed.shape[0] // parts
        shares.append(lax.dynamic_slice_in_dim(packed, at * rows, rows, 0))
    return swap_tensor(jnp.stack(shares).astype(f32))


def gather_experts(swapped):
    whole = lax.all_gather(swapped, "dp", axis=1, tiled=True)
    return whole.reshape(-1, whole.shape[-1])


def swap_bit(values, bit):
    size = lax.axis_size("dp")
    return lax.ppermute(values, "dp", [(i, i ^ bit) for i in range(size)])


def side_of(bit):
    return (lax.axis_index("dp") // bit) & 1


def blocks_of(values):
    parts = lax.axis_size("dp")
    return values.reshape(parts // 4, 2, 2, -1, values.shape[-1])


def picked(terms, which, axis):
    total = None
    for term in terms:
        part = lax.dynamic_index_in_dim(term, which, axis, keepdims=False)
        total = part if total is None else total + part
    return total


def core_terms(values):
    side = side_of(1)
    return picked([values], side, 2), [(picked([values], 1 - side, 2), 1)]


def x_terms(terms):
    side = side_of(2)
    axis = terms[0].ndim - 3
    return picked(terms, side, axis), [(picked(terms, 1 - side, axis), 2)]


def far_terms(terms):
    size = terms[0].shape[0]
    me = lax.axis_index("dp") // 4
    sends = [(picked(terms, me ^ k, 0), 4 * k) for k in range(size - 1, 0, -1)]
    return picked(terms, me, 0), sends


def ring_order(size):
    if size <= 2:
        return list(range(size))
    return [0] + list(range(1, size, 2)) + list(range(size - 2, 0, -2))


def ring_send(values):
    order = ring_order(lax.axis_size("dp") // 4)
    pairs = []
    for at, source in enumerate(order):
        target = order[(at + 1) % len(order)]
        pairs += [(source * 4 + low, target * 4 + low) for low in range(4)]
    return lax.ppermute(values, "dp", pairs)


def ring_sum(terms):
    order = ring_order(lax.axis_size("dp") // 4)
    size = len(order)
    place = jnp.asarray([order.index(z) for z in range(size)], i32)[lax.axis_index("dp") // 4]
    members = jnp.asarray(order, i32)
    piece = lambda p: picked(terms, members[jnp.mod(p, size)], 0)
    packet = piece(place - 1)
    for step in range(size - 1):
        packet = ring_send(packet) + piece(place - 2 - step)
    return packet


def send_all(keep, sends):
    return [keep] + [swap_bit(values, bit) for values, bit in sends]


def prepare(staged, *others):
    bits = [[bit for _, bit in sends] for _, sends in staged]
    values = [(keep, [value for value, _ in sends]) for keep, sends in staged]
    values, *others = together(values, *others)
    staged = [(keep, list(zip(sends, bit))) for (keep, sends), bit in zip(values, bits)]
    return [staged, *others]


def total_of(terms):
    return sum(terms[1:], terms[0])


def sum_small(values):
    bit = 1
    while bit < lax.axis_size("dp"):
        values = values + swap_bit(values, bit)
        bit *= 2
    return values


def start_out(w_out):
    at = lax.axis_index("dp")
    rows = w_out.shape[0] // 4
    place = (at & 1) * 2 + ((at >> 1) & 1)
    return swap_tensor(lax.dynamic_slice_in_dim(w_out, place * rows, rows, 0).astype(f32))


def per_device(
    layer_input,
    segments,
    expert_choice,
    dispatch_order,
    norm_gain_one,
    w_query,
    w_key,
    w_value,
    w_out,
    norm_gain_two,
    w_router,
    w_gate,
    w_up,
    w_down,
    out_grad,
):
    length = layer_input.shape[0]
    q_cols = w_query.shape[1]
    hid = w_down.shape[1]
    flat = lambda grad: grad.reshape(-1, grad.shape[-1])
    seg_row = segments
    seg_col = segments.reshape(length, 1)
    piece = start_out(w_out)
    input_one, qkv = project(layer_input, norm_gain_one[None, :], w_query, w_key, w_value)
    qkv, weights = together(qkv, (w_gate, w_up, w_down))
    swapped = start_experts(*weights)
    first = attn_fwd(qkv, seg_col, seg_row, q_cols, 0)
    first, piece, qkv = together(first, piece, qkv)
    first_other = swap_tensor(first)
    across = swap_bit(piece, 2)
    second = attn_fwd(qkv, seg_col, seg_row, q_cols, 1)
    slot_row = route(expert_choice.T, dispatch_order)
    second, slot_row, across, swapped = together(second, slot_row, across, swapped)
    other = gather_experts(swapped)
    mine = [first, second]
    theirs = [first_other, swap_tensor(second)]
    w_out_other = [piece, across, swap_bit(piece, 1), swap_bit(across, 1)]
    slot_col = slot_row.T

    wr_t = jnp.pad(w_router.T.astype(f32), ((0, ROWS8 - EXPERTS), (0, 0)))
    g2 = norm_gain_two[None, :]
    side = jnp.stack([side_of(1), side_of(2), lax.axis_index("dp") // 4]).astype(i32)[None, :]
    h_part, dys = expert_pre(layer_input, mine, w_out, slot_row, out_grad)
    middle, input_two, gates, rows_in, *rest = expert_own(
        side,
        h_part,
        theirs,
        w_out_other,
        g2,
        wr_t,
        slot_row,
        dys,
        w_gate,
        w_up,
        w_down,
    )
    *kept, mine_up, send_up, mine_two, send_two = rest
    kept = [rows_in, dys, *kept]
    got_up = swap_bit(send_up, 1)
    got_two = swap_bit(send_two, 1)
    (up, two), gates = prepare([far_terms([mine_up, got_up]), x_terms([mine_two, got_two])], gates)
    up, two = send_all(*up), send_all(*two)
    block_out, grad_middle, grad_attn, small = expert_all(
        (gates, slot_row, slot_col),
        kept,
        (w_gate, w_up, w_down),
        other,
        (middle, input_two, g2, wr_t, out_grad),
    )
    up, two, grad_attn = together(up, two, grad_attn)
    (two, up), grad_attn = prepare([far_terms(two), x_terms([total_of(up)])], grad_attn)
    two, up = send_all(*two), send_all(*up)
    attended = jnp.concatenate(mine, axis=1).astype(bf16)
    grad_wout = jnp.einsum("tn,td->nd", attended, grad_attn, preferred_element_type=f32)
    grad_wout = jnp.concatenate(column_blocks(grad_wout, hid), axis=0)
    out = send_all(*core_terms(blocks_of(grad_wout)))
    grad_heads = jnp.einsum("td,nd->tn", grad_attn, w_out, preferred_element_type=f32).astype(bf16)
    up, out, grad_heads = together(up, out, grad_heads)
    (out,), grad_heads = prepare([x_terms(out)], grad_heads)
    out = send_all(*out)
    dq, dk, dv = attn_bwd(qkv, grad_heads, seg_col, seg_row, q_cols)
    part, mine_qkv, send_qkv = attn_grads(side, input_one, dq, dk, dv, w_query, w_key, w_value)
    two, out, part, mine_qkv, send_qkv = together(two, out, part, mine_qkv, send_qkv)
    owned = jnp.concatenate([total_of(two).reshape(2, -1, hid), total_of(up)[None]], axis=0)
    sum_experts = lax.all_gather(owned, "dp", axis=1, tiled=True)
    part_other = swap_tensor(part)
    owned = [ring_sum(out)]
    crossed = send_all(*x_terms([mine_qkv, swap_bit(send_qkv, 1)]))
    owned.append(ring_sum(crossed))
    part_other, small, owned, sum_experts = together(part_other, small, owned, sum_experts)
    rest = lax.all_gather(jnp.concatenate(owned, axis=0), "dp", axis=0, tiled=False)
    residual = layer_input.astype(f32)
    inverse_one = lax.rsqrt(jnp.mean(residual * residual, axis=-1, keepdims=True) + norm_eps)
    normed_one = residual * inverse_one
    grad_input_one = part + part_other
    grad_gain_one = jnp.sum(grad_input_one * normed_one, axis=0)
    small = sum_small(jnp.concatenate([small[: EXPERTS + 1], grad_gain_one[None, :]], axis=0))
    scaled = grad_input_one * norm_gain_one
    mean_term = jnp.mean(scaled * normed_one, axis=-1, keepdims=True)
    grad_input = grad_middle + inverse_one * (scaled - normed_one * mean_term)
    sum_out, sum_query, sum_key, sum_value = attn_sums(rest, q_cols)
    sum_down = sum_experts[1].reshape(EXPERTS, D // hid, hid, hid)
    sum_down = jnp.concatenate([sum_down[:, c] for c in range(D // hid)], axis=-1)
    return (
        block_out,
        grad_input,
        small[EXPERTS + 1],
        sum_query,
        sum_key,
        sum_value,
        sum_out,
        small[EXPERTS],
        small[:EXPERTS].T,
        sum_experts[0].reshape(w_gate.shape),
        sum_experts[2].reshape(w_up.shape),
        sum_down,
    )


def solution(mesh):
    in_specs = (
        P("dp", None),
        P("dp", None),
        P("dp", None),
        P("dp", None),
        P(),
        P(None, "tensor"),
        P(None, "tensor"),
        P(None, "tensor"),
        P("tensor", None),
        P(),
        P(),
        P(None, None, "tensor"),
        P(None, None, "tensor"),
        P(None, "tensor", None),
        P("dp", None),
    )
    out_specs = (
        P("dp", None),
        P("dp", None),
        P(),
        P(None, "tensor"),
        P(None, "tensor"),
        P(None, "tensor"),
        P("tensor", None),
        P(),
        P(),
        P(None, None, "tensor"),
        P(None, None, "tensor"),
        P(None, "tensor", None),
    )
    return jax.shard_map(
        per_device, mesh=mesh, in_specs=in_specs, out_specs=out_specs, check_vma=False
    )
```

```python
import functools

import jax
import jax.numpy as jnp
from jax import lax
from jax.experimental import pallas as pl
from jax.experimental.pallas import tpu as pltpu
from jax.sharding import PartitionSpec as P

D = 1024
HEAD_DIM = 64
EXPERTS = 4
TOPK = 2
CAP = 640
MOST = 512
ROWS8 = 8

norm_eps = 1e-05
masked_value = -1e30
f32 = jnp.float32
bf16 = jnp.bfloat16
i32 = jnp.int32

NN = (((1,), (0,)), ((), ()))
NT = (((1,), (1,)), ((), ()))
TN = (((0,), (0,)), ((), ()))


def mm(left, right, dims=NN):
    return lax.dot_general(left, right, dims, preferred_element_type=f32)


def full_spec(shape):
    zeros = (0,) * len(shape)
    return pl.BlockSpec(shape, lambda *_: zeros, pipeline_mode=pl.Buffered(1))


def route_kernel(choice_ref, order_ref, slot_ref):
    length = choice_ref.shape[1]
    pairs = 2 * length
    order = order_ref[...]
    where_pair = (order & 1) * length + (order >> 1)
    match = (lax.broadcasted_iota(i32, (pairs, pairs), 0) == where_pair).astype(f32).astype(bf16)
    experts = lax.broadcasted_iota(i32, (ROWS8, length), 0)
    first = (choice_ref[0:1, :] == experts).astype(f32)
    second = (choice_ref[1:2, :] == experts).astype(f32)
    hot = jnp.concatenate([first, second], axis=1)
    ordered = mm(hot.astype(bf16), match)
    step = 512
    tri = (
        lax.broadcasted_iota(i32, (step, step), 0) < lax.broadcasted_iota(i32, (step, step), 1)
    ).astype(f32)
    carry = jnp.zeros((ROWS8, 1), f32)
    ranks = []
    for begin in range(0, pairs, step):
        part = ordered[:, begin : begin + step]
        inside = mm(part.astype(bf16), tri.astype(bf16)) + carry
        ranks.append(jnp.sum(inside * part, axis=0, keepdims=True))
        carry = carry + jnp.sum(part, axis=1, keepdims=True)
    rank = jnp.concatenate(ranks, axis=1)
    high = jnp.floor(rank * (1.0 / 64.0))
    low_part = rank - 64.0 * high
    row_id = lax.broadcasted_iota(i32, (ROWS8, pairs), 0)
    both = jnp.where(row_id == 0, high, jnp.where(row_id == 1, low_part, 0.0))
    back = mm(both.astype(bf16), match, NT)
    slot = (64.0 * back[0:1, :] + back[1:2, :]).astype(i32)
    slot_ref[...] = jnp.where(
        first > 0.5, slot[:, :length], jnp.where(second > 0.5, slot[:, length:], -1)
    )


def route(choice_t, order):
    length = choice_t.shape[1]
    return pl.pallas_call(
        route_kernel,
        out_shape=jax.ShapeDtypeStruct((ROWS8, length), i32),
        compiler_params=pltpu.CompilerParams(vmem_limit_bytes=50 << 20),
        cost_estimate=pl.CostEstimate(flops=1, transcendentals=0, bytes_accessed=1),
        name="route",
    )(choice_t, order)


def project_kernel(x_ref, g_ref, wq_ref, wk_ref, wv_ref, xn_ref, qkv_ref):
    x = x_ref[...].astype(f32)
    inverse = lax.rsqrt(jnp.mean(x * x, axis=1, keepdims=True) + norm_eps)
    xn = (x * inverse * g_ref[...]).astype(bf16)
    xn_ref[...] = xn
    at = 0
    for w_ref in (wq_ref, wk_ref, wv_ref):
        wide = w_ref.shape[1]
        qkv_ref[:, at : at + wide] = mm(xn, w_ref[...]).astype(bf16)
        at += wide


def project(x, gain, w_query, w_key, w_value):
    length = x.shape[0]
    q_cols = w_query.shape[1]
    kv_cols = w_key.shape[1]
    wide = q_cols + 2 * kv_cols
    rows = 256
    return pl.pallas_call(
        project_kernel,
        grid=(length // rows,),
        in_specs=[
            pl.BlockSpec((rows, D), lambda i: (i, 0)),
            full_spec((1, D)),
            full_spec((D, q_cols)),
            full_spec((D, kv_cols)),
            full_spec((D, kv_cols)),
        ],
        out_specs=[
            pl.BlockSpec((rows, D), lambda i: (i, 0)),
            pl.BlockSpec((rows, wide), lambda i: (i, 0)),
        ],
        out_shape=[
            jax.ShapeDtypeStruct((length, D), bf16),
            jax.ShapeDtypeStruct((length, wide), bf16),
        ],
        cost_estimate=pl.CostEstimate(flops=1, transcendentals=0, bytes_accessed=1),
        name="project",
    )(x, gain, w_query, w_key, w_value)


def attn_blocks(length, rows):
    blocks = []
    for begin in range(0, length, rows):
        start = max(0, begin + rows - MOST - rows)
        start = max(0, (begin + 1 - MOST) // 128 * 128)
        blocks.append((begin, start, begin + rows))
    return blocks


def attn_fwd_kernel(rows, q_ref, k_ref, v_ref, segc_ref, segr_ref, o_ref):
    length = q_ref.shape[0]
    for begin, start, stop in attn_blocks(length, rows):
        wide = stop - start
        row_pos = begin + lax.broadcasted_iota(i32, (rows, wide), 0)
        col_pos = start + lax.broadcasted_iota(i32, (rows, wide), 1)
        allowed = (segc_ref[begin:stop, :] == segr_ref[:, start:stop]) & (col_pos <= row_pos)
        bias = jnp.where(allowed, 0.0, masked_value)
        bias = jnp.concatenate([bias, bias], axis=0)
        for kv in range(2):
            lo = kv * HEAD_DIM
            q_two = jnp.concatenate(
                [
                    q_ref[begin:stop, 2 * lo : 2 * lo + HEAD_DIM],
                    q_ref[begin:stop, 2 * lo + HEAD_DIM : 2 * lo + 2 * HEAD_DIM],
                ],
                axis=0,
            )
            q_two = q_two * jnp.asarray(HEAD_DIM**-0.5, bf16)
            scores = mm(q_two, k_ref[start:stop, lo : lo + HEAD_DIM], NT) + bias
            peak = jnp.max(scores, axis=1, keepdims=True)
            raised = jnp.exp(scores - peak)
            total = jnp.sum(raised, axis=1, keepdims=True)
            probs = (raised * (1.0 / total)).astype(bf16)
            out = mm(probs, v_ref[start:stop, lo : lo + HEAD_DIM])
            out = out.astype(bf16).astype(f32)
            o_ref[begin:stop, 2 * lo : 2 * lo + 2 * HEAD_DIM] = jnp.concatenate(
                [out[:rows], out[rows:]], axis=1
            )


def attn_fwd(qkv, seg_col, seg_row, q_cols, g):
    length = qkv.shape[0]
    pairs = q_cols // 256
    return pl.pallas_call(
        functools.partial(attn_fwd_kernel, 256),
        grid=(1,),
        in_specs=[
            pl.BlockSpec((length, 256), lambda _: (0, g)),
            pl.BlockSpec((length, 128), lambda _: (0, 2 * pairs + g)),
            pl.BlockSpec((length, 128), lambda _: (0, 3 * pairs + g)),
            full_spec((length, 1)),
            full_spec((1, length)),
        ],
        out_specs=pl.BlockSpec((length, 256), lambda _: (0, 0)),
        out_shape=jax.ShapeDtypeStruct((length, 256), f32),
        compiler_params=pltpu.CompilerParams(vmem_limit_bytes=50 << 20),
        cost_estimate=pl.CostEstimate(flops=1, transcendentals=0, bytes_accessed=1),
        name="attn_fwd",
    )(qkv, qkv, qkv, seg_col, seg_row)


def attn_bwd_kernel(
    rows, q_ref, k_ref, v_ref, do_ref, segc_ref, segr_ref, dq_ref, dk_ref, dv_ref, dks, dvs
):
    length = q_ref.shape[0]
    scale = HEAD_DIM**-0.5
    dks[...] = jnp.zeros_like(dks)
    dvs[...] = jnp.zeros_like(dvs)
    for begin, start, stop in attn_blocks(length, rows):
        wide = stop - start
        row_pos = begin + lax.broadcasted_iota(i32, (wide, rows), 1)
        col_pos = start + lax.broadcasted_iota(i32, (wide, rows), 0)
        allowed = (segr_ref[:, begin:stop] == segc_ref[start:stop, :]) & (col_pos <= row_pos)
        bias = jnp.where(allowed, 0.0, masked_value)
        bias = jnp.concatenate([bias, bias], axis=1)
        for kv in range(2):
            lo = kv * HEAD_DIM
            q_two = jnp.concatenate(
                [
                    q_ref[begin:stop, 2 * lo : 2 * lo + HEAD_DIM],
                    q_ref[begin:stop, 2 * lo + HEAD_DIM : 2 * lo + 2 * HEAD_DIM],
                ],
                axis=0,
            )
            q_two = q_two * jnp.asarray(scale, bf16)
            do_two = jnp.concatenate(
                [
                    do_ref[begin:stop, 2 * lo : 2 * lo + HEAD_DIM],
                    do_ref[begin:stop, 2 * lo + HEAD_DIM : 2 * lo + 2 * HEAD_DIM],
                ],
                axis=0,
            )
            k_win = k_ref[start:stop, lo : lo + HEAD_DIM]
            v_win = v_ref[start:stop, lo : lo + HEAD_DIM]
            scores = mm(k_win, q_two, NT) + bias
            peak = jnp.max(scores, axis=0, keepdims=True)
            raised = jnp.exp(scores - peak)
            total = jnp.sum(raised, axis=0, keepdims=True)
            probs = raised * (1.0 / total)
            grad_probs = mm(v_win, do_two, NT)
            row_dot = jnp.sum(probs * grad_probs, axis=0, keepdims=True)
            grad_scores = (probs * (grad_probs - row_dot)).astype(bf16)
            dvs[start:stop, lo : lo + HEAD_DIM] += mm(probs.astype(bf16), do_two)
            dks[start:stop, lo : lo + HEAD_DIM] += mm(grad_scores, q_two)
            dq = (mm(grad_scores, k_win, TN) * scale).astype(bf16)
            dq_ref[begin:stop, 2 * lo : 2 * lo + 2 * HEAD_DIM] = jnp.concatenate(
                [dq[:rows], dq[rows:]], axis=1
            )
    dk_ref[...] = dks[...].astype(bf16)
    dv_ref[...] = dvs[...].astype(bf16)


def attn_bwd(qkv, grad_heads, seg_col, seg_row, q_cols):
    length = qkv.shape[0]
    pairs = q_cols // 256
    return pl.pallas_call(
        functools.partial(attn_bwd_kernel, 256),
        grid=(pairs,),
        in_specs=[
            pl.BlockSpec((length, 256), lambda g: (0, g)),
            pl.BlockSpec((length, 128), lambda g: (0, 2 * pairs + g)),
            pl.BlockSpec((length, 128), lambda g: (0, 3 * pairs + g)),
            pl.BlockSpec((length, 256), lambda g: (0, g)),
            full_spec((length, 1)),
            full_spec((1, length)),
        ],
        out_specs=[
            pl.BlockSpec((length, 256), lambda g: (0, g)),
            pl.BlockSpec((length, 128), lambda g: (0, g)),
            pl.BlockSpec((length, 128), lambda g: (0, g)),
        ],
        out_shape=[
            jax.ShapeDtypeStruct((length, q_cols), bf16),
            jax.ShapeDtypeStruct((length, q_cols // 2), bf16),
            jax.ShapeDtypeStruct((length, q_cols // 2), bf16),
        ],
        scratch_shapes=[pltpu.VMEM((length, 128), f32), pltpu.VMEM((length, 128), f32)],
        compiler_params=pltpu.CompilerParams(vmem_limit_bytes=50 << 20),
        cost_estimate=pl.CostEstimate(flops=24213000000, transcendentals=0, bytes_accessed=1),
        name="attn_bwd",
    )(qkv, qkv, qkv, grad_heads, seg_col, seg_row)


def attn_grads_kernel(
    side_ref, xn_ref, dq_ref, dk_ref, dv_ref, wq_ref, wk_ref, wv_ref, part_ref, mine_ref, send_ref, keep
):
    xn = xn_ref[...]
    wide = dk_ref.shape[1]
    side = side_ref[0, 0]
    queries = [mm(xn, dq_ref[:, c : c + wide], TN) for c in range(0, dq_ref.shape[1], wide)]
    hand_out(jnp.concatenate(queries, axis=0), keep, side, mine_ref, send_ref, 0)
    values = [mm(xn, dk_ref[...], TN), mm(xn, dv_ref[...], TN)]
    hand_out(jnp.concatenate(values, axis=0), keep, side, mine_ref, send_ref, 1)
    part = mm(dq_ref[...], wq_ref[...], NT) + mm(dk_ref[...], wk_ref[...], NT)
    part_ref[...] = part + mm(dv_ref[...], wv_ref[...], NT)


def attn_grads(side, xn, dq, dk, dv, w_query, w_key, w_value):
    length = xn.shape[0]
    wide = dk.shape[1]
    parts = lax.axis_size("dp")
    rows = 2 * dq.shape[1] // wide * D // parts
    shape = jax.ShapeDtypeStruct((parts // 4, 2, rows, wide), f32)
    arrays = (xn, dq, dk, dv, w_query, w_key, w_value)
    return pl.pallas_call(
        attn_grads_kernel,
        grid=(1,),
        in_specs=[pl.BlockSpec(memory_space=pltpu.SMEM)] + [full_spec(one.shape) for one in arrays],
        out_specs=[full_spec((length, D)), full_spec(shape.shape), full_spec(shape.shape)],
        out_shape=[jax.ShapeDtypeStruct((length, D), f32), shape, shape],
        scratch_shapes=[pltpu.VMEM((dq.shape[1] // wide * D, wide), f32)],
        compiler_params=pltpu.CompilerParams(vmem_limit_bytes=50 << 20),
        cost_estimate=pl.CostEstimate(flops=1, transcendentals=0, bytes_accessed=1),
        name="attn_grads",
    )(side, *arrays)


def attn_sums_kernel(in_ref, out_ref, q_ref, k_ref, v_ref):
    c = pl.program_id(0)
    pieces = in_ref.shape[0]
    rows = in_ref.shape[1] // 3
    for p in range(pieces):
        to = slice(p * rows, (p + 1) * rows)
        out_ref[to, :] = in_ref[p, :rows, :]
        q_ref[to, :] = in_ref[p, rows : 2 * rows, :]

    @pl.when(c < 2)
    def _():
        for p in range(pieces):
            k_ref[p * rows : (p + 1) * rows, :] = in_ref[p, 2 * rows :, :]

    @pl.when(c >= 2)
    def _():
        for p in range(pieces):
            v_ref[p * rows : (p + 1) * rows, :] = in_ref[p, 2 * rows :, :]


def attn_sums(gathered, q_cols):
    parts, rows, wide = gathered.shape
    block = (q_cols, wide)
    return pl.pallas_call(
        attn_sums_kernel,
        grid=(4,),
        in_specs=[pl.BlockSpec((parts // 4, rows, wide), lambda c: (c, 0, 0))],
        out_specs=[
            pl.BlockSpec(block, lambda c: (0, c)),
            pl.BlockSpec(block, lambda c: (c % 2, c // 2)),
            pl.BlockSpec(block, lambda c: (jnp.minimum(c, 1), 0)),
            pl.BlockSpec(block, lambda c: (jnp.maximum(c - 2, 0), 0)),
        ],
        out_shape=[
            jax.ShapeDtypeStruct((q_cols, D), f32),
            jax.ShapeDtypeStruct((D, q_cols), f32),
            jax.ShapeDtypeStruct((D, wide), f32),
            jax.ShapeDtypeStruct((D, wide), f32),
        ],
        cost_estimate=pl.CostEstimate(flops=5_000_000_000, transcendentals=0, bytes_accessed=1),
        name="attn_sums",
    )(gathered)


def place_rows(slot_row, length):
    return lax.broadcasted_iota(i32, (CAP, length), 0) == slot_row


def expert_pre_kernel(groups, *refs):
    x_ref = refs[0]
    oa = refs[1 : 1 + groups]
    wo_ref, slotr_ref, dy_ref, h_ref, dys_ref = refs[1 + groups :]
    e = pl.program_id(0)
    length = x_ref.shape[0]
    step = length // EXPERTS
    rows = pl.ds(pl.multiple_of(e * step, step), step)
    total = x_ref[rows, :].astype(f32)
    for g in range(groups):
        total = total + mm(oa[g][rows, :].astype(bf16), wo_ref[g * 256 : (g + 1) * 256, :])
    h_ref[...] = total
    place = place_rows(slotr_ref[pl.ds(e, 1), :], length).astype(f32).astype(bf16)
    dys_ref[...] = mm(place, dy_ref[...]).astype(bf16)


def expert_pre(x, mine, w_out, slot_row, dy):
    length = x.shape[0]
    groups = len(mine)
    return pl.pallas_call(
        functools.partial(expert_pre_kernel, groups),
        grid=(EXPERTS,),
        in_specs=[full_spec((length, D))]
        + [full_spec((length, 256))] * groups
        + [full_spec(w_out.shape), full_spec((ROWS8, length)), full_spec((length, D))],
        out_specs=[
            pl.BlockSpec((length // EXPERTS, D), lambda e: (e, 0)),
            pl.BlockSpec((CAP, D), lambda e: (e, 0)),
        ],
        out_shape=[
            jax.ShapeDtypeStruct((length, D), f32),
            jax.ShapeDtypeStruct((EXPERTS * CAP, D), bf16),
        ],
        compiler_params=pltpu.CompilerParams(vmem_limit_bytes=50 << 20),
        cost_estimate=pl.CostEstimate(flops=1, transcendentals=0, bytes_accessed=1),
        name="expert_pre",
    )(x, *mine, w_out, slot_row, dy)


def hand_out(value, keep, side, mine_ref, send_ref, place=0):
    keep[...] = value
    far = mine_ref.shape[0]
    rows = value.shape[0] // (4 * far)
    to = slice(place * rows, (place + 1) * rows)
    for z in range(far):
        for x in range(2):
            at = 4 * z + 2 * x
            mine_ref[z, x, to] = keep[pl.ds(pl.multiple_of((at + side) * rows, rows), rows), :]
            send_ref[z, x, to] = keep[pl.ds(pl.multiple_of((at + 1 - side) * rows, rows), rows), :]


def expert_own_kernel(groups, side_ref, *refs):
    part_ref = refs[0]
    ob = refs[1 : 1 + groups]
    wox_pieces = refs[1 + groups : 5 + groups]
    (
        g2_ref,
        wr_ref,
        slotr_ref,
        dys_ref,
        wg_ref,
        wu_ref,
        wd_ref,
        h_ref,
        xn_ref,
        gate_ref,
        rows_ref,
        hid_ref,
        dg_ref,
        du_ref,
        mine_up,
        send_up,
        mine_two,
        send_two,
        keep,
        wox_ref,
    ) = refs[5 + groups :]
    side = side_ref[0, 0]
    e = pl.program_id(0)
    length = part_ref.shape[0]
    chunk = 256

    @pl.when(e == 0)
    def _():
        x_side = side_ref[0, 1]
        for at, piece in enumerate(wox_pieces):
            core = side if at < 2 else 1 - side
            place = 2 * core + (x_side if at % 2 == 0 else 1 - x_side)
            height = piece.shape[0]
            to = pl.ds(pl.multiple_of(place * height, height), height)
            wox_ref[to, :] = piece[...].astype(bf16)
        for c in range(length // chunk):
            rows = slice(c * chunk, (c + 1) * chunk)
            h1 = part_ref[rows, :]
            for g in range(groups):
                cols = slice(g * 256, (g + 1) * 256)
                h1 = h1 + mm(ob[g][rows, :].astype(bf16), wox_ref[cols, :])
            h_ref[rows, :] = h1
            inverse = lax.rsqrt(jnp.mean(h1 * h1, axis=1, keepdims=True) + norm_eps)
            xn_ref[rows, :] = (h1 * inverse * g2_ref[...]).astype(bf16)
        logits = mm(wr_ref[...].astype(bf16), xn_ref[...], NT)
        chosen = slotr_ref[...] >= 0
        logits = jnp.where(chosen, logits, masked_value)
        peak = jnp.max(logits, axis=0, keepdims=True)
        raised = jnp.where(chosen, jnp.exp(logits - peak), 0.0)
        gate_ref[...] = raised / jnp.sum(raised, axis=0, keepdims=True)

    mask = place_rows(slotr_ref[pl.ds(e, 1), :], length)
    place = mask.astype(f32).astype(bf16)
    gate = jnp.sum(jnp.where(mask, gate_ref[pl.ds(e, 1), :], 0.0), axis=1, keepdims=True)
    rows_in = mm(place, xn_ref[...]).astype(bf16)
    rows_ref[...] = rows_in
    dy_gated = (gate * dys_ref[...].astype(f32)).astype(bf16)
    g = mm(rows_in, wg_ref[0])
    u = mm(rows_in, wu_ref[0])
    sig = 1.0 / (1.0 + jnp.exp(-g))
    act = g * sig
    hid = (act * u).astype(bf16)
    dhid = mm(dy_gated, wd_ref[0], NT)
    dg = (dhid * u * sig * (1.0 + g * (1.0 - sig))).astype(bf16)
    du = (dhid * act).astype(bf16)
    hid_ref[...] = hid
    dg_ref[...] = dg
    du_ref[...] = du
    both = mm(rows_in, jnp.concatenate([du, dg], axis=1), TN)
    half = du.shape[1]
    hand_out(both[:, :half], keep, side, mine_up, send_up)
    hand_out(both[:, half:], keep, side, mine_two, send_two)
    dwd = mm(hid, dy_gated, TN)
    wide = hid.shape[1]
    blocks = [dwd[:, c : c + wide] for c in range(0, D, wide)]
    hand_out(jnp.concatenate(blocks, axis=0), keep, side, mine_two, send_two, 1)


def piece_specs(hid, arrays):
    parts = lax.axis_size("dp")
    far = parts // 4
    rows = arrays * EXPERTS * D // parts
    spec = pl.BlockSpec((far // EXPERTS, 2, rows, hid), lambda e: (e, 0, 0, 0))
    return spec, jax.ShapeDtypeStruct((far, 2, rows, hid), f32)


def expert_own(side, part, theirs, w_out_other, g2, wr_t, slot_row, dys, w_gate, w_up, w_down):
    length = part.shape[0]
    hid = w_down.shape[1]
    groups = len(theirs)
    slots = EXPERTS * CAP
    q_cols = 4 * w_out_other[0].shape[0]
    piece, shape = piece_specs(hid, 1)
    piece_two, shape_two = piece_specs(hid, 2)
    return pl.pallas_call(
        functools.partial(expert_own_kernel, groups),
        grid=(EXPERTS,),
        in_specs=[pl.BlockSpec(memory_space=pltpu.SMEM), full_spec((length, D))]
        + [full_spec((length, 256))] * groups
        + [
            *[full_spec(one.shape) for one in w_out_other],
            full_spec((1, D)),
            full_spec((ROWS8, D)),
            full_spec((ROWS8, length)),
            pl.BlockSpec((CAP, D), lambda e: (e, 0)),
            pl.BlockSpec((1, D, hid), lambda e: (e, 0, 0)),
            pl.BlockSpec((1, D, hid), lambda e: (e, 0, 0)),
            pl.BlockSpec((1, hid, D), lambda e: (e, 0, 0)),
        ],
        out_specs=[
            full_spec((length, D)),
            full_spec((length, D)),
            full_spec((ROWS8, length)),
            pl.BlockSpec((CAP, D), lambda e: (e, 0)),
            pl.BlockSpec((CAP, hid), lambda e: (e, 0)),
            pl.BlockSpec((CAP, hid), lambda e: (e, 0)),
            pl.BlockSpec((CAP, hid), lambda e: (e, 0)),
            piece,
            piece,
            piece_two,
            piece_two,
        ],
        out_shape=[
            jax.ShapeDtypeStruct((length, D), f32),
            jax.ShapeDtypeStruct((length, D), bf16),
            jax.ShapeDtypeStruct((ROWS8, length), f32),
            jax.ShapeDtypeStruct((slots, D), bf16),
            jax.ShapeDtypeStruct((slots, hid), bf16),
            jax.ShapeDtypeStruct((slots, hid), bf16),
            jax.ShapeDtypeStruct((slots, hid), bf16),
            shape,
            shape,
            shape_two,
            shape_two,
        ],
        scratch_shapes=[pltpu.VMEM((D, hid), f32), pltpu.VMEM((q_cols, D), bf16)],
        compiler_params=pltpu.CompilerParams(vmem_limit_bytes=60 << 20),
        cost_estimate=pl.CostEstimate(flops=39202000000, transcendentals=0, bytes_accessed=1),
        name="expert_own",
    )(side, part, *theirs, *w_out_other, g2, wr_t, slot_row, dys, w_gate, w_up, w_down)


def expert_all_kernel(
    gate_ref,
    slotr_ref,
    slotc_ref,
    rows_ref,
    dys_ref,
    hid_ref,
    dg_ref,
    du_ref,
    wg_ref,
    wu_ref,
    wd_ref,
    wgx_ref,
    wux_ref,
    wdx_ref,
    *rest,
):
    (h_ref, xn_ref, g2_ref, wr_ref, dy_ref) = rest[:5]
    (out_ref, dh_ref, da_ref, small_ref, moe_s, dgate_s) = rest[5:]
    e = pl.program_id(0)
    length = slotr_ref.shape[1]
    chunk = 256

    @pl.when(e == 0)
    def _():
        moe_s[...] = jnp.zeros_like(moe_s)
        dh_ref[...] = jnp.zeros_like(dh_ref)
        dgate_s[...] = jnp.zeros_like(dgate_s)

    mask = place_rows(slotr_ref[pl.ds(e, 1), :], length)
    lane8 = lax.broadcasted_iota(i32, (length, ROWS8), 1)
    slot_col = jnp.sum(jnp.where(lane8 == e, slotc_ref[...], 0), axis=1, keepdims=True)
    place_t = (lax.broadcasted_iota(i32, (length, CAP), 1) == slot_col).astype(f32).astype(bf16)
    gate = jnp.sum(jnp.where(mask, gate_ref[pl.ds(e, 1), :], 0.0), axis=1, keepdims=True)
    rows_in = rows_ref[...]
    dy_slot = dys_ref[...].astype(f32)
    dy_gated = (gate * dy_slot).astype(bf16)
    hid_wide = wgx_ref.shape[1]
    wg = wgx_ref[...].astype(bf16)
    wu = wux_ref[...].astype(bf16)
    wd = jnp.concatenate(
        [wdx_ref[c * hid_wide : (c + 1) * hid_wide, :] for c in range(D // hid_wide)], axis=1
    ).astype(bf16)
    g = mm(rows_in, wg)
    u = mm(rows_in, wu)
    sig = 1.0 / (1.0 + jnp.exp(-g))
    act = g * sig
    hid = (act * u).astype(bf16)
    dhid = mm(dy_gated, wd, NT)
    dg = (dhid * u * sig * (1.0 + g * (1.0 - sig))).astype(bf16)
    du = (dhid * act).astype(bf16)
    y = mm(hid_ref[...], wd_ref[0]) + mm(hid, wd)
    dx = mm(dg_ref[...], wg_ref[0], NT) + mm(du_ref[...], wu_ref[0], NT)
    dx = dx + mm(dg, wg, NT) + mm(du, wu, NT)
    dgate_slot = jnp.sum(dy_slot * y, axis=1, keepdims=True)
    dgate_s[pl.ds(e, 1), :] = jnp.sum(jnp.where(mask, dgate_slot, 0.0), axis=0, keepdims=True)
    moe_s[...] += mm(place_t, (gate * y).astype(bf16))
    dh_ref[...] += mm(place_t, dx.astype(bf16))

    @pl.when(e == EXPERTS - 1)
    def _():
        gates = gate_ref[...]
        dgates = dgate_s[...]
        dsel = gates * (dgates - jnp.sum(gates * dgates, axis=0, keepdims=True))
        drouter = mm(dsel.astype(bf16), xn_ref[...])
        wr = wr_ref[...].astype(bf16)
        dlog_t = dsel.T.astype(bf16)
        small_ref[...] = jnp.zeros_like(small_ref)
        small_ref[0:EXPERTS, :] = drouter[0:EXPERTS, :]
        gain = jnp.zeros((1, D), f32)
        for c in range(length // chunk):
            rows = slice(c * chunk, (c + 1) * chunk)
            h1 = h_ref[rows, :]
            out_ref[rows, :] = (h1 + moe_s[rows, :]).astype(bf16)
            inverse = lax.rsqrt(jnp.mean(h1 * h1, axis=1, keepdims=True) + norm_eps)
            n2 = h1 * inverse
            dxn = dh_ref[rows, :] + mm(dlog_t[rows, :], wr)
            gain = gain + jnp.sum(dxn * n2, axis=0, keepdims=True)
            scaled = dxn * g2_ref[...]
            mean_term = jnp.mean(scaled * n2, axis=1, keepdims=True)
            dh1 = dy_ref[rows, :].astype(f32) + inverse * (scaled - n2 * mean_term)
            dh_ref[rows, :] = dh1
            da_ref[rows, :] = dh1.astype(bf16)
        small_ref[EXPERTS : EXPERTS + 1, :] = gain


def expert_all(routing, kept, weights, other, tail):
    gates, slot_row, slot_col = routing
    w_gate, w_up, w_down = weights
    length = slot_row.shape[1]
    hid = w_down.shape[1]
    slot_block = lambda wide: pl.BlockSpec((CAP, wide), lambda e: (e, 0))
    weight_in = pl.BlockSpec((1, D, hid), lambda e: (e, 0, 0))
    other_block = lambda at: pl.BlockSpec((D, hid), lambda e: (at + e, 0))
    whole = full_spec((length, D))
    in_specs = [
        full_spec((ROWS8, length)),
        full_spec((ROWS8, length)),
        full_spec((length, ROWS8)),
        slot_block(D),
        slot_block(D),
        slot_block(hid),
        slot_block(hid),
        slot_block(hid),
        weight_in,
        weight_in,
        pl.BlockSpec((1, hid, D), lambda e: (e, 0, 0)),
        other_block(0),
        other_block(EXPERTS),
        other_block(2 * EXPERTS),
    ]
    in_specs += [whole, whole, full_spec((1, D)), full_spec((ROWS8, D)), whole]
    return pl.pallas_call(
        expert_all_kernel,
        grid=(EXPERTS,),
        in_specs=in_specs,
        out_specs=[whole, whole, whole, full_spec((ROWS8, D))],
        out_shape=[
            jax.ShapeDtypeStruct((length, D), bf16),
            jax.ShapeDtypeStruct((length, D), f32),
            jax.ShapeDtypeStruct((length, D), bf16),
            jax.ShapeDtypeStruct((ROWS8, D), f32),
        ],
        scratch_shapes=[pltpu.VMEM((length, D), f32), pltpu.VMEM((ROWS8, length), f32)],
        compiler_params=pltpu.CompilerParams(vmem_limit_bytes=60 << 20),
        cost_estimate=pl.CostEstimate(flops=24_000_000_000, transcendentals=0, bytes_accessed=1),
        name="expert_all",
    )(gates, slot_row, slot_col, *kept, w_gate, w_up, w_down, other, other, other, *tail)


def swap_tensor(values):
    size = lax.axis_size("tensor")
    return lax.ppermute(values, "tensor", [(i, i ^ 1) for i in range(size)])


def together(*values):
    return lax.optimization_barrier(values)


def column_blocks(values, wide):
    return [values[..., c : c + wide] for c in range(0, values.shape[-1], wide)]


def start_experts(w_gate, w_up, w_down):
    parts = lax.axis_size("dp")
    at = lax.axis_index("dp")
    hid = w_down.shape[1]
    down = jnp.stack(column_blocks(w_down, hid), axis=1)
    shares = []
    for packed in (w_gate, w_up, down):
        packed = packed.reshape(-1, hid)
        rows = packed.shape[0] // parts
        shares.append(lax.dynamic_slice_in_dim(packed, at * rows, rows, 0))
    return swap_tensor(jnp.stack(shares).astype(f32))


def gather_experts(swapped):
    whole = lax.all_gather(swapped, "dp", axis=1, tiled=True)
    return whole.reshape(-1, whole.shape[-1])


def swap_bit(values, bit):
    size = lax.axis_size("dp")
    return lax.ppermute(values, "dp", [(i, i ^ bit) for i in range(size)])


def side_of(bit):
    return (lax.axis_index("dp") // bit) & 1


def blocks_of(values):
    parts = lax.axis_size("dp")
    return values.reshape(parts // 4, 2, 2, -1, values.shape[-1])


def picked(terms, which, axis):
    total = None
    for term in terms:
        part = lax.dynamic_index_in_dim(term, which, axis, keepdims=False)
        total = part if total is None else total + part
    return total


def core_terms(values):
    side = side_of(1)
    return picked([values], side, 2), [(picked([values], 1 - side, 2), 1)]


def x_terms(terms):
    side = side_of(2)
    axis = terms[0].ndim - 3
    return picked(terms, side, axis), [(picked(terms, 1 - side, axis), 2)]


def far_terms(terms):
    size = terms[0].shape[0]
    me = lax.axis_index("dp") // 4
    sends = [(picked(terms, me ^ k, 0), 4 * k) for k in range(size - 1, 0, -1)]
    return picked(terms, me, 0), sends


def ring_order(size):
    if size <= 2:
        return list(range(size))
    return [0] + list(range(1, size, 2)) + list(range(size - 2, 0, -2))


def ring_send(values):
    order = ring_order(lax.axis_size("dp") // 4)
    pairs = []
    for at, source in enumerate(order):
        target = order[(at + 1) % len(order)]
        pairs += [(source * 4 + low, target * 4 + low) for low in range(4)]
    return lax.ppermute(values, "dp", pairs)


def ring_sum(terms):
    order = ring_order(lax.axis_size("dp") // 4)
    size = len(order)
    place = jnp.asarray([order.index(z) for z in range(size)], i32)[lax.axis_index("dp") // 4]
    members = jnp.asarray(order, i32)
    piece = lambda p: picked(terms, members[jnp.mod(p, size)], 0)
    packet = piece(place - 1)
    for step in range(size - 1):
        packet = ring_send(packet) + piece(place - 2 - step)
    return packet


def send_all(keep, sends):
    return [keep] + [swap_bit(values, bit) for values, bit in sends]


def prepare(staged, *others):
    bits = [[bit for _, bit in sends] for _, sends in staged]
    values = [(keep, [value for value, _ in sends]) for keep, sends in staged]
    values, *others = together(values, *others)
    staged = [(keep, list(zip(sends, bit))) for (keep, sends), bit in zip(values, bits)]
    return [staged, *others]


def total_of(terms):
    return sum(terms[1:], terms[0])


def sum_small(values):
    bit = 1
    while bit < lax.axis_size("dp"):
        values = values + swap_bit(values, bit)
        bit *= 2
    return values


def start_out(w_out):
    at = lax.axis_index("dp")
    rows = w_out.shape[0] // 4
    place = (at & 1) * 2 + ((at >> 1) & 1)
    return swap_tensor(lax.dynamic_slice_in_dim(w_out, place * rows, rows, 0).astype(f32))


def per_device(
    layer_input,
    segments,
    expert_choice,
    dispatch_order,
    norm_gain_one,
    w_query,
    w_key,
    w_value,
    w_out,
    norm_gain_two,
    w_router,
    w_gate,
    w_up,
    w_down,
    out_grad,
):
    length = layer_input.shape[0]
    q_cols = w_query.shape[1]
    hid = w_down.shape[1]
    flat = lambda grad: grad.reshape(-1, grad.shape[-1])
    seg_row = segments
    seg_col = segments.reshape(length, 1)
    piece = start_out(w_out)
    input_one, qkv = project(layer_input, norm_gain_one[None, :], w_query, w_key, w_value)
    qkv, weights, piece = together(qkv, (w_gate, w_up, w_down), piece)
    swapped = start_experts(*weights)
    first = attn_fwd(qkv, seg_col, seg_row, q_cols, 0)
    first, qkv = together(first, qkv)
    first_other = swap_tensor(first)
    across = swap_bit(piece, 2)
    second = attn_fwd(qkv, seg_col, seg_row, q_cols, 1)
    second, swapped, order = together(second, swapped, dispatch_order)
    slot_row = route(expert_choice.T, order)
    other = gather_experts(swapped)
    slot_row, across = together(slot_row, across)
    mine = [first, second]
    theirs = [first_other, swap_tensor(second)]
    w_out_other = [piece, across, swap_bit(piece, 1), swap_bit(across, 1)]
    slot_col = slot_row.T

    wr_t = jnp.pad(w_router.T.astype(f32), ((0, ROWS8 - EXPERTS), (0, 0)))
    g2 = norm_gain_two[None, :]
    side = jnp.stack([side_of(1), side_of(2), lax.axis_index("dp") // 4]).astype(i32)[None, :]
    h_part, dys = expert_pre(layer_input, mine, w_out, slot_row, out_grad)
    middle, input_two, gates, rows_in, *rest = expert_own(
        side,
        h_part,
        theirs,
        w_out_other,
        g2,
        wr_t,
        slot_row,
        dys,
        w_gate,
        w_up,
        w_down,
    )
    *kept, mine_up, send_up, mine_two, send_two = rest
    kept = [rows_in, dys, *kept]
    got_up = swap_bit(send_up, 1)
    got_two = swap_bit(send_two, 1)
    (up, two), gates = prepare([far_terms([mine_up, got_up]), x_terms([mine_two, got_two])], gates)
    up, two = send_all(*up), send_all(*two)
    block_out, grad_middle, grad_attn, small = expert_all(
        (gates, slot_row, slot_col),
        kept,
        (w_gate, w_up, w_down),
        other,
        (middle, input_two, g2, wr_t, out_grad),
    )
    up, two, grad_attn = together(up, two, grad_attn)
    (two, up), grad_attn = prepare([far_terms(two), x_terms([total_of(up)])], grad_attn)
    two, up = send_all(*two), send_all(*up)
    attended = jnp.concatenate(mine, axis=1).astype(bf16)
    grad_wout = jnp.einsum("tn,td->nd", attended, grad_attn, preferred_element_type=f32)
    grad_wout = jnp.concatenate(column_blocks(grad_wout, hid), axis=0)
    out = send_all(*core_terms(blocks_of(grad_wout)))
    grad_heads = jnp.einsum("td,nd->tn", grad_attn, w_out, preferred_element_type=f32).astype(bf16)
    up, out, grad_heads = together(up, out, grad_heads)
    (out,), grad_heads = prepare([x_terms(out)], grad_heads)
    out = send_all(*out)
    dq, dk, dv = attn_bwd(qkv, grad_heads, seg_col, seg_row, q_cols)
    part, mine_qkv, send_qkv = attn_grads(side, input_one, dq, dk, dv, w_query, w_key, w_value)
    two, out, part, mine_qkv, send_qkv = together(two, out, part, mine_qkv, send_qkv)
    owned = jnp.concatenate([total_of(two).reshape(2, -1, hid), total_of(up)[None]], axis=0)
    sum_experts = lax.all_gather(owned, "dp", axis=1, tiled=True)
    part_other = swap_tensor(part)
    owned = [ring_sum(out)]
    crossed = send_all(*x_terms([mine_qkv, swap_bit(send_qkv, 1)]))
    owned.append(ring_sum(crossed))
    part_other, small, owned, sum_experts = together(part_other, small, owned, sum_experts)
    rest = lax.all_gather(jnp.concatenate(owned, axis=0), "dp", axis=0, tiled=False)
    residual = layer_input.astype(f32)
    inverse_one = lax.rsqrt(jnp.mean(residual * residual, axis=-1, keepdims=True) + norm_eps)
    normed_one = residual * inverse_one
    grad_input_one = part + part_other
    grad_gain_one = jnp.sum(grad_input_one * normed_one, axis=0)
    small = sum_small(jnp.concatenate([small[: EXPERTS + 1], grad_gain_one[None, :]], axis=0))
    scaled = grad_input_one * norm_gain_one
    mean_term = jnp.mean(scaled * normed_one, axis=-1, keepdims=True)
    grad_input = grad_middle + inverse_one * (scaled - normed_one * mean_term)
    sum_out, sum_query, sum_key, sum_value = attn_sums(rest, q_cols)
    sum_down = sum_experts[1].reshape(EXPERTS, D // hid, hid, hid)
    sum_down = jnp.concatenate([sum_down[:, c] for c in range(D // hid)], axis=-1)
    return (
        block_out,
        grad_input,
        small[EXPERTS + 1],
        sum_query,
        sum_key,
        sum_value,
        sum_out,
        small[EXPERTS],
        small[:EXPERTS].T,
        sum_experts[0].reshape(w_gate.shape),
        sum_experts[2].reshape(w_up.shape),
        sum_down,
    )


def solution(mesh):
    in_specs = (
        P("dp", None),
        P("dp", None),
        P("dp", None),
        P("dp", None),
        P(),
        P(None, "tensor"),
        P(None, "tensor"),
        P(None, "tensor"),
        P("tensor", None),
        P(),
        P(),
        P(None, None, "tensor"),
        P(None, None, "tensor"),
        P(None, "tensor", None),
        P("dp", None),
    )
    out_specs = (
        P("dp", None),
        P("dp", None),
        P(),
        P(None, "tensor"),
        P(None, "tensor"),
        P(None, "tensor"),
        P("tensor", None),
        P(),
        P(),
        P(None, None, "tensor"),
        P(None, None, "tensor"),
        P(None, "tensor", None),
    )
    return jax.shard_map(
        per_device, mesh=mesh, in_specs=in_specs, out_specs=out_specs, check_vma=False
    )
```

```python
import functools

import jax
import jax.numpy as jnp
from jax import lax
from jax.experimental import pallas as pl
from jax.experimental.pallas import tpu as pltpu
from jax.sharding import PartitionSpec as P

D = 1024
HEAD_DIM = 64
EXPERTS = 4
TOPK = 2
CAP = 640
MOST = 512
ROWS8 = 8

norm_eps = 1e-05
masked_value = -1e30
f32 = jnp.float32
bf16 = jnp.bfloat16
i32 = jnp.int32

NN = (((1,), (0,)), ((), ()))
NT = (((1,), (1,)), ((), ()))
TN = (((0,), (0,)), ((), ()))


def mm(left, right, dims=NN):
    return lax.dot_general(left, right, dims, preferred_element_type=f32)


def full_spec(shape):
    zeros = (0,) * len(shape)
    return pl.BlockSpec(shape, lambda *_: zeros, pipeline_mode=pl.Buffered(1))


def route_kernel(choice_ref, order_ref, slot_ref):
    length = choice_ref.shape[1]
    pairs = 2 * length
    order = order_ref[...]
    where_pair = (order & 1) * length + (order >> 1)
    match = (lax.broadcasted_iota(i32, (pairs, pairs), 0) == where_pair).astype(f32).astype(bf16)
    experts = lax.broadcasted_iota(i32, (ROWS8, length), 0)
    first = (choice_ref[0:1, :] == experts).astype(f32)
    second = (choice_ref[1:2, :] == experts).astype(f32)
    hot = jnp.concatenate([first, second], axis=1)
    ordered = mm(hot.astype(bf16), match)
    step = 512
    tri = (
        lax.broadcasted_iota(i32, (step, step), 0) < lax.broadcasted_iota(i32, (step, step), 1)
    ).astype(f32)
    carry = jnp.zeros((ROWS8, 1), f32)
    ranks = []
    for begin in range(0, pairs, step):
        part = ordered[:, begin : begin + step]
        inside = mm(part.astype(bf16), tri.astype(bf16)) + carry
        ranks.append(jnp.sum(inside * part, axis=0, keepdims=True))
        carry = carry + jnp.sum(part, axis=1, keepdims=True)
    rank = jnp.concatenate(ranks, axis=1)
    high = jnp.floor(rank * (1.0 / 64.0))
    low_part = rank - 64.0 * high
    row_id = lax.broadcasted_iota(i32, (ROWS8, pairs), 0)
    both = jnp.where(row_id == 0, high, jnp.where(row_id == 1, low_part, 0.0))
    back = mm(both.astype(bf16), match, NT)
    slot = (64.0 * back[0:1, :] + back[1:2, :]).astype(i32)
    slot_ref[...] = jnp.where(
        first > 0.5, slot[:, :length], jnp.where(second > 0.5, slot[:, length:], -1)
    )


def route(choice_t, order):
    length = choice_t.shape[1]
    return pl.pallas_call(
        route_kernel,
        out_shape=jax.ShapeDtypeStruct((ROWS8, length), i32),
        compiler_params=pltpu.CompilerParams(vmem_limit_bytes=50 << 20),
        cost_estimate=pl.CostEstimate(flops=1, transcendentals=0, bytes_accessed=1),
        name="route",
    )(choice_t, order)


def project_kernel(x_ref, g_ref, wq_ref, wk_ref, wv_ref, xn_ref, qkv_ref):
    x = x_ref[...].astype(f32)
    inverse = lax.rsqrt(jnp.mean(x * x, axis=1, keepdims=True) + norm_eps)
    xn = (x * inverse * g_ref[...]).astype(bf16)
    xn_ref[...] = xn
    at = 0
    for w_ref in (wq_ref, wk_ref, wv_ref):
        wide = w_ref.shape[1]
        qkv_ref[:, at : at + wide] = mm(xn, w_ref[...]).astype(bf16)
        at += wide


def project(x, gain, w_query, w_key, w_value):
    length = x.shape[0]
    q_cols = w_query.shape[1]
    kv_cols = w_key.shape[1]
    wide = q_cols + 2 * kv_cols
    rows = 256
    return pl.pallas_call(
        project_kernel,
        grid=(length // rows,),
        in_specs=[
            pl.BlockSpec((rows, D), lambda i: (i, 0)),
            full_spec((1, D)),
            full_spec((D, q_cols)),
            full_spec((D, kv_cols)),
            full_spec((D, kv_cols)),
        ],
        out_specs=[
            pl.BlockSpec((rows, D), lambda i: (i, 0)),
            pl.BlockSpec((rows, wide), lambda i: (i, 0)),
        ],
        out_shape=[
            jax.ShapeDtypeStruct((length, D), bf16),
            jax.ShapeDtypeStruct((length, wide), bf16),
        ],
        cost_estimate=pl.CostEstimate(flops=1, transcendentals=0, bytes_accessed=1),
        name="project",
    )(x, gain, w_query, w_key, w_value)


def attn_blocks(length, rows):
    blocks = []
    for begin in range(0, length, rows):
        start = max(0, begin + rows - MOST - rows)
        start = max(0, (begin + 1 - MOST) // 128 * 128)
        blocks.append((begin, start, begin + rows))
    return blocks


def attn_fwd_kernel(rows, q_ref, k_ref, v_ref, segc_ref, segr_ref, o_ref):
    length = q_ref.shape[0]
    for begin, start, stop in attn_blocks(length, rows):
        wide = stop - start
        row_pos = begin + lax.broadcasted_iota(i32, (rows, wide), 0)
        col_pos = start + lax.broadcasted_iota(i32, (rows, wide), 1)
        allowed = (segc_ref[begin:stop, :] == segr_ref[:, start:stop]) & (col_pos <= row_pos)
        bias = jnp.where(allowed, 0.0, masked_value)
        bias = jnp.concatenate([bias, bias], axis=0)
        for kv in range(2):
            lo = kv * HEAD_DIM
            q_two = jnp.concatenate(
                [
                    q_ref[begin:stop, 2 * lo : 2 * lo + HEAD_DIM],
                    q_ref[begin:stop, 2 * lo + HEAD_DIM : 2 * lo + 2 * HEAD_DIM],
                ],
                axis=0,
            )
            q_two = q_two * jnp.asarray(HEAD_DIM**-0.5, bf16)
            scores = mm(q_two, k_ref[start:stop, lo : lo + HEAD_DIM], NT) + bias
            peak = jnp.max(scores, axis=1, keepdims=True)
            raised = jnp.exp(scores - peak)
            total = jnp.sum(raised, axis=1, keepdims=True)
            probs = (raised * (1.0 / total)).astype(bf16)
            out = mm(probs, v_ref[start:stop, lo : lo + HEAD_DIM])
            out = out.astype(bf16).astype(f32)
            o_ref[begin:stop, 2 * lo : 2 * lo + 2 * HEAD_DIM] = jnp.concatenate(
                [out[:rows], out[rows:]], axis=1
            )


def attn_fwd(qkv, seg_col, seg_row, q_cols, g):
    length = qkv.shape[0]
    pairs = q_cols // 256
    return pl.pallas_call(
        functools.partial(attn_fwd_kernel, 256),
        grid=(1,),
        in_specs=[
            pl.BlockSpec((length, 256), lambda _: (0, g)),
            pl.BlockSpec((length, 128), lambda _: (0, 2 * pairs + g)),
            pl.BlockSpec((length, 128), lambda _: (0, 3 * pairs + g)),
            full_spec((length, 1)),
            full_spec((1, length)),
        ],
        out_specs=pl.BlockSpec((length, 256), lambda _: (0, 0)),
        out_shape=jax.ShapeDtypeStruct((length, 256), f32),
        compiler_params=pltpu.CompilerParams(vmem_limit_bytes=50 << 20),
        cost_estimate=pl.CostEstimate(flops=1, transcendentals=0, bytes_accessed=1),
        name="attn_fwd",
    )(qkv, qkv, qkv, seg_col, seg_row)


def attn_bwd_kernel(
    rows, q_ref, k_ref, v_ref, do_ref, segc_ref, segr_ref, dq_ref, dk_ref, dv_ref, dks, dvs
):
    length = q_ref.shape[0]
    scale = HEAD_DIM**-0.5
    dks[...] = jnp.zeros_like(dks)
    dvs[...] = jnp.zeros_like(dvs)
    for begin, start, stop in attn_blocks(length, rows):
        wide = stop - start
        row_pos = begin + lax.broadcasted_iota(i32, (wide, rows), 1)
        col_pos = start + lax.broadcasted_iota(i32, (wide, rows), 0)
        allowed = (segr_ref[:, begin:stop] == segc_ref[start:stop, :]) & (col_pos <= row_pos)
        bias = jnp.where(allowed, 0.0, masked_value)
        bias = jnp.concatenate([bias, bias], axis=1)
        for kv in range(2):
            lo = kv * HEAD_DIM
            q_two = jnp.concatenate(
                [
                    q_ref[begin:stop, 2 * lo : 2 * lo + HEAD_DIM],
                    q_ref[begin:stop, 2 * lo + HEAD_DIM : 2 * lo + 2 * HEAD_DIM],
                ],
                axis=0,
            )
            q_two = q_two * jnp.asarray(scale, bf16)
            do_two = jnp.concatenate(
                [
                    do_ref[begin:stop, 2 * lo : 2 * lo + HEAD_DIM],
                    do_ref[begin:stop, 2 * lo + HEAD_DIM : 2 * lo + 2 * HEAD_DIM],
                ],
                axis=0,
            )
            k_win = k_ref[start:stop, lo : lo + HEAD_DIM]
            v_win = v_ref[start:stop, lo : lo + HEAD_DIM]
            scores = mm(k_win, q_two, NT) + bias
            peak = jnp.max(scores, axis=0, keepdims=True)
            raised = jnp.exp(scores - peak)
            total = jnp.sum(raised, axis=0, keepdims=True)
            probs = raised * (1.0 / total)
            grad_probs = mm(v_win, do_two, NT)
            row_dot = jnp.sum(probs * grad_probs, axis=0, keepdims=True)
            grad_scores = (probs * (grad_probs - row_dot)).astype(bf16)
            dvs[start:stop, lo : lo + HEAD_DIM] += mm(probs.astype(bf16), do_two)
            dks[start:stop, lo : lo + HEAD_DIM] += mm(grad_scores, q_two)
            dq = (mm(grad_scores, k_win, TN) * scale).astype(bf16)
            dq_ref[begin:stop, 2 * lo : 2 * lo + 2 * HEAD_DIM] = jnp.concatenate(
                [dq[:rows], dq[rows:]], axis=1
            )
    dk_ref[...] = dks[...].astype(bf16)
    dv_ref[...] = dvs[...].astype(bf16)


def attn_bwd(qkv, grad_heads, seg_col, seg_row, q_cols):
    length = qkv.shape[0]
    pairs = q_cols // 256
    return pl.pallas_call(
        functools.partial(attn_bwd_kernel, 256),
        grid=(pairs,),
        in_specs=[
            pl.BlockSpec((length, 256), lambda g: (0, g)),
            pl.BlockSpec((length, 128), lambda g: (0, 2 * pairs + g)),
            pl.BlockSpec((length, 128), lambda g: (0, 3 * pairs + g)),
            pl.BlockSpec((length, 256), lambda g: (0, g)),
            full_spec((length, 1)),
            full_spec((1, length)),
        ],
        out_specs=[
            pl.BlockSpec((length, 256), lambda g: (0, g)),
            pl.BlockSpec((length, 128), lambda g: (0, g)),
            pl.BlockSpec((length, 128), lambda g: (0, g)),
        ],
        out_shape=[
            jax.ShapeDtypeStruct((length, q_cols), bf16),
            jax.ShapeDtypeStruct((length, q_cols // 2), bf16),
            jax.ShapeDtypeStruct((length, q_cols // 2), bf16),
        ],
        scratch_shapes=[pltpu.VMEM((length, 128), f32), pltpu.VMEM((length, 128), f32)],
        compiler_params=pltpu.CompilerParams(vmem_limit_bytes=50 << 20),
        cost_estimate=pl.CostEstimate(flops=24213000000, transcendentals=0, bytes_accessed=1),
        name="attn_bwd",
    )(qkv, qkv, qkv, grad_heads, seg_col, seg_row)


def attn_grads_kernel(
    side_ref, xn_ref, dq_ref, dk_ref, dv_ref, wq_ref, wk_ref, wv_ref, part_ref, mine_ref, send_ref, keep
):
    xn = xn_ref[...]
    wide = dk_ref.shape[1]
    side = side_ref[0, 0]
    queries = [mm(xn, dq_ref[:, c : c + wide], TN) for c in range(0, dq_ref.shape[1], wide)]
    hand_out(jnp.concatenate(queries, axis=0), keep, side, mine_ref, send_ref, 0)
    values = [mm(xn, dk_ref[...], TN), mm(xn, dv_ref[...], TN)]
    hand_out(jnp.concatenate(values, axis=0), keep, side, mine_ref, send_ref, 1)
    part = mm(dq_ref[...], wq_ref[...], NT) + mm(dk_ref[...], wk_ref[...], NT)
    part_ref[...] = part + mm(dv_ref[...], wv_ref[...], NT)


def attn_grads(side, xn, dq, dk, dv, w_query, w_key, w_value):
    length = xn.shape[0]
    wide = dk.shape[1]
    parts = lax.axis_size("dp")
    rows = 2 * dq.shape[1] // wide * D // parts
    shape = jax.ShapeDtypeStruct((parts // 4, 2, rows, wide), f32)
    arrays = (xn, dq, dk, dv, w_query, w_key, w_value)
    return pl.pallas_call(
        attn_grads_kernel,
        grid=(1,),
        in_specs=[pl.BlockSpec(memory_space=pltpu.SMEM)] + [full_spec(one.shape) for one in arrays],
        out_specs=[full_spec((length, D)), full_spec(shape.shape), full_spec(shape.shape)],
        out_shape=[jax.ShapeDtypeStruct((length, D), f32), shape, shape],
        scratch_shapes=[pltpu.VMEM((dq.shape[1] // wide * D, wide), f32)],
        compiler_params=pltpu.CompilerParams(vmem_limit_bytes=50 << 20),
        cost_estimate=pl.CostEstimate(flops=1, transcendentals=0, bytes_accessed=1),
        name="attn_grads",
    )(side, *arrays)


def attn_sums_kernel(in_ref, out_ref, q_ref, k_ref, v_ref):
    c = pl.program_id(0)
    pieces = in_ref.shape[0]
    rows = in_ref.shape[1] // 3
    for p in range(pieces):
        to = slice(p * rows, (p + 1) * rows)
        out_ref[to, :] = in_ref[p, :rows, :]
        q_ref[to, :] = in_ref[p, rows : 2 * rows, :]

    @pl.when(c < 2)
    def _():
        for p in range(pieces):
            k_ref[p * rows : (p + 1) * rows, :] = in_ref[p, 2 * rows :, :]

    @pl.when(c >= 2)
    def _():
        for p in range(pieces):
            v_ref[p * rows : (p + 1) * rows, :] = in_ref[p, 2 * rows :, :]


def attn_sums(gathered, q_cols):
    parts, rows, wide = gathered.shape
    block = (q_cols, wide)
    return pl.pallas_call(
        attn_sums_kernel,
        grid=(4,),
        in_specs=[pl.BlockSpec((parts // 4, rows, wide), lambda c: (c, 0, 0))],
        out_specs=[
            pl.BlockSpec(block, lambda c: (0, c)),
            pl.BlockSpec(block, lambda c: (c % 2, c // 2)),
            pl.BlockSpec(block, lambda c: (jnp.minimum(c, 1), 0)),
            pl.BlockSpec(block, lambda c: (jnp.maximum(c - 2, 0), 0)),
        ],
        out_shape=[
            jax.ShapeDtypeStruct((q_cols, D), f32),
            jax.ShapeDtypeStruct((D, q_cols), f32),
            jax.ShapeDtypeStruct((D, wide), f32),
            jax.ShapeDtypeStruct((D, wide), f32),
        ],
        cost_estimate=pl.CostEstimate(flops=5_000_000_000, transcendentals=0, bytes_accessed=1),
        name="attn_sums",
    )(gathered)


def place_rows(slot_row, length):
    return lax.broadcasted_iota(i32, (CAP, length), 0) == slot_row


def expert_pre_kernel(groups, *refs):
    x_ref = refs[0]
    oa = refs[1 : 1 + groups]
    wo_ref, slotr_ref, dy_ref, h_ref, dys_ref = refs[1 + groups :]
    e = pl.program_id(0)
    length = x_ref.shape[0]
    step = length // EXPERTS
    rows = pl.ds(pl.multiple_of(e * step, step), step)
    total = x_ref[rows, :].astype(f32)
    for g in range(groups):
        total = total + mm(oa[g][rows, :].astype(bf16), wo_ref[g * 256 : (g + 1) * 256, :])
    h_ref[...] = total
    place = place_rows(slotr_ref[pl.ds(e, 1), :], length).astype(f32).astype(bf16)
    dys_ref[...] = mm(place, dy_ref[...]).astype(bf16)


def expert_pre(x, mine, w_out, slot_row, dy):
    length = x.shape[0]
    groups = len(mine)
    return pl.pallas_call(
        functools.partial(expert_pre_kernel, groups),
        grid=(EXPERTS,),
        in_specs=[full_spec((length, D))]
        + [full_spec((length, 256))] * groups
        + [full_spec(w_out.shape), full_spec((ROWS8, length)), full_spec((length, D))],
        out_specs=[
            pl.BlockSpec((length // EXPERTS, D), lambda e: (e, 0)),
            pl.BlockSpec((CAP, D), lambda e: (e, 0)),
        ],
        out_shape=[
            jax.ShapeDtypeStruct((length, D), f32),
            jax.ShapeDtypeStruct((EXPERTS * CAP, D), bf16),
        ],
        compiler_params=pltpu.CompilerParams(vmem_limit_bytes=50 << 20),
        cost_estimate=pl.CostEstimate(flops=1, transcendentals=0, bytes_accessed=1),
        name="expert_pre",
    )(x, *mine, w_out, slot_row, dy)


def hand_out(value, keep, side, mine_ref, send_ref, place=0):
    keep[...] = value
    far = mine_ref.shape[0]
    rows = value.shape[0] // (4 * far)
    to = slice(place * rows, (place + 1) * rows)
    for z in range(far):
        for x in range(2):
            at = 4 * z + 2 * x
            mine_ref[z, x, to] = keep[pl.ds(pl.multiple_of((at + side) * rows, rows), rows), :]
            send_ref[z, x, to] = keep[pl.ds(pl.multiple_of((at + 1 - side) * rows, rows), rows), :]


def expert_own_kernel(groups, side_ref, *refs):
    part_ref = refs[0]
    ob = refs[1 : 1 + groups]
    wox_pieces = refs[1 + groups : 5 + groups]
    (
        g2_ref,
        wr_ref,
        slotr_ref,
        dys_ref,
        wg_ref,
        wu_ref,
        wd_ref,
        h_ref,
        xn_ref,
        gate_ref,
        rows_ref,
        hid_ref,
        dg_ref,
        du_ref,
        mine_up,
        send_up,
        mine_two,
        send_two,
        keep,
        wox_ref,
    ) = refs[5 + groups :]
    side = side_ref[0, 0]
    e = pl.program_id(0)
    length = part_ref.shape[0]
    chunk = 256

    @pl.when(e == 0)
    def _():
        x_side = side_ref[0, 1]
        for at, piece in enumerate(wox_pieces):
            core = side if at < 2 else 1 - side
            place = 2 * core + (x_side if at % 2 == 0 else 1 - x_side)
            height = piece.shape[0]
            to = pl.ds(pl.multiple_of(place * height, height), height)
            wox_ref[to, :] = piece[...].astype(bf16)
        for c in range(length // chunk):
            rows = slice(c * chunk, (c + 1) * chunk)
            h1 = part_ref[rows, :]
            for g in range(groups):
                cols = slice(g * 256, (g + 1) * 256)
                h1 = h1 + mm(ob[g][rows, :].astype(bf16), wox_ref[cols, :])
            h_ref[rows, :] = h1
            inverse = lax.rsqrt(jnp.mean(h1 * h1, axis=1, keepdims=True) + norm_eps)
            xn_ref[rows, :] = (h1 * inverse * g2_ref[...]).astype(bf16)
        logits = mm(wr_ref[...].astype(bf16), xn_ref[...], NT)
        chosen = slotr_ref[...] >= 0
        logits = jnp.where(chosen, logits, masked_value)
        peak = jnp.max(logits, axis=0, keepdims=True)
        raised = jnp.where(chosen, jnp.exp(logits - peak), 0.0)
        gate_ref[...] = raised / jnp.sum(raised, axis=0, keepdims=True)

    mask = place_rows(slotr_ref[pl.ds(e, 1), :], length)
    place = mask.astype(f32).astype(bf16)
    gate = jnp.sum(jnp.where(mask, gate_ref[pl.ds(e, 1), :], 0.0), axis=1, keepdims=True)
    rows_in = mm(place, xn_ref[...]).astype(bf16)
    rows_ref[...] = rows_in
    dy_gated = (gate * dys_ref[...].astype(f32)).astype(bf16)
    g = mm(rows_in, wg_ref[0])
    u = mm(rows_in, wu_ref[0])
    sig = 1.0 / (1.0 + jnp.exp(-g))
    act = g * sig
    hid = (act * u).astype(bf16)
    dhid = mm(dy_gated, wd_ref[0], NT)
    dg = (dhid * u * sig * (1.0 + g * (1.0 - sig))).astype(bf16)
    du = (dhid * act).astype(bf16)
    hid_ref[...] = hid
    dg_ref[...] = dg
    du_ref[...] = du
    both = mm(rows_in, jnp.concatenate([du, dg], axis=1), TN)
    half = du.shape[1]
    hand_out(both[:, :half], keep, side, mine_up, send_up)
    hand_out(both[:, half:], keep, side, mine_two, send_two)
    dwd = mm(hid, dy_gated, TN)
    wide = hid.shape[1]
    blocks = [dwd[:, c : c + wide] for c in range(0, D, wide)]
    hand_out(jnp.concatenate(blocks, axis=0), keep, side, mine_two, send_two, 1)


def piece_specs(hid, arrays):
    parts = lax.axis_size("dp")
    far = parts // 4
    rows = arrays * EXPERTS * D // parts
    spec = pl.BlockSpec((far // EXPERTS, 2, rows, hid), lambda e: (e, 0, 0, 0))
    return spec, jax.ShapeDtypeStruct((far, 2, rows, hid), f32)


def expert_own(side, part, theirs, w_out_other, g2, wr_t, slot_row, dys, w_gate, w_up, w_down):
    length = part.shape[0]
    hid = w_down.shape[1]
    groups = len(theirs)
    slots = EXPERTS * CAP
    q_cols = 4 * w_out_other[0].shape[0]
    piece, shape = piece_specs(hid, 1)
    piece_two, shape_two = piece_specs(hid, 2)
    return pl.pallas_call(
        functools.partial(expert_own_kernel, groups),
        grid=(EXPERTS,),
        in_specs=[pl.BlockSpec(memory_space=pltpu.SMEM), full_spec((length, D))]
        + [full_spec((length, 256))] * groups
        + [
            *[full_spec(one.shape) for one in w_out_other],
            full_spec((1, D)),
            full_spec((ROWS8, D)),
            full_spec((ROWS8, length)),
            pl.BlockSpec((CAP, D), lambda e: (e, 0)),
            pl.BlockSpec((1, D, hid), lambda e: (e, 0, 0)),
            pl.BlockSpec((1, D, hid), lambda e: (e, 0, 0)),
            pl.BlockSpec((1, hid, D), lambda e: (e, 0, 0)),
        ],
        out_specs=[
            full_spec((length, D)),
            full_spec((length, D)),
            full_spec((ROWS8, length)),
            pl.BlockSpec((CAP, D), lambda e: (e, 0)),
            pl.BlockSpec((CAP, hid), lambda e: (e, 0)),
            pl.BlockSpec((CAP, hid), lambda e: (e, 0)),
            pl.BlockSpec((CAP, hid), lambda e: (e, 0)),
            piece,
            piece,
            piece_two,
            piece_two,
        ],
        out_shape=[
            jax.ShapeDtypeStruct((length, D), f32),
            jax.ShapeDtypeStruct((length, D), bf16),
            jax.ShapeDtypeStruct((ROWS8, length), f32),
            jax.ShapeDtypeStruct((slots, D), bf16),
            jax.ShapeDtypeStruct((slots, hid), bf16),
            jax.ShapeDtypeStruct((slots, hid), bf16),
            jax.ShapeDtypeStruct((slots, hid), bf16),
            shape,
            shape,
            shape_two,
            shape_two,
        ],
        scratch_shapes=[pltpu.VMEM((D, hid), f32), pltpu.VMEM((q_cols, D), bf16)],
        compiler_params=pltpu.CompilerParams(vmem_limit_bytes=60 << 20),
        cost_estimate=pl.CostEstimate(flops=39202000000, transcendentals=0, bytes_accessed=1),
        name="expert_own",
    )(side, part, *theirs, *w_out_other, g2, wr_t, slot_row, dys, w_gate, w_up, w_down)


def expert_all_kernel(
    gate_ref,
    slotr_ref,
    slotc_ref,
    rows_ref,
    dys_ref,
    hid_ref,
    dg_ref,
    du_ref,
    wg_ref,
    wu_ref,
    wd_ref,
    wgx_ref,
    wux_ref,
    wdx_ref,
    *rest,
):
    (h_ref, xn_ref, g2_ref, wr_ref, dy_ref) = rest[:5]
    (out_ref, dh_ref, da_ref, small_ref, moe_s, dgate_s) = rest[5:]
    e = pl.program_id(0)
    length = slotr_ref.shape[1]
    chunk = 256

    @pl.when(e == 0)
    def _():
        moe_s[...] = jnp.zeros_like(moe_s)
        dh_ref[...] = jnp.zeros_like(dh_ref)
        dgate_s[...] = jnp.zeros_like(dgate_s)

    mask = place_rows(slotr_ref[pl.ds(e, 1), :], length)
    lane8 = lax.broadcasted_iota(i32, (length, ROWS8), 1)
    slot_col = jnp.sum(jnp.where(lane8 == e, slotc_ref[...], 0), axis=1, keepdims=True)
    place_t = (lax.broadcasted_iota(i32, (length, CAP), 1) == slot_col).astype(f32).astype(bf16)
    gate = jnp.sum(jnp.where(mask, gate_ref[pl.ds(e, 1), :], 0.0), axis=1, keepdims=True)
    rows_in = rows_ref[...]
    dy_slot = dys_ref[...].astype(f32)
    dy_gated = (gate * dy_slot).astype(bf16)
    hid_wide = wgx_ref.shape[1]
    wg = wgx_ref[...].astype(bf16)
    wu = wux_ref[...].astype(bf16)
    wd = jnp.concatenate(
        [wdx_ref[c * hid_wide : (c + 1) * hid_wide, :] for c in range(D // hid_wide)], axis=1
    ).astype(bf16)
    g = mm(rows_in, wg)
    u = mm(rows_in, wu)
    sig = 1.0 / (1.0 + jnp.exp(-g))
    act = g * sig
    hid = (act * u).astype(bf16)
    dhid = mm(dy_gated, wd, NT)
    dg = (dhid * u * sig * (1.0 + g * (1.0 - sig))).astype(bf16)
    du = (dhid * act).astype(bf16)
    y = mm(hid_ref[...], wd_ref[0]) + mm(hid, wd)
    dx = mm(dg_ref[...], wg_ref[0], NT) + mm(du_ref[...], wu_ref[0], NT)
    dx = dx + mm(dg, wg, NT) + mm(du, wu, NT)
    dgate_slot = jnp.sum(dy_slot * y, axis=1, keepdims=True)
    dgate_s[pl.ds(e, 1), :] = jnp.sum(jnp.where(mask, dgate_slot, 0.0), axis=0, keepdims=True)
    moe_s[...] += mm(place_t, (gate * y).astype(bf16))
    dh_ref[...] += mm(place_t, dx.astype(bf16))

    @pl.when(e == EXPERTS - 1)
    def _():
        gates = gate_ref[...]
        dgates = dgate_s[...]
        dsel = gates * (dgates - jnp.sum(gates * dgates, axis=0, keepdims=True))
        drouter = mm(dsel.astype(bf16), xn_ref[...])
        wr = wr_ref[...].astype(bf16)
        dlog_t = dsel.T.astype(bf16)
        small_ref[...] = jnp.zeros_like(small_ref)
        small_ref[0:EXPERTS, :] = drouter[0:EXPERTS, :]
        gain = jnp.zeros((1, D), f32)
        for c in range(length // chunk):
            rows = slice(c * chunk, (c + 1) * chunk)
            h1 = h_ref[rows, :]
            out_ref[rows, :] = (h1 + moe_s[rows, :]).astype(bf16)
            inverse = lax.rsqrt(jnp.mean(h1 * h1, axis=1, keepdims=True) + norm_eps)
            n2 = h1 * inverse
            dxn = dh_ref[rows, :] + mm(dlog_t[rows, :], wr)
            gain = gain + jnp.sum(dxn * n2, axis=0, keepdims=True)
            scaled = dxn * g2_ref[...]
            mean_term = jnp.mean(scaled * n2, axis=1, keepdims=True)
            dh1 = dy_ref[rows, :].astype(f32) + inverse * (scaled - n2 * mean_term)
            dh_ref[rows, :] = dh1
            da_ref[rows, :] = dh1.astype(bf16)
        small_ref[EXPERTS : EXPERTS + 1, :] = gain


def expert_all(routing, kept, weights, other, tail):
    gates, slot_row, slot_col = routing
    w_gate, w_up, w_down = weights
    length = slot_row.shape[1]
    hid = w_down.shape[1]
    slot_block = lambda wide: pl.BlockSpec((CAP, wide), lambda e: (e, 0))
    weight_in = pl.BlockSpec((1, D, hid), lambda e: (e, 0, 0))
    other_block = lambda at: pl.BlockSpec((D, hid), lambda e: (at + e, 0))
    whole = full_spec((length, D))
    in_specs = [
        full_spec((ROWS8, length)),
        full_spec((ROWS8, length)),
        full_spec((length, ROWS8)),
        slot_block(D),
        slot_block(D),
        slot_block(hid),
        slot_block(hid),
        slot_block(hid),
        weight_in,
        weight_in,
        pl.BlockSpec((1, hid, D), lambda e: (e, 0, 0)),
        other_block(0),
        other_block(EXPERTS),
        other_block(2 * EXPERTS),
    ]
    in_specs += [whole, whole, full_spec((1, D)), full_spec((ROWS8, D)), whole]
    return pl.pallas_call(
        expert_all_kernel,
        grid=(EXPERTS,),
        in_specs=in_specs,
        out_specs=[whole, whole, whole, full_spec((ROWS8, D))],
        out_shape=[
            jax.ShapeDtypeStruct((length, D), bf16),
            jax.ShapeDtypeStruct((length, D), f32),
            jax.ShapeDtypeStruct((length, D), bf16),
            jax.ShapeDtypeStruct((ROWS8, D), f32),
        ],
        scratch_shapes=[pltpu.VMEM((length, D), f32), pltpu.VMEM((ROWS8, length), f32)],
        compiler_params=pltpu.CompilerParams(vmem_limit_bytes=60 << 20),
        cost_estimate=pl.CostEstimate(flops=24_000_000_000, transcendentals=0, bytes_accessed=1),
        name="expert_all",
    )(gates, slot_row, slot_col, *kept, w_gate, w_up, w_down, other, other, other, *tail)


def swap_tensor(values):
    size = lax.axis_size("tensor")
    return lax.ppermute(values, "tensor", [(i, i ^ 1) for i in range(size)])


def together(*values):
    return lax.optimization_barrier(values)


def column_blocks(values, wide):
    return [values[..., c : c + wide] for c in range(0, values.shape[-1], wide)]


def expert_shares(w_gate, w_up, w_down):
    parts = lax.axis_size("dp")
    at = lax.axis_index("dp")
    hid = w_down.shape[1]
    down = jnp.stack(column_blocks(w_down, hid), axis=1)
    shares = []
    for packed in (w_gate, w_up, down):
        packed = packed.reshape(-1, hid)
        rows = packed.shape[0] // parts
        shares.append(lax.dynamic_slice_in_dim(packed, at * rows, rows, 0))
    return jnp.stack(shares).astype(f32)


def gather_experts(swapped):
    whole = lax.all_gather(swapped, "dp", axis=1, tiled=True)
    return whole.reshape(-1, whole.shape[-1])


def swap_bit(values, bit):
    size = lax.axis_size("dp")
    return lax.ppermute(values, "dp", [(i, i ^ bit) for i in range(size)])


def side_of(bit):
    return (lax.axis_index("dp") // bit) & 1


def blocks_of(values):
    parts = lax.axis_size("dp")
    return values.reshape(parts // 4, 2, 2, -1, values.shape[-1])


def picked(terms, which, axis):
    total = None
    for term in terms:
        part = lax.dynamic_index_in_dim(term, which, axis, keepdims=False)
        total = part if total is None else total + part
    return total


def core_terms(values):
    side = side_of(1)
    return picked([values], side, 2), [(picked([values], 1 - side, 2), 1)]


def x_terms(terms):
    side = side_of(2)
    axis = terms[0].ndim - 3
    return picked(terms, side, axis), [(picked(terms, 1 - side, axis), 2)]


def far_terms(terms):
    size = terms[0].shape[0]
    me = lax.axis_index("dp") // 4
    sends = [(picked(terms, me ^ k, 0), 4 * k) for k in range(size - 1, 0, -1)]
    return picked(terms, me, 0), sends


def ring_order(size):
    if size <= 2:
        return list(range(size))
    return [0] + list(range(1, size, 2)) + list(range(size - 2, 0, -2))


def ring_send(values):
    order = ring_order(lax.axis_size("dp") // 4)
    pairs = []
    for at, source in enumerate(order):
        target = order[(at + 1) % len(order)]
        pairs += [(source * 4 + low, target * 4 + low) for low in range(4)]
    return lax.ppermute(values, "dp", pairs)


def ring_sum(terms):
    order = ring_order(lax.axis_size("dp") // 4)
    size = len(order)
    place = jnp.asarray([order.index(z) for z in range(size)], i32)[lax.axis_index("dp") // 4]
    members = jnp.asarray(order, i32)
    piece = lambda p: picked(terms, members[jnp.mod(p, size)], 0)
    packet = piece(place - 1)
    for step in range(size - 1):
        packet = ring_send(packet) + piece(place - 2 - step)
    return packet


def send_all(keep, sends):
    return [keep] + [swap_bit(values, bit) for values, bit in sends]


def prepare(staged, *others):
    bits = [[bit for _, bit in sends] for _, sends in staged]
    values = [(keep, [value for value, _ in sends]) for keep, sends in staged]
    values, *others = together(values, *others)
    staged = [(keep, list(zip(sends, bit))) for (keep, sends), bit in zip(values, bits)]
    return [staged, *others]


def total_of(terms):
    return sum(terms[1:], terms[0])


def sum_small(values):
    bit = 1
    while bit < lax.axis_size("dp"):
        values = values + swap_bit(values, bit)
        bit *= 2
    return values


def start_out(w_out):
    at = lax.axis_index("dp")
    rows = w_out.shape[0] // 4
    place = (at & 1) * 2 + ((at >> 1) & 1)
    return swap_tensor(lax.dynamic_slice_in_dim(w_out, place * rows, rows, 0).astype(f32))


def per_device(
    layer_input,
    segments,
    expert_choice,
    dispatch_order,
    norm_gain_one,
    w_query,
    w_key,
    w_value,
    w_out,
    norm_gain_two,
    w_router,
    w_gate,
    w_up,
    w_down,
    out_grad,
):
    length = layer_input.shape[0]
    q_cols = w_query.shape[1]
    hid = w_down.shape[1]
    flat = lambda grad: grad.reshape(-1, grad.shape[-1])
    seg_row = segments
    seg_col = segments.reshape(length, 1)
    piece = start_out(w_out)
    input_one, qkv = project(layer_input, norm_gain_one[None, :], w_query, w_key, w_value)
    qkv, weights = together(qkv, (w_gate, w_up, w_down))
    qkv, shares, piece = together(qkv, expert_shares(*weights), piece)
    swapped = swap_tensor(shares)
    first = attn_fwd(qkv, seg_col, seg_row, q_cols, 0)
    first, qkv = together(first, qkv)
    first_other = swap_tensor(first)
    across = swap_bit(piece, 2)
    second = attn_fwd(qkv, seg_col, seg_row, q_cols, 1)
    second, swapped, order = together(second, swapped, dispatch_order)
    slot_row = route(expert_choice.T, order)
    other = gather_experts(swapped)
    slot_row, across = together(slot_row, across)
    mine = [first, second]
    theirs = [first_other, swap_tensor(second)]
    w_out_other = [piece, across, swap_bit(piece, 1), swap_bit(across, 1)]
    slot_col = slot_row.T

    wr_t = jnp.pad(w_router.T.astype(f32), ((0, ROWS8 - EXPERTS), (0, 0)))
    g2 = norm_gain_two[None, :]
    side = jnp.stack([side_of(1), side_of(2), lax.axis_index("dp") // 4]).astype(i32)[None, :]
    h_part, dys = expert_pre(layer_input, mine, w_out, slot_row, out_grad)
    middle, input_two, gates, rows_in, *rest = expert_own(
        side,
        h_part,
        theirs,
        w_out_other,
        g2,
        wr_t,
        slot_row,
        dys,
        w_gate,
        w_up,
        w_down,
    )
    *kept, mine_up, send_up, mine_two, send_two = rest
    kept = [rows_in, dys, *kept]
    got_up = swap_bit(send_up, 1)
    got_two = swap_bit(send_two, 1)
    (up, two), gates = prepare([far_terms([mine_up, got_up]), x_terms([mine_two, got_two])], gates)
    up, two = send_all(*up), send_all(*two)
    block_out, grad_middle, grad_attn, small = expert_all(
        (gates, slot_row, slot_col),
        kept,
        (w_gate, w_up, w_down),
        other,
        (middle, input_two, g2, wr_t, out_grad),
    )
    up, two, grad_attn = together(up, two, grad_attn)
    (two, up), grad_attn = prepare([far_terms(two), x_terms([total_of(up)])], grad_attn)
    two, up = send_all(*two), send_all(*up)
    attended = jnp.concatenate(mine, axis=1).astype(bf16)
    grad_wout = jnp.einsum("tn,td->nd", attended, grad_attn, preferred_element_type=f32)
    grad_wout = jnp.concatenate(column_blocks(grad_wout, hid), axis=0)
    out = send_all(*core_terms(blocks_of(grad_wout)))
    grad_heads = jnp.einsum("td,nd->tn", grad_attn, w_out, preferred_element_type=f32).astype(bf16)
    up, out, grad_heads = together(up, out, grad_heads)
    (out,), grad_heads = prepare([x_terms(out)], grad_heads)
    out = send_all(*out)
    dq, dk, dv = attn_bwd(qkv, grad_heads, seg_col, seg_row, q_cols)
    part, mine_qkv, send_qkv = attn_grads(side, input_one, dq, dk, dv, w_query, w_key, w_value)
    two, out, part, mine_qkv, send_qkv = together(two, out, part, mine_qkv, send_qkv)
    owned = jnp.concatenate([total_of(two).reshape(2, -1, hid), total_of(up)[None]], axis=0)
    sum_experts = lax.all_gather(owned, "dp", axis=1, tiled=True)
    part_other = swap_tensor(part)
    owned = [ring_sum(out)]
    crossed = send_all(*x_terms([mine_qkv, swap_bit(send_qkv, 1)]))
    owned.append(ring_sum(crossed))
    part_other, small, owned, sum_experts = together(part_other, small, owned, sum_experts)
    rest = lax.all_gather(jnp.concatenate(owned, axis=0), "dp", axis=0, tiled=False)
    residual = layer_input.astype(f32)
    inverse_one = lax.rsqrt(jnp.mean(residual * residual, axis=-1, keepdims=True) + norm_eps)
    normed_one = residual * inverse_one
    grad_input_one = part + part_other
    grad_gain_one = jnp.sum(grad_input_one * normed_one, axis=0)
    small = sum_small(jnp.concatenate([small[: EXPERTS + 1], grad_gain_one[None, :]], axis=0))
    scaled = grad_input_one * norm_gain_one
    mean_term = jnp.mean(scaled * normed_one, axis=-1, keepdims=True)
    grad_input = grad_middle + inverse_one * (scaled - normed_one * mean_term)
    sum_out, sum_query, sum_key, sum_value = attn_sums(rest, q_cols)
    sum_down = sum_experts[1].reshape(EXPERTS, D // hid, hid, hid)
    sum_down = jnp.concatenate([sum_down[:, c] for c in range(D // hid)], axis=-1)
    return (
        block_out,
        grad_input,
        small[EXPERTS + 1],
        sum_query,
        sum_key,
        sum_value,
        sum_out,
        small[EXPERTS],
        small[:EXPERTS].T,
        sum_experts[0].reshape(w_gate.shape),
        sum_experts[2].reshape(w_up.shape),
        sum_down,
    )


def solution(mesh):
    in_specs = (
        P("dp", None),
        P("dp", None),
        P("dp", None),
        P("dp", None),
        P(),
        P(None, "tensor"),
        P(None, "tensor"),
        P(None, "tensor"),
        P("tensor", None),
        P(),
        P(),
        P(None, None, "tensor"),
        P(None, None, "tensor"),
        P(None, "tensor", None),
        P("dp", None),
    )
    out_specs = (
        P("dp", None),
        P("dp", None),
        P(),
        P(None, "tensor"),
        P(None, "tensor"),
        P(None, "tensor"),
        P("tensor", None),
        P(),
        P(),
        P(None, None, "tensor"),
        P(None, None, "tensor"),
        P(None, "tensor", None),
    )
    return jax.shard_map(
        per_device, mesh=mesh, in_specs=in_specs, out_specs=out_specs, check_vma=False
    )
```
